32 devices in a mesh: ctx: 16 (over z, y, x), wsh: 2 (over core).
Axes of the slice: x: 2, y: 2, z: 4, core: 2. Of those that a mesh axis runs over, the one named last changes fastest.
Arguments:
- inputs: float32 [2, 2048, 1024], P('wsh', 'ctx'), may hold values from -6 to 6
- norm_gain1: float32 [1024], replicated, may hold values from 0.5 to 1.5
- mix_in: bfloat16 [1024, 4096], P(('ctx', 'wsh')), may hold values from -1 to 1
- step_proj: bfloat16 [1024, 24], replicated, may hold values from -0.4375 to 0.4375
- conv_weight: float32 [4, 1792], replicated, may hold values from -3 to 3
- conv_bias: float32 [1792], replicated, may hold values from -3 to 3
- step_bias: float32 [24], replicated, may hold values from -1 to 1
- decay_log: float32 [24], replicated, may hold values from -11.5 to -3
- skip_gain: float32 [24], replicated, may hold values from 0.5 to 1.5
- mamba_gain: float32 [1536], replicated, may hold values from 0.5 to 1.5
- mix_out: bfloat16 [2048, 1024], P(('ctx', 'wsh')), may hold values from -0.25 to 0.25
- norm_gain2: float32 [1024], replicated, may hold values from 0.5 to 1.5
- mlp_in: bfloat16 [1024, 4096], P(('ctx', 'wsh')), may hold values from -0.1875 to 0.1875
- mlp_out: bfloat16 [2048, 1024], P(('ctx', 'wsh')), may hold values from -0.125 to 0.125
- out_grad: float32 [2, 2048, 1024], P('wsh', 'ctx'), may hold values from -6 to 6
Outputs:
- outputs: float32 [2, 2048, 1024], P('wsh', 'ctx')
- input_grad: float32 [2, 2048, 1024], P('wsh', 'ctx')
- norm_gain1_grad: float32 [1024], replicated
- mix_in_grad: float32 [1024, 4096], P(('ctx', 'wsh'))
- step_proj_grad: float32 [1024, 24], replicated
- conv_weight_grad: float32 [4, 1792], replicated
- conv_bias_grad: float32 [1792], replicated
- step_bias_grad: float32 [24], replicated
- decay_log_grad: float32 [24], replicated
- skip_gain_grad: float32 [24], replicated
- mamba_gain_grad: float32 [1536], replicated
- mix_out_grad: float32 [2048, 1024], P(('ctx', 'wsh'))
- norm_gain2_grad: float32 [1024], replicated
- mlp_in_grad: float32 [1024, 4096], P(('ctx', 'wsh'))
- mlp_out_grad: float32 [2048, 1024], P(('ctx', 'wsh'))
The draws below stay inside these ranges and needn't reach their ends.
All inputs are finite; a program needn't handle non-finite values.
Results may differ from the reference program's by a relative error of at most 0.015.
The reference program's roundings to bfloat16 on the way count: a program that leaves them out, or rounds other values in their place, can miss the bound.
Values may be sent and summed in bfloat16 or wider, within the bound.
No kernel may reach another device: no remote copies, remote signals or barrier semaphores. Data moves between devices by JAX's collectives and lax.ppermute only.
A program may use at most 320 MiB of HBM per device.

```python
from functools import partial
from functools import reduce
import jax
import jax.numpy as jnp
from jax import lax

D = 1024
MHEADS = 24
MHEAD_DIM = 64
STATE = 128
CONV = 4
ATT_HEADS = 8
KV_HEADS = 2
HEAD_DIM = 64
FF = 2048
TOK_DEV = 128
SEQLEN = 2048
SEQS = 2
INNER = 1536
CONV_CH = 1792
PROJ = 4096
MIXED = 2048
N_CTX = 16


def draw_mix_in(key, part):
    weights = jnp.clip(jax.random.normal(jax.random.fold_in(key, 7311), (D, PROJ), jnp.float32), -4.0, 4.0) * D ** (-0.5)
    return weights.astype(jnp.bfloat16)


def draw_inputs(key, part):
    shape_all = (SEQS, SEQLEN, D)
    drawn = jax.random.normal(jax.random.fold_in(key, 7325), shape_all, jnp.float32)
    return jnp.clip(drawn, -6.0, 6.0)


def levels(rng, shape, split, low, top_value):
    factor_of = 1.0
    for dim, shards_of in split:
        heights = jax.random.uniform(jax.random.fold_in(jax.random.fold_in(rng, 6), dim), (shards_of,), jnp.float32, low / len(split), top_value / len(split))
        factor_of = factor_of * jnp.repeat(jnp.exp(heights), shape[dim] // shards_of).reshape((-1,) + (1,) * (len(shape) - 1 - dim))
    return factor_of


def gaussian(stream_key, extent, width, limit, pieces=(), kind=jnp.bfloat16):
    values = jax.random.normal(stream_key, extent, jnp.float32) * width
    if len(pieces) > 0:
        values = levels(stream_key, extent, pieces, -0.22, 0.18) * values
    return jnp.clip(values, min=-limit, max=limit).astype(kind)


def setup_inputs(seed: int = 0) -> dict:
    seeds = jax.random.split(jax.random.key(seed), 16)
    return {
        "inputs": draw_inputs(jax.random.fold_in(seeds[15], 71), 0),
        "norm_gain1": jnp.clip(1.0 + 0.1 * jax.random.normal(seeds[1], (D,), jnp.float32), 0.5, 1.5),
        "mix_in": draw_mix_in(jax.random.fold_in(seeds[15], 71), 0),
        "step_proj": gaussian(seeds[3], (D, MHEADS), (D // 6) ** -0.5, 0.4375),
        "conv_weight": gaussian(seeds[4], (CONV, CONV_CH), 0.5, 3.0, (), jnp.float32),
        "conv_bias": gaussian(seeds[5], (CONV_CH,), 0.5, 3.0, (), jnp.float32),
        "step_bias": jnp.clip(jax.random.uniform(seeds[6], (MHEADS,), jnp.float32, -1.0, 1.0), -1.0, 1.0),
        "decay_log": jnp.clip(jax.random.uniform(seeds[7], (MHEADS,), jnp.float32, -11.5, -3.0), -11.5, -3.0),
        "skip_gain": jnp.clip(jax.random.uniform(seeds[8], (MHEADS,), jnp.float32, 0.5, 1.5), 0.5, 1.5),
        "mamba_gain": jnp.clip(1.0 + 0.1 * jax.random.normal(seeds[9], (INNER,), jnp.float32), 0.5, 1.5),
        "mix_out": gaussian(seeds[10], (MIXED, D), (MIXED // 4) ** -0.5, 0.25, ((0, 32),)),
        "norm_gain2": jnp.clip(1.0 + 0.1 * jax.random.normal(seeds[11], (D,), jnp.float32), 0.5, 1.5),
        "mlp_in": gaussian(seeds[12], (D, 2 * FF), D ** -0.5, 0.1875, ((0, 32),)),
        "mlp_out": gaussian(seeds[13], (FF, D), FF ** -0.5, 0.125, ((0, 32),)),
        "out_grad": gaussian(seeds[14], (SEQS, SEQLEN, D), 1.0, 6.0, ((0, 2), (1, 16)), jnp.float32),
    }


EPSILON = 1e-05
ROPE_BASE = 10000.0
NEG_LARGE = -1e+30
HIGHEST = lax.Precision.HIGHEST

def rms_scale(values, gain_vec):
    return values * lax.rsqrt(lax.optimization_barrier(jnp.mean(values * values, axis=-1, keepdims=True)) + EPSILON) * gain_vec

def rope_apply(values, positions):
    half_dim = values.shape[-1] // 2
    frequency = ROPE_BASE ** (-jnp.arange(half_dim, dtype=jnp.float32) / half_dim)
    angles = positions.astype(jnp.float32)[:, None] * frequency[None, :]
    cosine = jnp.cos(angles)[:, None, :]
    sine_v = jnp.sin(angles)[:, None, :]
    first_part = values[..., :half_dim]
    second = values[..., half_dim:]
    return jnp.concatenate([first_part * cosine - second * sine_v, second * cosine + first_part * sine_v], axis=-1)

def token_positions(device, dev_count, row_count, row_index):
    half_rows = row_count // 2
    return jnp.where(row_index < half_rows, device * half_rows + row_index, (2 * dev_count - 1 - device) * half_rows + row_index - half_rows).astype(jnp.int32)

def round_bf16(values):
    return lax.optimization_barrier(values.astype(jnp.bfloat16)).astype(jnp.float32)

def conv_silu(padded, conv_weight, conv_bias):
    taps_count = conv_weight.shape[0]
    length = padded.shape[0] - taps_count + 1
    summed = conv_bias[None, :]
    for offset in range(taps_count):
        summed = summed + conv_weight[offset][None, :] * padded[offset:offset + length]
    return jax.nn.silu(summed)

def mixer_inputs(padded, step_raw, conv_weight, conv_bias, step_bias, decay_log):
    conv_act = conv_silu(padded, conv_weight, conv_bias)
    x_heads = conv_act[:, :INNER].reshape(conv_act.shape[0], MHEADS, MHEAD_DIM)
    b_proj = conv_act[:, INNER:INNER + STATE]
    c_proj = conv_act[:, INNER + STATE:]
    step_size = jax.nn.softplus(step_raw + step_bias[None, :])
    decay_rate = -jnp.exp(decay_log)
    return (x_heads, step_size, decay_rate, b_proj, c_proj)

def span_local(x_heads, step_size, decay_rate, b_proj, c_proj, skip_gain):
    length = x_heads.shape[0]
    causal = jnp.arange(length)[:, None] >= jnp.arange(length)[None, :]
    cumulative = jnp.cumsum(step_size * decay_rate[None, :], axis=0)
    log_gap = cumulative[:, None, :] - cumulative[None, :, :]
    causal3 = causal[:, :, None]
    decay_mat = jnp.where(causal3, jnp.exp(jnp.where(causal3, log_gap, 0.0)), 0.0)
    intersection = jnp.dot(c_proj, b_proj.T, precision=HIGHEST)
    weights = decay_mat * intersection[:, :, None] * step_size[None, :, :]
    intra_out = jnp.einsum('tsh,shp->thp', weights, x_heads, precision=HIGHEST)
    local_out = intra_out + skip_gain[None, :, None] * x_heads
    tail_weight = jnp.exp(cumulative[-1][None, :] - cumulative) * step_size
    weighted_x = tail_weight[:, :, None] * x_heads
    fresh_state = jnp.einsum('shp,sn->hpn', weighted_x, b_proj, precision=HIGHEST)
    return (local_out, fresh_state, cumulative)

def carry_term(c_proj, cumulative, state_in):
    return jnp.einsum('tn,hpn->thp', c_proj, state_in, precision=HIGHEST) * jnp.exp(cumulative)[:, :, None]

def half_mixer(padded, step_raw, conv_weight, conv_bias, step_bias, decay_log, skip_gain, state_in):
    x_heads, step_size, decay_rate, b_proj, c_proj = mixer_inputs(padded, step_raw, conv_weight, conv_bias, step_bias, decay_log)
    local_out, fresh_state, cumulative = span_local(x_heads, step_size, decay_rate, b_proj, c_proj, skip_gain)
    result = local_out + carry_term(c_proj, cumulative, state_in)
    new_state = jnp.exp(cumulative[-1])[:, None, None] * state_in + fresh_state
    return (result.reshape(result.shape[0], INNER), new_state)

def mamba_sequence(conv_in, step_raw, conv_weight, conv_bias, step_bias, decay_log, skip_gain):
    total_rows = conv_in.shape[0]
    half_rows = TOK_DEV // 2
    spans = total_rows // half_rows
    padded = jnp.concatenate([jnp.zeros((CONV - 1, conv_in.shape[1]), jnp.float32), conv_in], axis=0)
    window_ids = jnp.arange(spans, dtype=jnp.int32)[:, None] * half_rows + jnp.arange(half_rows + CONV - 1, dtype=jnp.int32)[None, :]
    windows = padded[window_ids]
    step_spans = step_raw.reshape(spans, half_rows, MHEADS)

    def advance(state_in, block_item):
        result, new_state = half_mixer(block_item[0], block_item[1], conv_weight, conv_bias, step_bias, decay_log, skip_gain, state_in)
        return (new_state, result)
    start_state = jnp.zeros((MHEADS, MHEAD_DIM, STATE), jnp.float32)
    unused, results = lax.scan(advance, start_state, (windows, step_spans))
    return results.reshape(total_rows, INNER)

def gated_tail(ssm_out, gate_z, mamba_gain):
    return rms_scale(ssm_out * jax.nn.silu(gate_z), mamba_gain)

def attend_block(q_block, q_pos, keys_f, key_pos):
    scores = jnp.einsum('tkgd,skd->kgts', q_block, keys_f) * HEAD_DIM ** (-0.5)
    return jnp.where(key_pos[None, None, None, :] <= q_pos[None, None, :, None], scores, NEG_LARGE)

def attention_reference(queries, keys_b, values_b):
    total_rows = queries.shape[0]
    q_len = min(1024, total_rows)
    q_blocks = total_rows // q_len
    group_size = ATT_HEADS // KV_HEADS
    keys_f = keys_b.astype(jnp.float32).reshape(total_rows, KV_HEADS, HEAD_DIM)
    values_f = values_b.astype(jnp.float32).reshape(total_rows, KV_HEADS, HEAD_DIM)
    key_pos = jnp.arange(total_rows, dtype=jnp.int32)
    q_all = queries.astype(jnp.float32).reshape(q_blocks, q_len, KV_HEADS, group_size, HEAD_DIM)
    pos_all = key_pos.reshape(q_blocks, q_len)

    def forward_block(block_item):
        q_block, q_pos = block_item
        scores = attend_block(q_block, q_pos, keys_f, key_pos)
        peak = lax.optimization_barrier(jnp.max(scores, axis=-1, keepdims=True))
        log_total = peak[..., 0] + jnp.log(lax.optimization_barrier(jnp.sum(jnp.exp(scores - peak), axis=-1)))
        attn_prob = round_bf16(jnp.exp(scores - log_total[..., None]))
        result = jnp.einsum('kgts,skd->tkgd', attn_prob, values_f)
        return (result.reshape(q_len, ATT_HEADS * HEAD_DIM), log_total)
    results, log_totals = lax.map(forward_block, (q_all, pos_all))
    return (results.reshape(total_rows, ATT_HEADS * HEAD_DIM), log_totals)

def attention_grads(queries, keys_b, values_b, log_totals, attn_f32, grad_attn):
    total_rows = queries.shape[0]
    q_len = min(1024, total_rows)
    q_blocks = total_rows // q_len
    group_size = ATT_HEADS // KV_HEADS
    score_scale = HEAD_DIM ** (-0.5)
    keys_f = keys_b.astype(jnp.float32).reshape(total_rows, KV_HEADS, HEAD_DIM)
    values_f = values_b.astype(jnp.float32).reshape(total_rows, KV_HEADS, HEAD_DIM)
    key_pos = jnp.arange(total_rows, dtype=jnp.int32)
    q_all = queries.astype(jnp.float32).reshape(q_blocks, q_len, KV_HEADS, group_size, HEAD_DIM)
    d_all = grad_attn.astype(jnp.float32).reshape(q_blocks, q_len, KV_HEADS, group_size, HEAD_DIM)
    o_all = attn_f32.reshape(q_blocks, q_len, KV_HEADS, group_size, HEAD_DIM)
    pos_all = key_pos.reshape(q_blocks, q_len)

    def back_block(carried, block_item):
        grad_k, grad_v = carried
        q_block, d_block, o_block, q_pos, log_total = block_item
        scores = attend_block(q_block, q_pos, keys_f, key_pos)
        attn_prob = jnp.exp(scores - log_total[..., None])
        row_dot = jnp.transpose(lax.optimization_barrier(jnp.sum(d_block * o_block, axis=-1)), (1, 2, 0))
        grad_prob = jnp.einsum('tkgd,skd->kgts', d_block, values_f)
        grad_score = round_bf16(attn_prob * (grad_prob - row_dot[..., None]))
        grad_v = grad_v + jnp.einsum('kgts,tkgd->skd', round_bf16(attn_prob), d_block)
        grad_k = grad_k + jnp.einsum('kgts,tkgd->skd', grad_score, q_block) * score_scale
        grad_qb = jnp.einsum('kgts,skd->tkgd', grad_score, keys_f) * score_scale
        return ((grad_k, grad_v), grad_qb.reshape(q_len, ATT_HEADS, HEAD_DIM))
    zero_kv = jnp.zeros((total_rows, KV_HEADS, HEAD_DIM), jnp.float32)
    (grad_k, grad_v), grad_q = lax.scan(back_block, (zero_kv, zero_kv), (q_all, d_all, o_all, pos_all, log_totals))
    return (grad_q.reshape(total_rows, ATT_HEADS, HEAD_DIM), grad_k.reshape(total_rows, KV_HEADS * HEAD_DIM), grad_v.reshape(total_rows, KV_HEADS * HEAD_DIM))

def sequence_pass(residual, grad_top, norm_gain1, mix_in, step_proj, conv_weight, conv_bias, step_bias, decay_log, skip_gain, mamba_gain, mix_out, norm_gain2, mlp_in, mlp_out):
    total_rows = residual.shape[0]
    positions = jnp.arange(total_rows, dtype=jnp.int32)
    q_width = ATT_HEADS * HEAD_DIM
    kv_width = KV_HEADS * HEAD_DIM
    normed1 = rms_scale(residual, norm_gain1).astype(jnp.bfloat16)
    projected = jnp.dot(normed1, mix_in, preferred_element_type=jnp.float32)
    step_raw = jnp.dot(normed1, step_proj, preferred_element_type=jnp.float32)
    gate_z = projected[:, :INNER]
    conv_in = projected[:, INNER:INNER + CONV_CH]
    attn_cols = projected[:, INNER + CONV_CH:]
    q_raw = attn_cols[:, :q_width].reshape(total_rows, ATT_HEADS, HEAD_DIM)
    k_raw = attn_cols[:, q_width:q_width + kv_width].reshape(total_rows, KV_HEADS, HEAD_DIM)
    v_raw = attn_cols[:, q_width + kv_width:]
    ssm_out, mamba_back = jax.vjp(mamba_sequence, conv_in, step_raw, conv_weight, conv_bias, step_bias, decay_log, skip_gain)
    mamba_part, tail_back = jax.vjp(gated_tail, ssm_out, gate_z, mamba_gain)
    queries = rope_apply(q_raw, positions).astype(jnp.bfloat16)
    keys_b = rope_apply(k_raw, positions).reshape(total_rows, kv_width).astype(jnp.bfloat16)
    values_b = v_raw.astype(jnp.bfloat16)
    attn_f32, log_totals = attention_reference(queries, keys_b, values_b)
    joined = jnp.concatenate([mamba_part.astype(jnp.bfloat16), attn_f32.astype(jnp.bfloat16)], axis=1)
    middle = residual + jnp.dot(joined, mix_out, preferred_element_type=jnp.float32)
    normed2 = rms_scale(middle, norm_gain2).astype(jnp.bfloat16)
    up_proj = jnp.dot(normed2, mlp_in, preferred_element_type=jnp.float32)
    gate_part = up_proj[:, :FF]
    up_part = up_proj[:, FF:]
    activated = (jax.nn.silu(gate_part) * up_part).astype(jnp.bfloat16)
    outputs = middle + jnp.dot(activated, mlp_out, preferred_element_type=jnp.float32)
    grad_top_b = grad_top.astype(jnp.bfloat16)
    down_grad = jnp.dot(activated.T, grad_top_b, preferred_element_type=jnp.float32)
    grad_act = jnp.dot(grad_top_b, mlp_out.T, preferred_element_type=jnp.float32)
    sigmoid_g = jax.nn.sigmoid(gate_part)
    grad_gate = grad_act * up_part * sigmoid_g * (1.0 + gate_part * (1.0 - sigmoid_g))
    grad_up = grad_act * gate_part * sigmoid_g
    grad_mlp = jnp.concatenate([grad_gate, grad_up], axis=1).astype(jnp.bfloat16)
    up_grad = jnp.dot(normed2.T, grad_mlp, preferred_element_type=jnp.float32)
    grad_normed2 = jnp.dot(grad_mlp, mlp_in.T, preferred_element_type=jnp.float32)
    unused_two, norm_back2 = jax.vjp(rms_scale, middle, norm_gain2)
    grad_mid_n, gain2_part = norm_back2(grad_normed2)
    grad_middle = grad_top + grad_mid_n
    grad_mid_b = grad_middle.astype(jnp.bfloat16)
    mixout_grad = jnp.dot(joined.T, grad_mid_b, preferred_element_type=jnp.float32)
    grad_joined = jnp.dot(grad_mid_b, mix_out.T, preferred_element_type=jnp.float32)
    grad_ssm, grad_z, mgain_part = tail_back(grad_joined[:, :INNER])
    grad_attn = grad_joined[:, INNER:].astype(jnp.bfloat16)
    grad_q, grad_keys, grad_values = attention_grads(queries, keys_b, values_b, log_totals, attn_f32, grad_attn)
    unused_q, rope_back_q = jax.vjp(partial(rope_apply, positions=positions), q_raw)
    unused_k, rope_back_k = jax.vjp(partial(rope_apply, positions=positions), k_raw)
    grad_q_raw, = rope_back_q(grad_q)
    grad_k_raw, = rope_back_k(grad_keys.reshape(total_rows, KV_HEADS, HEAD_DIM))
    grad_conv, grad_steps, conv_w_grad, conv_b_grad, step_b_grad, decay_grad, skip_grad = mamba_back(grad_ssm)
    grad_proj = jnp.concatenate([grad_z, grad_conv, grad_q_raw.reshape(total_rows, q_width), grad_k_raw.reshape(total_rows, kv_width), grad_values], axis=1).astype(jnp.bfloat16)
    grad_step = grad_steps.astype(jnp.bfloat16)
    in_grad = jnp.dot(normed1.T, grad_proj, preferred_element_type=jnp.float32)
    step_grad = jnp.dot(normed1.T, grad_step, preferred_element_type=jnp.float32)
    grad_normed1 = jnp.dot(grad_proj, mix_in.T, preferred_element_type=jnp.float32) + jnp.dot(grad_step, step_proj.T, preferred_element_type=jnp.float32)
    unused_one, norm_back1 = jax.vjp(rms_scale, residual, norm_gain1)
    grad_res_n, gain1_part = norm_back1(grad_normed1)
    input_grad = grad_middle + grad_res_n
    grads = (gain1_part, in_grad, step_grad, conv_w_grad, conv_b_grad, step_b_grad, decay_grad, skip_grad, mgain_part, mixout_grad, gain2_part, up_grad, down_grad)
    return (outputs, input_grad, grads)

def reference(inputs, norm_gain1, mix_in, step_proj, conv_weight, conv_bias, step_bias, decay_log, skip_gain, mamba_gain, mix_out, norm_gain2, mlp_in, mlp_out, out_grad):
    row_ids = jnp.arange(SEQLEN, dtype=jnp.int32)
    layout_pos = token_positions(row_ids // TOK_DEV, N_CTX, TOK_DEV, row_ids % TOK_DEV)
    order = jnp.argsort(layout_pos).astype(jnp.int32)
    passes = [sequence_pass(inputs[seq_index][order], out_grad[seq_index][order], norm_gain1, mix_in, step_proj, conv_weight, conv_bias, step_bias, decay_log, skip_gain, mamba_gain, mix_out, norm_gain2, mlp_in, mlp_out) for seq_index in range(SEQS)]
    outputs = jnp.stack([entry[0][layout_pos] for entry in passes])
    input_grad = jnp.stack([entry[1][layout_pos] for entry in passes])
    sums = reduce(lambda left_tree, right_tree: jax.tree.map(jnp.add, left_tree, right_tree), [entry[2] for entry in passes])
    return (outputs, input_grad, sums[0], sums[1], sums[2], sums[3], sums[4], sums[5], sums[6], sums[7], sums[8], sums[9], sums[10], sums[11], sums[12])
```

```python
from functools import partial

import jax
import jax.numpy as jnp
from jax import lax
from jax.experimental import pallas as pl
from jax.experimental.pallas import tpu as pltpu
from jax.sharding import PartitionSpec as P

MHEADS = 24
MHEAD_DIM = 64
STATE = 128
CONV = 4
ATT_HEADS = 8
KV_HEADS = 2
HEAD_DIM = 64
FF = 2048
INNER = 1536
CONV_CH = 1792


EPSILON = 1e-05
ROPE_BASE = 10000.0
NEG_LARGE = -1e30
HIGHEST = lax.Precision.HIGHEST


def rms_scale(values, gain_vec):
    return (
        values * lax.rsqrt(jnp.mean(values * values, axis=-1, keepdims=True) + EPSILON) * gain_vec
    )


def rope_apply(values, positions):
    half_dim = values.shape[-1] // 2
    frequency = ROPE_BASE ** (-jnp.arange(half_dim, dtype=jnp.float32) / half_dim)
    angles = positions.astype(jnp.float32)[:, None] * frequency[None, :]
    cosine = jnp.cos(angles)[:, None, :]
    sine_v = jnp.sin(angles)[:, None, :]
    first_part = values[..., :half_dim]
    second = values[..., half_dim:]
    return jnp.concatenate(
        [first_part * cosine - second * sine_v, second * cosine + first_part * sine_v], axis=-1
    )


def token_positions(device, dev_count, row_count, row_index):
    half_rows = row_count // 2
    return jnp.where(
        row_index < half_rows,
        device * half_rows + row_index,
        (2 * dev_count - 1 - device) * half_rows + row_index - half_rows,
    )


def conv_silu(padded, conv_weight, conv_bias):
    taps_count = conv_weight.shape[0]
    length = padded.shape[0] - taps_count + 1
    summed = conv_bias[None, :]
    for offset in range(taps_count):
        summed = summed + conv_weight[offset][None, :] * padded[offset : offset + length]
    return jax.nn.silu(summed)


def mixer_inputs(padded, step_raw, conv_weight, conv_bias, step_bias, decay_log):
    conv_act = conv_silu(padded, conv_weight, conv_bias)
    x_heads = conv_act[:, :INNER].reshape(conv_act.shape[0], MHEADS, MHEAD_DIM)
    b_proj = conv_act[:, INNER : INNER + STATE]
    c_proj = conv_act[:, INNER + STATE :]
    step_size = jax.nn.softplus(step_raw + step_bias[None, :])
    decay_rate = -jnp.exp(decay_log)
    return (x_heads, step_size, decay_rate, b_proj, c_proj)


def span_local(x_heads, step_size, decay_rate, b_proj, c_proj, skip_gain):
    length = x_heads.shape[0]
    causal = jnp.arange(length)[:, None] >= jnp.arange(length)[None, :]
    cumulative = jnp.cumsum(step_size * decay_rate[None, :], axis=0)
    log_gap = cumulative[:, None, :] - cumulative[None, :, :]
    causal3 = causal[:, :, None]
    decay_mat = jnp.where(causal3, jnp.exp(jnp.where(causal3, log_gap, 0.0)), 0.0)
    intersection = jnp.dot(c_proj, b_proj.T, precision=HIGHEST)
    weights = decay_mat * intersection[:, :, None] * step_size[None, :, :]
    intra_out = jnp.einsum("tsh,shp->thp", weights, x_heads, precision=HIGHEST)
    local_out = intra_out + skip_gain[None, :, None] * x_heads
    tail_weight = jnp.exp(cumulative[-1][None, :] - cumulative) * step_size
    weighted_x = tail_weight[:, :, None] * x_heads
    fresh_state = jnp.einsum("shp,sn->hpn", weighted_x, b_proj, precision=HIGHEST)
    return (local_out, fresh_state, cumulative)


def carry_term(c_proj, cumulative, state_in):
    return (
        jnp.einsum("tn,hpn->thp", c_proj, state_in, precision=HIGHEST)
        * jnp.exp(cumulative)[:, :, None]
    )


def half_mixer(padded, step_raw, conv_weight, conv_bias, step_bias, decay_log, skip_gain, state_in):
    x_heads, step_size, decay_rate, b_proj, c_proj = mixer_inputs(
        padded, step_raw, conv_weight, conv_bias, step_bias, decay_log
    )
    local_out, fresh_state, cumulative = span_local(
        x_heads, step_size, decay_rate, b_proj, c_proj, skip_gain
    )
    result = local_out + carry_term(c_proj, cumulative, state_in)
    new_state = jnp.exp(cumulative[-1])[:, None, None] * state_in + fresh_state
    return (result.reshape(result.shape[0], INNER), new_state)


def gated_tail(ssm_out, gate_z, mamba_gain):
    return rms_scale(ssm_out * jax.nn.silu(gate_z), mamba_gain)


def score_block(q_groups, query_pos, key_block, pos_block):
    raw_scores = jnp.einsum(
        "tkgd,skd->kgts", q_groups, key_block, preferred_element_type=jnp.float32
    ) * HEAD_DIM ** (-0.5)
    return jnp.where(
        pos_block[None, None, None, :] <= query_pos[None, None, :, None], raw_scores, NEG_LARGE
    )


def split_blocks(all_keys, all_values, key_pos):
    key_count = all_keys.shape[0]
    block_len = min(2048, key_count)
    blocks = key_count // block_len
    return (
        all_keys.reshape(blocks, block_len, KV_HEADS, HEAD_DIM),
        all_values.reshape(blocks, block_len, KV_HEADS, HEAD_DIM),
        key_pos.reshape(blocks, block_len),
    )


def attention_forward(queries, all_keys, all_values, query_pos, key_pos):
    row_count = queries.shape[0]
    group_size = ATT_HEADS // KV_HEADS
    q_groups = queries.reshape(row_count, KV_HEADS, group_size, HEAD_DIM)
    key_blocks, value_blocks, pos_blocks = split_blocks(all_keys, all_values, key_pos)

    def max_step(carried, block_item):
        running_max, running_sum = carried
        scores = score_block(q_groups, query_pos, block_item[0], block_item[1])
        new_max = jnp.maximum(running_max, jnp.max(scores, axis=-1))
        running_sum = running_sum * jnp.exp(running_max - new_max) + jnp.sum(
            jnp.exp(scores - new_max[..., None]), axis=-1
        )
        return ((new_max, running_sum), None)

    start_max = jnp.full((KV_HEADS, group_size, row_count), NEG_LARGE, jnp.float32)
    (final_max, final_sum), unused = lax.scan(
        max_step, (start_max, jnp.zeros_like(start_max)), (key_blocks, pos_blocks)
    )
    log_total = final_max + jnp.log(final_sum)

    def out_step(weighted, block_item):
        scores = score_block(q_groups, query_pos, block_item[0], block_item[2])
        attn_prob = jnp.exp(scores - log_total[..., None]).astype(jnp.bfloat16)
        return (
            weighted
            + jnp.einsum(
                "kgts,skd->tkgd", attn_prob, block_item[1], preferred_element_type=jnp.float32
            ),
            None,
        )

    start_out = jnp.zeros((row_count, KV_HEADS, group_size, HEAD_DIM), jnp.float32)
    weighted, unused_two = lax.scan(out_step, start_out, (key_blocks, value_blocks, pos_blocks))
    return (weighted.reshape(row_count, ATT_HEADS * HEAD_DIM), log_total)


def attention_backward(
    queries, all_keys, all_values, query_pos, key_pos, log_total, attn_f32, grad_attn
):
    row_count = queries.shape[0]
    key_count = all_keys.shape[0]
    group_size = ATT_HEADS // KV_HEADS
    score_scale = HEAD_DIM ** (-0.5)
    q_groups = queries.reshape(row_count, KV_HEADS, group_size, HEAD_DIM)
    d_groups = grad_attn.reshape(row_count, KV_HEADS, group_size, HEAD_DIM)
    row_dot = jnp.sum(
        (grad_attn.astype(jnp.float32) * attn_f32).reshape(
            row_count, KV_HEADS, group_size, HEAD_DIM
        ),
        axis=-1,
    )
    row_dot = jnp.transpose(row_dot, (1, 2, 0))
    key_blocks, value_blocks, pos_blocks = split_blocks(all_keys, all_values, key_pos)

    def grad_step(grad_q, block_item):
        key_block, value_block, pos_block = block_item
        scores = score_block(q_groups, query_pos, key_block, pos_block)
        attn_prob = jnp.exp(scores - log_total[..., None])
        grad_prob = jnp.einsum(
            "tkgd,skd->kgts", d_groups, value_block, preferred_element_type=jnp.float32
        )
        grad_score = (attn_prob * (grad_prob - row_dot[..., None])).astype(jnp.bfloat16)
        grad_vb = jnp.einsum(
            "kgts,tkgd->skd",
            attn_prob.astype(jnp.bfloat16),
            d_groups,
            preferred_element_type=jnp.float32,
        )
        grad_kb = (
            jnp.einsum("kgts,tkgd->skd", grad_score, q_groups, preferred_element_type=jnp.float32)
            * score_scale
        )
        grad_q = (
            grad_q
            + jnp.einsum(
                "kgts,skd->tkgd", grad_score, key_block, preferred_element_type=jnp.float32
            )
            * score_scale
        )
        return (grad_q, (grad_kb, grad_vb))

    start_q = jnp.zeros((row_count, KV_HEADS, group_size, HEAD_DIM), jnp.float32)
    grad_q, (grad_keys, grad_values) = lax.scan(
        grad_step, start_q, (key_blocks, value_blocks, pos_blocks)
    )
    return (
        grad_q.reshape(row_count, ATT_HEADS, HEAD_DIM),
        grad_keys.reshape(key_count, KV_HEADS * HEAD_DIM),
        grad_values.reshape(key_count, KV_HEADS * HEAD_DIM),
    )


def chain_scan(fresh, decays, reverse):
    dev_count, _, rows, width = fresh.shape
    spans = 2 * dev_count

    def kernel(fresh_ref, decay_ref, out_ref):
        state = jnp.zeros((rows, width), jnp.float32)
        for step in range(spans):
            at = spans - 1 - step if reverse else step
            dev, half = (at, 0) if at < dev_count else (spans - 1 - at, 1)
            out_ref[dev, half] = state.astype(jnp.bfloat16)
            state = decay_ref[:, at : at + 1] * state + fresh_ref[dev, half].astype(jnp.float32)

    return pl.pallas_call(
        kernel, out_shape=jax.ShapeDtypeStruct(fresh.shape, jnp.bfloat16), name="chain_scan"
    )(fresh, decays)


def swap(array):
    return lax.ppermute(array, "wsh", [(0, 1), (1, 0)])


def half_pair(values, dev_count, core):
    tokens, width = values.shape
    blocks = values.T.reshape(dev_count, 2, width // (2 * dev_count), tokens)
    own = lax.dynamic_index_in_dim(blocks, core, 1, keepdims=False)
    other = lax.dynamic_index_in_dim(blocks, 1 - core, 1, keepdims=False)
    joined = jnp.concatenate([own, swap(other)], axis=-1)
    return joined.reshape(width // 2, 2 * tokens)


def both_cores(values):
    return jnp.concatenate([values, swap(values)], axis=0)


def exchange(array):
    return lax.all_to_all(array, "ctx", 0, 0, tiled=True)


def butterfly_sum(array):
    array = array + swap(array)
    size = lax.axis_size("ctx")
    step = 1
    while step < size:
        array = array + lax.ppermute(array, "ctx", [(i, i ^ step) for i in range(size)])
        step *= 2
    return array


def body(
    inputs,
    norm_gain1,
    mix_in,
    step_proj,
    conv_weight,
    conv_bias,
    step_bias,
    decay_log,
    skip_gain,
    mamba_gain,
    mix_out,
    norm_gain2,
    mlp_in,
    mlp_out,
    out_grad,
):
    residual = inputs[0]
    row_count, width = residual.shape
    half_rows = row_count // 2
    rim_len = CONV - 1
    q_width = ATT_HEADS * HEAD_DIM
    kv_width = KV_HEADS * HEAD_DIM
    dev_count = lax.axis_size("ctx")
    device = lax.axis_index("ctx")
    core = lax.axis_index("wsh")
    is_last = device == dev_count - 1
    state_rows = MHEADS * MHEAD_DIM // dev_count
    in_rows = mix_in.shape[0]
    out_rows = mix_out.shape[0]
    up = [(i, i + 1) for i in range(dev_count - 1)]
    down = [(j, i) for i, j in up]
    local_pos = token_positions(
        device, dev_count, row_count, jnp.arange(row_count, dtype=jnp.int32)
    )
    key_ids = jnp.arange(row_count * dev_count, dtype=jnp.int32)
    key_pos = token_positions(key_ids // row_count, dev_count, row_count, key_ids % row_count)
    full_in = lax.all_gather(mix_in, ("ctx", "wsh"), axis=0, tiled=True)
    packed = jnp.concatenate(
        [jnp.concatenate([mlp_in[:, :FF], mlp_in[:, FF:]], axis=0), mix_out, mlp_out], axis=1
    )
    full_in, packed = lax.optimization_barrier((full_in, packed))
    gathered = lax.all_gather(packed, ("ctx", "wsh"), axis=0)
    full_gate = gathered[:, :in_rows, :FF].reshape(width, FF)
    full_upw = gathered[:, in_rows:, :FF].reshape(width, FF)
    full_out = gathered[:, :, FF : FF + width].reshape(-1, width)
    full_down = gathered[:, :, FF + width :].reshape(-1, width)

    normed1 = rms_scale(residual, norm_gain1).astype(jnp.bfloat16)
    tail_first = normed1[half_rows - rim_len : half_rows]
    tail_second = normed1[row_count - rim_len :]
    rim_first = lax.ppermute(tail_first, "ctx", up)
    rim_second = jnp.where(is_last, tail_first, lax.ppermute(tail_second, "ctx", down))
    spare = 16 - 2 * rim_len
    extended = jnp.concatenate(
        [normed1, rim_first, rim_second, jnp.zeros((spare, width), jnp.bfloat16)], axis=0
    )
    step_raw = jnp.dot(normed1, step_proj, preferred_element_type=jnp.float32)
    step_pair = step_raw.reshape(2, half_rows, MHEADS)
    early_steps = jax.nn.softplus(step_pair + step_bias[None, None, :])
    decays = jnp.exp(jnp.sum(early_steps * -jnp.exp(decay_log), axis=1))
    all_decays = exchange(
        jnp.broadcast_to(decays.reshape(1, 2 * MHEADS), (dev_count, 2 * MHEADS))
    ).reshape(dev_count, 2, MHEADS)
    span_decays = jnp.concatenate([all_decays[:, 0], all_decays[::-1, 1]], axis=0)
    row_head = (device * state_rows + jnp.arange(state_rows)) // MHEAD_DIM
    row_pick = (row_head[:, None] == jnp.arange(MHEADS)[None, :]).astype(jnp.float32)
    row_decays = jnp.dot(row_pick, span_decays.T, precision=HIGHEST)
    grad_top = out_grad[0]
    grad_top_b = grad_top.astype(jnp.bfloat16)

    projected = jnp.dot(extended, full_in, preferred_element_type=jnp.float32)
    gate_z = projected[:row_count, :INNER]
    conv_all = projected[:, INNER : INNER + CONV_CH]
    attn_cols = projected[:row_count, INNER + CONV_CH :]
    q_raw = attn_cols[:, :q_width].reshape(row_count, ATT_HEADS, HEAD_DIM)
    k_raw = attn_cols[:, q_width : q_width + kv_width].reshape(row_count, KV_HEADS, HEAD_DIM)
    v_raw = attn_cols[:, q_width + kv_width :]
    padded = jnp.stack(
        [
            jnp.concatenate(
                [conv_all[row_count : row_count + rim_len], conv_all[:half_rows]], axis=0
            ),
            jnp.concatenate(
                [
                    conv_all[row_count + rim_len : row_count + 2 * rim_len],
                    conv_all[half_rows:row_count],
                ],
                axis=0,
            ),
        ]
    )

    def local_parts(padded_one, step_one):
        x_heads, step_size, decay_rate, b_proj, c_proj = mixer_inputs(
            padded_one, step_one, conv_weight, conv_bias, step_bias, decay_log
        )
        local_out, fresh_state, cumulative = span_local(
            x_heads, step_size, decay_rate, b_proj, c_proj, skip_gain
        )
        return (local_out, fresh_state, cumulative, c_proj)

    local_out, fresh_state, cumulative, c_proj = jax.vmap(local_parts)(padded, step_pair)
    queries = rope_apply(q_raw, local_pos).astype(jnp.bfloat16)
    keys_local = rope_apply(k_raw, local_pos).reshape(row_count, kv_width).astype(jnp.bfloat16)

    def to_slices(states):
        return (
            states.astype(jnp.bfloat16)
            .reshape(2, dev_count, state_rows, STATE)
            .transpose(1, 0, 2, 3)
            .reshape(dev_count, 2 * state_rows, STATE)
        )

    def from_slices(slices):
        return (
            slices.reshape(dev_count, 2, state_rows, STATE)
            .transpose(1, 0, 2, 3)
            .reshape(2, MHEADS, MHEAD_DIM, STATE)
            .astype(jnp.float32)
        )

    kv_local = jnp.concatenate([keys_local, v_raw.astype(jnp.bfloat16)], axis=0)
    arrived = exchange(
        jnp.concatenate(
            [
                to_slices(fresh_state),
                jnp.broadcast_to(kv_local[None], (dev_count, 2 * row_count, kv_width)),
            ],
            axis=1,
        )
    )
    fresh_all = arrived[:, : 2 * state_rows].reshape(dev_count, 2, state_rows, STATE)
    all_keys = arrived[:, 2 * state_rows : 2 * state_rows + row_count].reshape(-1, kv_width)
    all_values = arrived[:, 2 * state_rows + row_count :].reshape(-1, kv_width)
    entering = chain_scan(fresh_all, row_decays, False)
    states = from_slices(exchange(entering.reshape(dev_count, 2 * state_rows, STATE)))
    ssm_out = (local_out + jax.vmap(carry_term)(c_proj, cumulative, states)).reshape(
        row_count, INNER
    )
    mamba_part = gated_tail(ssm_out, gate_z, mamba_gain)
    attn_f32, log_total = attention_forward(queries, all_keys, all_values, local_pos, key_pos)
    joined = jnp.concatenate(
        [mamba_part.astype(jnp.bfloat16), attn_f32.astype(jnp.bfloat16)], axis=1
    )
    middle = residual + jnp.dot(joined, full_out, preferred_element_type=jnp.float32)
    normed2 = rms_scale(middle, norm_gain2).astype(jnp.bfloat16)
    gate_part = jnp.dot(normed2, full_gate, preferred_element_type=jnp.float32)
    up_part = jnp.dot(normed2, full_upw, preferred_element_type=jnp.float32)
    activated = (jax.nn.silu(gate_part) * up_part).astype(jnp.bfloat16)
    outputs = middle + jnp.dot(activated, full_down, preferred_element_type=jnp.float32)
    grad_act = jnp.dot(grad_top_b, full_down.T, preferred_element_type=jnp.float32)
    sigmoid_g = jax.nn.sigmoid(gate_part)
    grad_gate = (grad_act * up_part * sigmoid_g * (1.0 + gate_part * (1.0 - sigmoid_g))).astype(
        jnp.bfloat16
    )
    grad_up = (grad_act * gate_part * sigmoid_g).astype(jnp.bfloat16)
    grad_normed2 = jnp.dot(grad_gate, full_gate.T, preferred_element_type=jnp.float32) + jnp.dot(
        grad_up, full_upw.T, preferred_element_type=jnp.float32
    )
    unused_two, norm_back2 = jax.vjp(rms_scale, middle, norm_gain2)
    grad_mid_n, gain2_part = norm_back2(grad_normed2)
    grad_middle = grad_top + grad_mid_n
    grad_mid_b = grad_middle.astype(jnp.bfloat16)

    def half_grad(values, grads):
        return jnp.dot(
            half_pair(values, dev_count, core),
            both_cores(grads),
            preferred_element_type=jnp.float32,
        ).astype(jnp.bfloat16)

    down_half = half_grad(activated, grad_top_b).reshape(dev_count, out_rows, width)
    up_half = half_grad(normed2, jnp.concatenate([grad_gate, grad_up], axis=1)).reshape(
        dev_count, in_rows, 2 * FF
    )
    mixout_half = half_grad(joined, grad_mid_b).reshape(dev_count, out_rows, width)
    grad_pack = jnp.concatenate(
        [
            jnp.concatenate([up_half[:, :, :FF], up_half[:, :, FF:]], axis=1),
            mixout_half,
            down_half,
        ],
        axis=2,
    ).reshape(dev_count * out_rows, -1)
    pack_shard = lax.psum_scatter(grad_pack, "ctx", scatter_dimension=0, tiled=True)

    grad_joined = jnp.dot(grad_mid_b, full_out.T, preferred_element_type=jnp.float32)
    unused_tail, tail_back = jax.vjp(gated_tail, ssm_out, gate_z, mamba_gain)
    grad_ssm, grad_z, mgain_part = tail_back(grad_joined[:, :INNER])
    grad_pair = grad_ssm.reshape(2, half_rows, INNER)
    grad_heads = grad_ssm.reshape(2, half_rows, MHEADS, MHEAD_DIM)
    own_grads = jnp.einsum(
        "athp,atn->ahpn",
        grad_heads * jnp.exp(cumulative)[:, :, :, None],
        c_proj,
        precision=HIGHEST,
    )
    grad_attn = grad_joined[:, INNER:].astype(jnp.bfloat16)
    grad_q, grad_keys, grad_values = attention_backward(
        queries, all_keys, all_values, local_pos, key_pos, log_total, attn_f32, grad_attn
    )
    kv_grads = jnp.concatenate(
        [
            grad_keys.astype(jnp.bfloat16).reshape(dev_count, row_count, kv_width),
            grad_values.astype(jnp.bfloat16).reshape(dev_count, row_count, kv_width),
        ],
        axis=1,
    )
    returned = exchange(jnp.concatenate([to_slices(own_grads), kv_grads], axis=1))
    own_all = returned[:, : 2 * state_rows].reshape(dev_count, 2, state_rows, STATE)
    kv_back = jnp.sum(returned[:, 2 * state_rows :].astype(jnp.float32), axis=0)
    keys_back = kv_back[:row_count]
    values_back = kv_back[row_count:]
    leaving = chain_scan(own_all, row_decays, True)
    end_grads = from_slices(exchange(leaving.reshape(dev_count, 2 * state_rows, STATE)))
    unused_q, rope_back_q = jax.vjp(partial(rope_apply, positions=local_pos), q_raw)
    unused_k, rope_back_k = jax.vjp(partial(rope_apply, positions=local_pos), k_raw)
    (grad_q_raw,) = rope_back_q(grad_q)
    (grad_k_raw,) = rope_back_k(keys_back.reshape(row_count, KV_HEADS, HEAD_DIM))
    pair_mixer = jax.vmap(half_mixer, in_axes=(0, 0, None, None, None, None, None, 0))
    unused_m, mixer_back = jax.vjp(
        pair_mixer,
        padded,
        step_pair,
        conv_weight,
        conv_bias,
        step_bias,
        decay_log,
        skip_gain,
        states,
    )
    mixer_grads = mixer_back((grad_pair, end_grads))
    grad_padded = mixer_grads[0]
    grad_rims = grad_padded[:, :rim_len].reshape(2 * rim_len, CONV_CH)
    grad_conv = grad_padded[:, rim_len:].reshape(row_count, CONV_CH)
    grad_proj = jnp.concatenate(
        [
            jnp.concatenate(
                [
                    grad_z,
                    grad_conv,
                    grad_q_raw.reshape(row_count, q_width),
                    grad_k_raw.reshape(row_count, kv_width),
                    values_back,
                ],
                axis=1,
            ).astype(jnp.bfloat16),
            jnp.pad(
                grad_rims.astype(jnp.bfloat16), ((0, spare), (INNER, q_width + 2 * kv_width))
            ),
        ],
        axis=0,
    )
    in_half = half_grad(extended, grad_proj)
    in_shard = lax.psum_scatter(in_half, "ctx", scatter_dimension=0, tiled=True)
    grad_step = mixer_grads[1].reshape(row_count, MHEADS).astype(jnp.bfloat16)
    step_grad = jnp.dot(grad_step.T, normed1, preferred_element_type=jnp.float32)
    grad_ext = jnp.dot(grad_proj, full_in.T, preferred_element_type=jnp.float32)
    back_first = grad_ext[row_count : row_count + rim_len]
    back_second = grad_ext[row_count + rim_len : row_count + 2 * rim_len]
    add_first = lax.ppermute(back_first, "ctx", down) + jnp.where(is_last, back_second, 0.0)
    add_second = lax.ppermute(back_second, "ctx", up)
    fill = jnp.zeros((half_rows - rim_len, width), jnp.float32)
    grad_normed1 = (
        grad_ext[:row_count]
        + jnp.concatenate([fill, add_first, fill, add_second], axis=0)
        + jnp.dot(grad_step, step_proj.T, preferred_element_type=jnp.float32)
    )
    unused_one, norm_back1 = jax.vjp(rms_scale, residual, norm_gain1)
    grad_res_n, gain1_part = norm_back1(grad_normed1)
    input_grad = grad_middle + grad_res_n
    parts = (
        gain1_part,
        step_grad,
        mixer_grads[2],
        mixer_grads[3],
        mgain_part,
        gain2_part,
        mixer_grads[4],
        mixer_grads[5],
        mixer_grads[6],
    )
    flat = jnp.concatenate([part.reshape(-1) for part in parts])
    total_len = flat.shape[0]
    summed = butterfly_sum(jnp.pad(flat, (0, -total_len % 1024)).reshape(-1, 128)).reshape(-1)
    sums = []
    start = 0
    for part in parts:
        sums.append(summed[start : start + part.size].reshape(part.shape))
        start += part.size
    pack_f32 = pack_shard.astype(jnp.float32)
    up_shard = jnp.concatenate([pack_f32[:in_rows, :FF], pack_f32[in_rows:, :FF]], axis=1)
    return (
        outputs[None],
        input_grad[None],
        sums[0],
        in_shard.astype(jnp.float32),
        sums[1].T,
        sums[2],
        sums[3],
        sums[6],
        sums[7],
        sums[8],
        sums[4],
        pack_f32[:, FF : FF + width],
        sums[5],
        up_shard,
        pack_f32[:, FF + width :],
    )


def solution(mesh):
    return jax.shard_map(
        body,
        mesh=mesh,
        in_specs=(
            P("wsh", "ctx", None),
            P(),
            P(("ctx", "wsh"), None),
            P(),
            P(),
            P(),
            P(),
            P(),
            P(),
            P(),
            P(("ctx", "wsh"), None),
            P(),
            P(("ctx", "wsh"), None),
            P(("ctx", "wsh"), None),
            P("wsh", "ctx", None),
        ),
        out_specs=(
            P("wsh", "ctx", None),
            P("wsh", "ctx", None),
            P(),
            P(("ctx", "wsh"), None),
            P(),
            P(),
            P(),
            P(),
            P(),
            P(),
            P(),
            P(("ctx", "wsh"), None),
            P(),
            P(("ctx", "wsh"), None),
            P(("ctx", "wsh"), None),
        ),
        check_vma=False,
    )
```

```python
from functools import partial

import jax
import jax.numpy as jnp
from jax import lax
from jax.experimental import pallas as pl
from jax.experimental.pallas import tpu as pltpu
from jax.sharding import PartitionSpec as P

MHEADS = 24
MHEAD_DIM = 64
STATE = 128
CONV = 4
ATT_HEADS = 8
KV_HEADS = 2
HEAD_DIM = 64
FF = 2048
INNER = 1536
CONV_CH = 1792


EPSILON = 1e-05
ROPE_BASE = 10000.0
NEG_LARGE = -1e30
HIGHEST = lax.Precision.HIGHEST


def rms_scale(values, gain_vec):
    return (
        values * lax.rsqrt(jnp.mean(values * values, axis=-1, keepdims=True) + EPSILON) * gain_vec
    )


def rope_apply(values, positions):
    half_dim = values.shape[-1] // 2
    frequency = ROPE_BASE ** (-jnp.arange(half_dim, dtype=jnp.float32) / half_dim)
    angles = positions.astype(jnp.float32)[:, None] * frequency[None, :]
    cosine = jnp.cos(angles)[:, None, :]
    sine_v = jnp.sin(angles)[:, None, :]
    first_part = values[..., :half_dim]
    second = values[..., half_dim:]
    return jnp.concatenate(
        [first_part * cosine - second * sine_v, second * cosine + first_part * sine_v], axis=-1
    )


def token_positions(device, dev_count, row_count, row_index):
    half_rows = row_count // 2
    return jnp.where(
        row_index < half_rows,
        device * half_rows + row_index,
        (2 * dev_count - 1 - device) * half_rows + row_index - half_rows,
    )


def conv_silu(padded, conv_weight, conv_bias):
    taps_count = conv_weight.shape[0]
    length = padded.shape[0] - taps_count + 1
    summed = conv_bias[None, :]
    for offset in range(taps_count):
        summed = summed + conv_weight[offset][None, :] * padded[offset : offset + length]
    return jax.nn.silu(summed)


def mixer_inputs(padded, step_raw, conv_weight, conv_bias, step_bias, decay_log):
    conv_act = conv_silu(padded, conv_weight, conv_bias)
    x_heads = conv_act[:, :INNER].reshape(conv_act.shape[0], MHEADS, MHEAD_DIM)
    b_proj = conv_act[:, INNER : INNER + STATE]
    c_proj = conv_act[:, INNER + STATE :]
    step_size = jax.nn.softplus(step_raw + step_bias[None, :])
    decay_rate = -jnp.exp(decay_log)
    return (x_heads, step_size, decay_rate, b_proj, c_proj)


def span_local(x_heads, step_size, decay_rate, b_proj, c_proj, skip_gain):
    length = x_heads.shape[0]
    causal = jnp.arange(length)[:, None] >= jnp.arange(length)[None, :]
    cumulative = jnp.cumsum(step_size * decay_rate[None, :], axis=0)
    log_gap = cumulative[:, None, :] - cumulative[None, :, :]
    causal3 = causal[:, :, None]
    decay_mat = jnp.where(causal3, jnp.exp(jnp.where(causal3, log_gap, 0.0)), 0.0)
    intersection = jnp.dot(c_proj, b_proj.T, precision=HIGHEST)
    weights = decay_mat * intersection[:, :, None] * step_size[None, :, :]
    intra_out = jnp.einsum("tsh,shp->thp", weights, x_heads, precision=HIGHEST)
    local_out = intra_out + skip_gain[None, :, None] * x_heads
    tail_weight = jnp.exp(cumulative[-1][None, :] - cumulative) * step_size
    weighted_x = tail_weight[:, :, None] * x_heads
    fresh_state = jnp.einsum("shp,sn->hpn", weighted_x, b_proj, precision=HIGHEST)
    return (local_out, fresh_state, cumulative)


def carry_term(c_proj, cumulative, state_in):
    return (
        jnp.einsum("tn,hpn->thp", c_proj, state_in, precision=HIGHEST)
        * jnp.exp(cumulative)[:, :, None]
    )


def half_mixer(padded, step_raw, conv_weight, conv_bias, step_bias, decay_log, skip_gain, state_in):
    x_heads, step_size, decay_rate, b_proj, c_proj = mixer_inputs(
        padded, step_raw, conv_weight, conv_bias, step_bias, decay_log
    )
    local_out, fresh_state, cumulative = span_local(
        x_heads, step_size, decay_rate, b_proj, c_proj, skip_gain
    )
    result = local_out + carry_term(c_proj, cumulative, state_in)
    new_state = jnp.exp(cumulative[-1])[:, None, None] * state_in + fresh_state
    return (result.reshape(result.shape[0], INNER), new_state)


def gated_tail(ssm_out, gate_z, mamba_gain):
    return rms_scale(ssm_out * jax.nn.silu(gate_z), mamba_gain)


def score_block(q_groups, query_pos, key_block, pos_block):
    raw_scores = jnp.einsum(
        "tkgd,skd->kgts", q_groups, key_block, preferred_element_type=jnp.float32
    ) * HEAD_DIM ** (-0.5)
    return jnp.where(
        pos_block[None, None, None, :] <= query_pos[None, None, :, None], raw_scores, NEG_LARGE
    )


def split_blocks(all_keys, all_values, key_pos):
    key_count = all_keys.shape[0]
    block_len = min(2048, key_count)
    blocks = key_count // block_len
    return (
        all_keys.reshape(blocks, block_len, KV_HEADS, HEAD_DIM),
        all_values.reshape(blocks, block_len, KV_HEADS, HEAD_DIM),
        key_pos.reshape(blocks, block_len),
    )


def attention_forward(queries, all_keys, all_values, query_pos, key_pos):
    row_count = queries.shape[0]
    group_size = ATT_HEADS // KV_HEADS
    q_groups = queries.reshape(row_count, KV_HEADS, group_size, HEAD_DIM)
    key_blocks, value_blocks, pos_blocks = split_blocks(all_keys, all_values, key_pos)

    def max_step(carried, block_item):
        running_max, running_sum = carried
        scores = score_block(q_groups, query_pos, block_item[0], block_item[1])
        new_max = jnp.maximum(running_max, jnp.max(scores, axis=-1))
        running_sum = running_sum * jnp.exp(running_max - new_max) + jnp.sum(
            jnp.exp(scores - new_max[..., None]), axis=-1
        )
        return ((new_max, running_sum), None)

    start_max = jnp.full((KV_HEADS, group_size, row_count), NEG_LARGE, jnp.float32)
    (final_max, final_sum), unused = lax.scan(
        max_step, (start_max, jnp.zeros_like(start_max)), (key_blocks, pos_blocks)
    )
    log_total = final_max + jnp.log(final_sum)

    def out_step(weighted, block_item):
        scores = score_block(q_groups, query_pos, block_item[0], block_item[2])
        attn_prob = jnp.exp(scores - log_total[..., None]).astype(jnp.bfloat16)
        return (
            weighted
            + jnp.einsum(
                "kgts,skd->tkgd", attn_prob, block_item[1], preferred_element_type=jnp.float32
            ),
            None,
        )

    start_out = jnp.zeros((row_count, KV_HEADS, group_size, HEAD_DIM), jnp.float32)
    weighted, unused_two = lax.scan(out_step, start_out, (key_blocks, value_blocks, pos_blocks))
    return (weighted.reshape(row_count, ATT_HEADS * HEAD_DIM), log_total)


def attention_backward(
    queries, all_keys, all_values, query_pos, key_pos, log_total, attn_f32, grad_attn
):
    row_count = queries.shape[0]
    key_count = all_keys.shape[0]
    group_size = ATT_HEADS // KV_HEADS
    score_scale = HEAD_DIM ** (-0.5)
    q_groups = queries.reshape(row_count, KV_HEADS, group_size, HEAD_DIM)
    d_groups = grad_attn.reshape(row_count, KV_HEADS, group_size, HEAD_DIM)
    row_dot = jnp.sum(
        (grad_attn.astype(jnp.float32) * attn_f32).reshape(
            row_count, KV_HEADS, group_size, HEAD_DIM
        ),
        axis=-1,
    )
    row_dot = jnp.transpose(row_dot, (1, 2, 0))
    key_blocks, value_blocks, pos_blocks = split_blocks(all_keys, all_values, key_pos)

    def grad_step(grad_q, block_item):
        key_block, value_block, pos_block = block_item
        scores = score_block(q_groups, query_pos, key_block, pos_block)
        attn_prob = jnp.exp(scores - log_total[..., None])
        grad_prob = jnp.einsum(
            "tkgd,skd->kgts", d_groups, value_block, preferred_element_type=jnp.float32
        )
        grad_score = (attn_prob * (grad_prob - row_dot[..., None])).astype(jnp.bfloat16)
        grad_vb = jnp.einsum(
            "kgts,tkgd->skd",
            attn_prob.astype(jnp.bfloat16),
            d_groups,
            preferred_element_type=jnp.float32,
        )
        grad_kb = (
            jnp.einsum("kgts,tkgd->skd", grad_score, q_groups, preferred_element_type=jnp.float32)
            * score_scale
        )
        grad_q = (
            grad_q
            + jnp.einsum(
                "kgts,skd->tkgd", grad_score, key_block, preferred_element_type=jnp.float32
            )
            * score_scale
        )
        return (grad_q, (grad_kb, grad_vb))

    start_q = jnp.zeros((row_count, KV_HEADS, group_size, HEAD_DIM), jnp.float32)
    grad_q, (grad_keys, grad_values) = lax.scan(
        grad_step, start_q, (key_blocks, value_blocks, pos_blocks)
    )
    return (
        grad_q.reshape(row_count, ATT_HEADS, HEAD_DIM),
        grad_keys.reshape(key_count, KV_HEADS * HEAD_DIM),
        grad_values.reshape(key_count, KV_HEADS * HEAD_DIM),
    )


def chain_scan(fresh, decays, reverse):
    dev_count, _, rows, width = fresh.shape
    spans = 2 * dev_count

    def kernel(fresh_ref, decay_ref, out_ref):
        state = jnp.zeros((rows, width), jnp.float32)
        for step in range(spans):
            at = spans - 1 - step if reverse else step
            dev, half = (at, 0) if at < dev_count else (spans - 1 - at, 1)
            out_ref[dev, half] = state.astype(jnp.bfloat16)
            state = decay_ref[:, at : at + 1] * state + fresh_ref[dev, half].astype(jnp.float32)

    return pl.pallas_call(
        kernel, out_shape=jax.ShapeDtypeStruct(fresh.shape, jnp.bfloat16), name="chain_scan"
    )(fresh, decays)


def swap(array):
    return lax.ppermute(array, "wsh", [(0, 1), (1, 0)])


def half_pair(values, dev_count, core):
    tokens, width = values.shape
    blocks = values.T.reshape(dev_count, 2, width // (2 * dev_count), tokens)
    own = lax.dynamic_index_in_dim(blocks, core, 1, keepdims=False)
    other = lax.dynamic_index_in_dim(blocks, 1 - core, 1, keepdims=False)
    joined = jnp.concatenate([own, swap(other)], axis=-1)
    return joined.reshape(width // 2, 2 * tokens)


def both_cores(values):
    return jnp.concatenate([values, swap(values)], axis=0)


def exchange(array):
    return lax.all_to_all(array, "ctx", 0, 0, tiled=True)


def butterfly_sum(array):
    array = array + swap(array)
    size = lax.axis_size("ctx")
    step = 1
    while step < size:
        array = array + lax.ppermute(array, "ctx", [(i, i ^ step) for i in range(size)])
        step *= 2
    return array


def body(
    inputs,
    norm_gain1,
    mix_in,
    step_proj,
    conv_weight,
    conv_bias,
    step_bias,
    decay_log,
    skip_gain,
    mamba_gain,
    mix_out,
    norm_gain2,
    mlp_in,
    mlp_out,
    out_grad,
):
    residual = inputs[0]
    row_count, width = residual.shape
    half_rows = row_count // 2
    rim_len = CONV - 1
    q_width = ATT_HEADS * HEAD_DIM
    kv_width = KV_HEADS * HEAD_DIM
    dev_count = lax.axis_size("ctx")
    device = lax.axis_index("ctx")
    core = lax.axis_index("wsh")
    is_last = device == dev_count - 1
    state_rows = MHEADS * MHEAD_DIM // dev_count
    in_rows = mix_in.shape[0]
    out_rows = mix_out.shape[0]
    up = [(i, i + 1) for i in range(dev_count - 1)]
    down = [(j, i) for i, j in up]
    local_pos = token_positions(
        device, dev_count, row_count, jnp.arange(row_count, dtype=jnp.int32)
    )
    key_ids = jnp.arange(row_count * dev_count, dtype=jnp.int32)
    key_pos = token_positions(key_ids // row_count, dev_count, row_count, key_ids % row_count)
    mix_first = lax.all_gather(mix_in[:, INNER:], ("ctx", "wsh"), axis=0, tiled=True)
    half_gate = INNER // 2
    packed = jnp.concatenate(
        [
            jnp.concatenate([mlp_in[:, :FF], mlp_in[:, FF:]], axis=0),
            mix_out,
            mlp_out,
            jnp.concatenate([mix_in[:, :half_gate], mix_in[:, half_gate:INNER]], axis=0),
        ],
        axis=1,
    )
    normed1 = rms_scale(residual, norm_gain1).astype(jnp.bfloat16)
    tail_first = normed1[half_rows - rim_len : half_rows]
    tail_second = normed1[row_count - rim_len :]
    rim_first = lax.ppermute(tail_first, "ctx", up)
    rim_second = jnp.where(is_last, tail_first, lax.ppermute(tail_second, "ctx", down))
    spare = 16 - 2 * rim_len
    extended = jnp.concatenate(
        [normed1, rim_first, rim_second, jnp.zeros((spare, width), jnp.bfloat16)], axis=0
    )
    step_raw = jnp.dot(normed1, step_proj, preferred_element_type=jnp.float32)
    step_pair = step_raw.reshape(2, half_rows, MHEADS)
    early_steps = jax.nn.softplus(step_pair + step_bias[None, None, :])
    decays = jnp.exp(jnp.sum(early_steps * -jnp.exp(decay_log), axis=1))
    all_decays = exchange(
        jnp.broadcast_to(decays.reshape(1, 2 * MHEADS), (dev_count, 2 * MHEADS))
    ).reshape(dev_count, 2, MHEADS)
    span_decays = jnp.concatenate([all_decays[:, 0], all_decays[::-1, 1]], axis=0)
    row_head = (device * state_rows + jnp.arange(state_rows)) // MHEAD_DIM
    row_pick = (row_head[:, None] == jnp.arange(MHEADS)[None, :]).astype(jnp.float32)
    row_decays = jnp.dot(row_pick, span_decays.T, precision=HIGHEST)
    grad_top = out_grad[0]
    grad_top_b = grad_top.astype(jnp.bfloat16)
    extended, row_decays, packed = lax.optimization_barrier((extended, row_decays, packed))
    gathered = lax.all_gather(packed, ("ctx", "wsh"), axis=0)
    full_gate = gathered[:, :in_rows, :FF].reshape(width, FF)
    full_upw = gathered[:, in_rows:, :FF].reshape(width, FF)
    full_out = gathered[:, :, FF : FF + width].reshape(-1, width)
    full_down = gathered[:, :, FF + width : FF + 2 * width].reshape(-1, width)
    mix_gate = jnp.concatenate(
        [
            gathered[:, :in_rows, FF + 2 * width :].reshape(width, half_gate),
            gathered[:, in_rows:, FF + 2 * width :].reshape(width, half_gate),
        ],
        axis=1,
    )

    projected = jnp.dot(extended, mix_first, preferred_element_type=jnp.float32)
    conv_all = projected[:, :CONV_CH]
    attn_cols = projected[:row_count, CONV_CH:]
    q_raw = attn_cols[:, :q_width].reshape(row_count, ATT_HEADS, HEAD_DIM)
    k_raw = attn_cols[:, q_width : q_width + kv_width].reshape(row_count, KV_HEADS, HEAD_DIM)
    v_raw = attn_cols[:, q_width + kv_width :]
    padded = jnp.stack(
        [
            jnp.concatenate(
                [conv_all[row_count : row_count + rim_len], conv_all[:half_rows]], axis=0
            ),
            jnp.concatenate(
                [
                    conv_all[row_count + rim_len : row_count + 2 * rim_len],
                    conv_all[half_rows:row_count],
                ],
                axis=0,
            ),
        ]
    )

    def local_parts(padded_one, step_one):
        x_heads, step_size, decay_rate, b_proj, c_proj = mixer_inputs(
            padded_one, step_one, conv_weight, conv_bias, step_bias, decay_log
        )
        local_out, fresh_state, cumulative = span_local(
            x_heads, step_size, decay_rate, b_proj, c_proj, skip_gain
        )
        return (local_out, fresh_state, cumulative, c_proj)

    local_out, fresh_state, cumulative, c_proj = jax.vmap(local_parts)(padded, step_pair)
    queries = rope_apply(q_raw, local_pos).astype(jnp.bfloat16)
    keys_local = rope_apply(k_raw, local_pos).reshape(row_count, kv_width).astype(jnp.bfloat16)

    def to_slices(states):
        return (
            states.astype(jnp.bfloat16)
            .reshape(2, dev_count, state_rows, STATE)
            .transpose(1, 0, 2, 3)
            .reshape(dev_count, 2 * state_rows, STATE)
        )

    def from_slices(slices):
        return (
            slices.reshape(dev_count, 2, state_rows, STATE)
            .transpose(1, 0, 2, 3)
            .reshape(2, MHEADS, MHEAD_DIM, STATE)
            .astype(jnp.float32)
        )

    kv_local = jnp.concatenate([keys_local, v_raw.astype(jnp.bfloat16)], axis=0)
    arrived = exchange(
        jnp.concatenate(
            [
                to_slices(fresh_state),
                jnp.broadcast_to(kv_local[None], (dev_count, 2 * row_count, kv_width)),
            ],
            axis=1,
        )
    )
    fresh_all = arrived[:, : 2 * state_rows].reshape(dev_count, 2, state_rows, STATE)
    all_keys = arrived[:, 2 * state_rows : 2 * state_rows + row_count].reshape(-1, kv_width)
    all_values = arrived[:, 2 * state_rows + row_count :].reshape(-1, kv_width)
    entering = chain_scan(fresh_all, row_decays, False)
    entering, local_out = lax.optimization_barrier((entering, local_out))
    states = from_slices(exchange(entering.reshape(dev_count, 2 * state_rows, STATE)))
    ssm_out = (local_out + jax.vmap(carry_term)(c_proj, cumulative, states)).reshape(
        row_count, INNER
    )
    gate_z = jnp.dot(normed1, mix_gate, preferred_element_type=jnp.float32)
    mamba_part = gated_tail(ssm_out, gate_z, mamba_gain)
    attn_f32, log_total = attention_forward(queries, all_keys, all_values, local_pos, key_pos)
    joined = jnp.concatenate(
        [mamba_part.astype(jnp.bfloat16), attn_f32.astype(jnp.bfloat16)], axis=1
    )
    middle = residual + jnp.dot(joined, full_out, preferred_element_type=jnp.float32)
    normed2 = rms_scale(middle, norm_gain2).astype(jnp.bfloat16)
    gate_part = jnp.dot(normed2, full_gate, preferred_element_type=jnp.float32)
    up_part = jnp.dot(normed2, full_upw, preferred_element_type=jnp.float32)
    activated = (jax.nn.silu(gate_part) * up_part).astype(jnp.bfloat16)
    outputs = middle + jnp.dot(activated, full_down, preferred_element_type=jnp.float32)
    grad_act = jnp.dot(grad_top_b, full_down.T, preferred_element_type=jnp.float32)
    sigmoid_g = jax.nn.sigmoid(gate_part)
    grad_gate = (grad_act * up_part * sigmoid_g * (1.0 + gate_part * (1.0 - sigmoid_g))).astype(
        jnp.bfloat16
    )
    grad_up = (grad_act * gate_part * sigmoid_g).astype(jnp.bfloat16)
    grad_normed2 = jnp.dot(grad_gate, full_gate.T, preferred_element_type=jnp.float32) + jnp.dot(
        grad_up, full_upw.T, preferred_element_type=jnp.float32
    )
    unused_two, norm_back2 = jax.vjp(rms_scale, middle, norm_gain2)
    grad_mid_n, gain2_part = norm_back2(grad_normed2)
    grad_middle = grad_top + grad_mid_n
    grad_mid_b = grad_middle.astype(jnp.bfloat16)

    grad_joined = jnp.dot(grad_mid_b, full_out.T, preferred_element_type=jnp.float32)
    unused_tail, tail_back = jax.vjp(gated_tail, ssm_out, gate_z, mamba_gain)
    grad_ssm, grad_z, mgain_part = tail_back(grad_joined[:, :INNER])
    grad_z = grad_z.astype(jnp.bfloat16)

    def half_grad(values, grads):
        return jnp.dot(
            half_pair(values, dev_count, core),
            both_cores(grads),
            preferred_element_type=jnp.float32,
        ).astype(jnp.bfloat16)

    down_half = half_grad(activated, grad_top_b).reshape(dev_count, out_rows, width)
    up_half = half_grad(normed2, jnp.concatenate([grad_gate, grad_up], axis=1)).reshape(
        dev_count, in_rows, 2 * FF
    )
    mixout_half = half_grad(joined, grad_mid_b).reshape(dev_count, out_rows, width)
    gate_half = half_grad(normed1, grad_z).reshape(dev_count, in_rows, INNER)
    grad_pack = jnp.concatenate(
        [
            jnp.concatenate([up_half[:, :, :FF], up_half[:, :, FF:]], axis=1),
            mixout_half,
            down_half,
            jnp.concatenate([gate_half[:, :, :half_gate], gate_half[:, :, half_gate:]], axis=1),
        ],
        axis=2,
    ).reshape(dev_count * out_rows, -1)
    grad_joined, grad_ssm, grad_pack = lax.optimization_barrier((grad_joined, grad_ssm, grad_pack))
    pack_shard = lax.psum_scatter(grad_pack, "ctx", scatter_dimension=0, tiled=True)

    grad_pair = grad_ssm.reshape(2, half_rows, INNER)
    grad_heads = grad_ssm.reshape(2, half_rows, MHEADS, MHEAD_DIM)
    own_grads = jnp.einsum(
        "athp,atn->ahpn",
        grad_heads * jnp.exp(cumulative)[:, :, :, None],
        c_proj,
        precision=HIGHEST,
    )
    grad_attn = grad_joined[:, INNER:].astype(jnp.bfloat16)
    grad_q, grad_keys, grad_values = attention_backward(
        queries, all_keys, all_values, local_pos, key_pos, log_total, attn_f32, grad_attn
    )
    kv_grads = jnp.concatenate(
        [
            grad_keys.astype(jnp.bfloat16).reshape(dev_count, row_count, kv_width),
            grad_values.astype(jnp.bfloat16).reshape(dev_count, row_count, kv_width),
        ],
        axis=1,
    )
    returned = exchange(jnp.concatenate([to_slices(own_grads), kv_grads], axis=1))
    own_all = returned[:, : 2 * state_rows].reshape(dev_count, 2, state_rows, STATE)
    kv_back = jnp.sum(returned[:, 2 * state_rows :].astype(jnp.float32), axis=0)
    keys_back = kv_back[:row_count]
    values_back = kv_back[row_count:]
    leaving = chain_scan(own_all, row_decays, True)
    end_grads = from_slices(exchange(leaving.reshape(dev_count, 2 * state_rows, STATE)))
    unused_q, rope_back_q = jax.vjp(partial(rope_apply, positions=local_pos), q_raw)
    unused_k, rope_back_k = jax.vjp(partial(rope_apply, positions=local_pos), k_raw)
    (grad_q_raw,) = rope_back_q(grad_q)
    (grad_k_raw,) = rope_back_k(keys_back.reshape(row_count, KV_HEADS, HEAD_DIM))
    pair_mixer = jax.vmap(half_mixer, in_axes=(0, 0, None, None, None, None, None, 0))
    unused_m, mixer_back = jax.vjp(
        pair_mixer,
        padded,
        step_pair,
        conv_weight,
        conv_bias,
        step_bias,
        decay_log,
        skip_gain,
        states,
    )
    mixer_grads = mixer_back((grad_pair, end_grads))
    grad_padded = mixer_grads[0]
    grad_rims = grad_padded[:, :rim_len].reshape(2 * rim_len, CONV_CH)
    grad_conv = grad_padded[:, rim_len:].reshape(row_count, CONV_CH)
    grad_proj = jnp.concatenate(
        [
            jnp.concatenate(
                [
                    grad_conv,
                    grad_q_raw.reshape(row_count, q_width),
                    grad_k_raw.reshape(row_count, kv_width),
                    values_back,
                ],
                axis=1,
            ).astype(jnp.bfloat16),
            jnp.pad(
                grad_rims.astype(jnp.bfloat16), ((0, spare), (0, q_width + 2 * kv_width))
            ),
        ],
        axis=0,
    )
    in_half = half_grad(extended, grad_proj)
    in_half, pack_shard = lax.optimization_barrier((in_half, pack_shard))
    in_shard = lax.psum_scatter(in_half, "ctx", scatter_dimension=0, tiled=True)
    grad_step = mixer_grads[1].reshape(row_count, MHEADS).astype(jnp.bfloat16)
    step_grad = jnp.dot(grad_step.T, normed1, preferred_element_type=jnp.float32)
    grad_ext = jnp.dot(grad_proj, mix_first.T, preferred_element_type=jnp.float32)
    back_first = grad_ext[row_count : row_count + rim_len]
    back_second = grad_ext[row_count + rim_len : row_count + 2 * rim_len]
    add_first = lax.ppermute(back_first, "ctx", down) + jnp.where(is_last, back_second, 0.0)
    add_second = lax.ppermute(back_second, "ctx", up)
    fill = jnp.zeros((half_rows - rim_len, width), jnp.float32)
    grad_normed1 = (
        grad_ext[:row_count]
        + jnp.concatenate([fill, add_first, fill, add_second], axis=0)
        + jnp.dot(grad_step, step_proj.T, preferred_element_type=jnp.float32)
        + jnp.dot(grad_z, mix_gate.T, preferred_element_type=jnp.float32)
    )
    unused_one, norm_back1 = jax.vjp(rms_scale, residual, norm_gain1)
    grad_res_n, gain1_part = norm_back1(grad_normed1)
    input_grad = grad_middle + grad_res_n
    parts = (
        gain1_part,
        step_grad,
        mixer_grads[2],
        mixer_grads[3],
        mgain_part,
        gain2_part,
        mixer_grads[4],
        mixer_grads[5],
        mixer_grads[6],
    )
    flat = jnp.concatenate([part.reshape(-1) for part in parts])
    total_len = flat.shape[0]
    summed = butterfly_sum(jnp.pad(flat, (0, -total_len % 1024)).reshape(-1, 128)).reshape(-1)
    sums = []
    start = 0
    for part in parts:
        sums.append(summed[start : start + part.size].reshape(part.shape))
        start += part.size
    pack_f32 = pack_shard.astype(jnp.float32)
    up_shard = jnp.concatenate([pack_f32[:in_rows, :FF], pack_f32[in_rows:, :FF]], axis=1)
    return (
        outputs[None],
        input_grad[None],
        sums[0],
        jnp.concatenate(
            [
                pack_f32[:in_rows, FF + 2 * width :],
                pack_f32[in_rows:, FF + 2 * width :],
                in_shard.astype(jnp.float32),
            ],
            axis=1,
        ),
        sums[1].T,
        sums[2],
        sums[3],
        sums[6],
        sums[7],
        sums[8],
        sums[4],
        pack_f32[:, FF : FF + width],
        sums[5],
        up_shard,
        pack_f32[:, FF + width : FF + 2 * width],
    )


def solution(mesh):
    return jax.shard_map(
        body,
        mesh=mesh,
        in_specs=(
            P("wsh", "ctx", None),
            P(),
            P(("ctx", "wsh"), None),
            P(),
            P(),
            P(),
            P(),
            P(),
            P(),
            P(),
            P(("ctx", "wsh"), None),
            P(),
            P(("ctx", "wsh"), None),
            P(("ctx", "wsh"), None),
            P("wsh", "ctx", None),
        ),
        out_specs=(
            P("wsh", "ctx", None),
            P("wsh", "ctx", None),
            P(),
            P(("ctx", "wsh"), None),
            P(),
            P(),
            P(),
            P(),
            P(),
            P(),
            P(),
            P(("ctx", "wsh"), None),
            P(),
            P(("ctx", "wsh"), None),
            P(("ctx", "wsh"), None),
        ),
        check_vma=False,
    )
```

```python
from functools import partial

import jax
import jax.numpy as jnp
from jax import lax
from jax.experimental import pallas as pl
from jax.experimental.pallas import tpu as pltpu
from jax.sharding import PartitionSpec as P

MHEADS = 24
MHEAD_DIM = 64
STATE = 128
CONV = 4
ATT_HEADS = 8
KV_HEADS = 2
HEAD_DIM = 64
FF = 2048
INNER = 1536
CONV_CH = 1792


EPSILON = 1e-05
ROPE_BASE = 10000.0
NEG_LARGE = -1e30
HIGHEST = lax.Precision.HIGHEST


def rms_scale(values, gain_vec):
    return (
        values * lax.rsqrt(jnp.mean(values * values, axis=-1, keepdims=True) + EPSILON) * gain_vec
    )


def rope_apply(values, positions):
    half_dim = values.shape[-1] // 2
    frequency = ROPE_BASE ** (-jnp.arange(half_dim, dtype=jnp.float32) / half_dim)
    angles = positions.astype(jnp.float32)[:, None] * frequency[None, :]
    cosine = jnp.cos(angles)[:, None, :]
    sine_v = jnp.sin(angles)[:, None, :]
    first_part = values[..., :half_dim]
    second = values[..., half_dim:]
    return jnp.concatenate(
        [first_part * cosine - second * sine_v, second * cosine + first_part * sine_v], axis=-1
    )


def token_positions(device, dev_count, row_count, row_index):
    half_rows = row_count // 2
    return jnp.where(
        row_index < half_rows,
        device * half_rows + row_index,
        (2 * dev_count - 1 - device) * half_rows + row_index - half_rows,
    )


def conv_silu(padded, conv_weight, conv_bias):
    taps_count = conv_weight.shape[0]
    length = padded.shape[0] - taps_count + 1
    summed = conv_bias[None, :]
    for offset in range(taps_count):
        summed = summed + conv_weight[offset][None, :] * padded[offset : offset + length]
    return jax.nn.silu(summed)


def mixer_inputs(padded, step_raw, conv_weight, conv_bias, step_bias, decay_log):
    conv_act = conv_silu(padded, conv_weight, conv_bias)
    x_heads = conv_act[:, :INNER].reshape(conv_act.shape[0], MHEADS, MHEAD_DIM)
    b_proj = conv_act[:, INNER : INNER + STATE]
    c_proj = conv_act[:, INNER + STATE :]
    step_size = jax.nn.softplus(step_raw + step_bias[None, :])
    decay_rate = -jnp.exp(decay_log)
    return (x_heads, step_size, decay_rate, b_proj, c_proj)


def span_local(x_heads, step_size, decay_rate, b_proj, c_proj, skip_gain):
    length = x_heads.shape[0]
    causal = jnp.arange(length)[:, None] >= jnp.arange(length)[None, :]
    cumulative = jnp.cumsum(step_size * decay_rate[None, :], axis=0)
    log_gap = cumulative[:, None, :] - cumulative[None, :, :]
    causal3 = causal[:, :, None]
    decay_mat = jnp.where(causal3, jnp.exp(jnp.where(causal3, log_gap, 0.0)), 0.0)
    intersection = jnp.dot(c_proj, b_proj.T, precision=HIGHEST)
    weights = decay_mat * intersection[:, :, None] * step_size[None, :, :]
    intra_out = jnp.einsum("tsh,shp->thp", weights, x_heads, precision=HIGHEST)
    local_out = intra_out + skip_gain[None, :, None] * x_heads
    tail_weight = jnp.exp(cumulative[-1][None, :] - cumulative) * step_size
    weighted_x = tail_weight[:, :, None] * x_heads
    fresh_state = jnp.einsum("shp,sn->hpn", weighted_x, b_proj, precision=HIGHEST)
    return (local_out, fresh_state, cumulative)


def carry_term(c_proj, cumulative, state_in):
    return (
        jnp.einsum("tn,hpn->thp", c_proj, state_in, precision=HIGHEST)
        * jnp.exp(cumulative)[:, :, None]
    )


def half_mixer(padded, step_raw, conv_weight, conv_bias, step_bias, decay_log, skip_gain, state_in):
    x_heads, step_size, decay_rate, b_proj, c_proj = mixer_inputs(
        padded, step_raw, conv_weight, conv_bias, step_bias, decay_log
    )
    local_out, fresh_state, cumulative = span_local(
        x_heads, step_size, decay_rate, b_proj, c_proj, skip_gain
    )
    result = local_out + carry_term(c_proj, cumulative, state_in)
    new_state = jnp.exp(cumulative[-1])[:, None, None] * state_in + fresh_state
    return (result.reshape(result.shape[0], INNER), new_state)


def gated_tail(ssm_out, gate_z, mamba_gain):
    return rms_scale(ssm_out * jax.nn.silu(gate_z), mamba_gain)


def score_block(q_groups, query_pos, key_block, pos_block):
    raw_scores = jnp.einsum(
        "tkgd,skd->kgts", q_groups, key_block, preferred_element_type=jnp.float32
    ) * HEAD_DIM ** (-0.5)
    return jnp.where(
        pos_block[None, None, None, :] <= query_pos[None, None, :, None], raw_scores, NEG_LARGE
    )


def split_blocks(all_keys, all_values, key_pos):
    key_count = all_keys.shape[0]
    block_len = min(2048, key_count)
    blocks = key_count // block_len
    return (
        all_keys.reshape(blocks, block_len, KV_HEADS, HEAD_DIM),
        all_values.reshape(blocks, block_len, KV_HEADS, HEAD_DIM),
        key_pos.reshape(blocks, block_len),
    )


def attention_forward(queries, all_keys, all_values, query_pos, key_pos):
    row_count = queries.shape[0]
    group_size = ATT_HEADS // KV_HEADS
    q_groups = queries.reshape(row_count, KV_HEADS, group_size, HEAD_DIM)
    key_blocks, value_blocks, pos_blocks = split_blocks(all_keys, all_values, key_pos)

    def max_step(carried, block_item):
        running_max, running_sum = carried
        scores = score_block(q_groups, query_pos, block_item[0], block_item[1])
        new_max = jnp.maximum(running_max, jnp.max(scores, axis=-1))
        running_sum = running_sum * jnp.exp(running_max - new_max) + jnp.sum(
            jnp.exp(scores - new_max[..., None]), axis=-1
        )
        return ((new_max, running_sum), None)

    start_max = jnp.full((KV_HEADS, group_size, row_count), NEG_LARGE, jnp.float32)
    (final_max, final_sum), unused = lax.scan(
        max_step, (start_max, jnp.zeros_like(start_max)), (key_blocks, pos_blocks)
    )
    log_total = final_max + jnp.log(final_sum)

    def out_step(weighted, block_item):
        scores = score_block(q_groups, query_pos, block_item[0], block_item[2])
        attn_prob = jnp.exp(scores - log_total[..., None]).astype(jnp.bfloat16)
        return (
            weighted
            + jnp.einsum(
                "kgts,skd->tkgd", attn_prob, block_item[1], preferred_element_type=jnp.float32
            ),
            None,
        )

    start_out = jnp.zeros((row_count, KV_HEADS, group_size, HEAD_DIM), jnp.float32)
    weighted, unused_two = lax.scan(out_step, start_out, (key_blocks, value_blocks, pos_blocks))
    return (weighted.reshape(row_count, ATT_HEADS * HEAD_DIM), log_total)


def attention_backward(
    queries, all_keys, all_values, query_pos, key_pos, log_total, attn_f32, grad_attn
):
    row_count = queries.shape[0]
    key_count = all_keys.shape[0]
    group_size = ATT_HEADS // KV_HEADS
    score_scale = HEAD_DIM ** (-0.5)
    q_groups = queries.reshape(row_count, KV_HEADS, group_size, HEAD_DIM)
    d_groups = grad_attn.reshape(row_count, KV_HEADS, group_size, HEAD_DIM)
    row_dot = jnp.sum(
        (grad_attn.astype(jnp.float32) * attn_f32).reshape(
            row_count, KV_HEADS, group_size, HEAD_DIM
        ),
        axis=-1,
    )
    row_dot = jnp.transpose(row_dot, (1, 2, 0))
    key_blocks, value_blocks, pos_blocks = split_blocks(all_keys, all_values, key_pos)

    def grad_step(grad_q, block_item):
        key_block, value_block, pos_block = block_item
        scores = score_block(q_groups, query_pos, key_block, pos_block)
        attn_prob = jnp.exp(scores - log_total[..., None])
        grad_prob = jnp.einsum(
            "tkgd,skd->kgts", d_groups, value_block, preferred_element_type=jnp.float32
        )
        grad_score = (attn_prob * (grad_prob - row_dot[..., None])).astype(jnp.bfloat16)
        grad_vb = jnp.einsum(
            "kgts,tkgd->skd",
            attn_prob.astype(jnp.bfloat16),
            d_groups,
            preferred_element_type=jnp.float32,
        )
        grad_kb = (
            jnp.einsum("kgts,tkgd->skd", grad_score, q_groups, preferred_element_type=jnp.float32)
            * score_scale
        )
        grad_q = (
            grad_q
            + jnp.einsum(
                "kgts,skd->tkgd", grad_score, key_block, preferred_element_type=jnp.float32
            )
            * score_scale
        )
        return (grad_q, (grad_kb, grad_vb))

    start_q = jnp.zeros((row_count, KV_HEADS, group_size, HEAD_DIM), jnp.float32)
    grad_q, (grad_keys, grad_values) = lax.scan(
        grad_step, start_q, (key_blocks, value_blocks, pos_blocks)
    )
    return (
        grad_q.reshape(row_count, ATT_HEADS, HEAD_DIM),
        grad_keys.reshape(key_count, KV_HEADS * HEAD_DIM),
        grad_values.reshape(key_count, KV_HEADS * HEAD_DIM),
    )


def chain_scan(fresh, decays, reverse):
    dev_count, _, rows, width = fresh.shape
    spans = 2 * dev_count

    def kernel(fresh_ref, decay_ref, out_ref):
        state = jnp.zeros((rows, width), jnp.float32)
        for step in range(spans):
            at = spans - 1 - step if reverse else step
            dev, half = (at, 0) if at < dev_count else (spans - 1 - at, 1)
            out_ref[dev, half] = state.astype(jnp.bfloat16)
            state = decay_ref[:, at : at + 1] * state + fresh_ref[dev, half].astype(jnp.float32)

    return pl.pallas_call(
        kernel, out_shape=jax.ShapeDtypeStruct(fresh.shape, jnp.bfloat16), name="chain_scan"
    )(fresh, decays)


TILE = 256


def ring_order(dev_count):
    if dev_count != 16:
        return list(range(dev_count))
    order = []
    for k, plane in enumerate((0, 1, 3, 2)):
        line = range(4) if k % 2 == 0 else range(3, -1, -1)
        order += [4 * z + plane for z in line]
    return order


def scatter_ring(array):
    order = ring_order(lax.axis_size("ctx"))
    return lax.psum_scatter(
        array, "ctx", scatter_dimension=0, tiled=True, axis_index_groups=[order]
    )


def half_grads(core, dev_count, block_rows, segments):
    order = ring_order(dev_count)
    operands, specs, plan, scratch = [], [], [], []
    start = 0
    for (x_own, x_sib, x_col, x_width), pieces, columns in segments:
        tokens = x_own.shape[0]
        rows = x_width // (2 * dev_count)
        entry = {"rows": rows, "tokens": tokens, "width": x_width, "x": len(operands)}
        for arr in (x_own, x_sib):
            operands.append(arr)
            specs.append(pl.BlockSpec((tokens, x_width), lambda j, c, at=x_col // x_width: (0, at)))
        entry["dy"] = []
        count = columns // TILE
        for d_own, d_sib, d_col in pieces:
            entry["dy"].append(len(operands))
            for arr in (d_own, d_sib):
                operands.append(arr)
                specs.append(
                    pl.BlockSpec(
                        (tokens, TILE),
                        lambda j, c, base=d_col // TILE, first=start, last=count - 1: (
                            0,
                            base + jnp.clip(j - first, 0, last),
                        ),
                    )
                )
        entry["start"], entry["stop"] = start, start + count
        entry["scratch"] = len(scratch)
        scratch += [
            pltpu.VMEM((x_width, 2 * tokens), jnp.bfloat16),
            pltpu.VMEM((x_width // 2, 2 * tokens), jnp.bfloat16),
        ]
        start += count
        plan.append(entry)
    total = start

    def kernel(core_ref, *refs):
        ins = refs[: len(operands)]
        out_ref = refs[len(operands)]
        spare = refs[len(operands) + 1 :]
        step = pl.program_id(0)
        half = core_ref[0]
        for entry in plan:
            whole, picked = spare[entry["scratch"]], spare[entry["scratch"] + 1]
            rows = entry["rows"]

            @pl.when(step == entry["start"])
            def _():
                both = jnp.concatenate([ins[entry["x"]][...], ins[entry["x"] + 1][...]], axis=0)
                whole[...] = both.T
                for k, dev in enumerate(order):
                    at = pl.multiple_of(2 * dev * rows + half * rows, rows)
                    picked[k * rows : (k + 1) * rows, :] = whole[pl.ds(at, rows), :]

            @pl.when((step >= entry["start"]) & (step < entry["stop"]))
            def _():
                for slot, at in enumerate(entry["dy"]):
                    grads = jnp.concatenate([ins[at][...], ins[at + 1][...]], axis=0)
                    made = jnp.dot(picked[...], grads, preferred_element_type=jnp.float32)
                    out_ref[:, slot * rows : (slot + 1) * rows, :] = made.astype(
                        jnp.bfloat16
                    ).reshape(dev_count, rows, TILE)

    return pl.pallas_call(
        kernel,
        out_shape=jax.ShapeDtypeStruct((dev_count, block_rows, total * TILE), jnp.bfloat16),
        grid_spec=pltpu.PrefetchScalarGridSpec(
            num_scalar_prefetch=1,
            grid=(total,),
            in_specs=specs,
            out_specs=pl.BlockSpec((dev_count, block_rows, TILE), lambda j, c: (0, 0, j)),
            scratch_shapes=scratch,
        ),
        compiler_params=pltpu.CompilerParams(dimension_semantics=("arbitrary",)),
        name="half_grads",
    )(core.reshape(1), *operands)


def dense_core(joined, residual, grad_top, norm_gain2, gathered):
    tokens, width = residual.shape
    devs, block, _ = gathered.shape
    mixed = devs * block
    in_rows = block // 2
    down_devs = TILE // block
    tiles = FF // TILE
    bundle_width = 3 * FF + 2 * width
    transposed = (((1,), (1,)), ((), ()))

    def kernel(
        joined_ref,
        res_ref,
        top_ref,
        gain_ref,
        out_w_ref,
        in_w_ref,
        down_ref,
        outputs_ref,
        grad_mid_ref,
        grad_joined_ref,
        gain_grad_ref,
        bundle_ref,
        middle,
        total,
        grad_norm,
    ):
        step = pl.program_id(0)

        @pl.when(step == 0)
        def _():
            weights = out_w_ref[...].reshape(mixed, width)
            mid = res_ref[...] + jnp.dot(
                joined_ref[...], weights, preferred_element_type=jnp.float32
            )
            middle[...] = mid
            scale = lax.rsqrt(jnp.mean(mid * mid, axis=-1, keepdims=True) + EPSILON)
            bundle_ref[:, 3 * FF : 3 * FF + width] = (mid * scale * gain_ref[...]).astype(
                jnp.bfloat16
            )
            total[...] = jnp.zeros_like(total)
            grad_norm[...] = jnp.zeros_like(grad_norm)

        normed = bundle_ref[:, 3 * FF : 3 * FF + width]
        w_gate = in_w_ref[:, :in_rows, :].reshape(width, TILE)
        w_up = in_w_ref[:, in_rows:, :].reshape(width, TILE)
        w_down = down_ref[...].reshape(TILE, width)
        gate = jnp.dot(normed, w_gate, preferred_element_type=jnp.float32)
        up_part = jnp.dot(normed, w_up, preferred_element_type=jnp.float32)
        sig = jax.nn.sigmoid(gate)
        silu = gate * sig
        activated = (silu * up_part).astype(jnp.bfloat16)
        total[...] += jnp.dot(activated, w_down, preferred_element_type=jnp.float32)
        grad_act = lax.dot_general(
            top_ref[...].astype(jnp.bfloat16), w_down, transposed, preferred_element_type=jnp.float32
        )
        grad_gate = (grad_act * up_part * sig * (1.0 + gate * (1.0 - sig))).astype(jnp.bfloat16)
        grad_up = (grad_act * silu).astype(jnp.bfloat16)
        grad_norm[...] += lax.dot_general(
            grad_gate, w_gate, transposed, preferred_element_type=jnp.float32
        ) + lax.dot_general(grad_up, w_up, transposed, preferred_element_type=jnp.float32)
        at = pl.multiple_of(step * TILE, TILE)
        bundle_ref[:, pl.ds(at, TILE)] = activated
        bundle_ref[:, pl.ds(FF + at, TILE)] = grad_gate
        bundle_ref[:, pl.ds(2 * FF + at, TILE)] = grad_up

        @pl.when(step == tiles - 1)
        def _():
            mid = middle[...]
            outputs_ref[...] = mid + total[...]
            scale = lax.rsqrt(jnp.mean(mid * mid, axis=-1, keepdims=True) + EPSILON)
            unit = mid * scale
            grads = grad_norm[...]
            gain_grad_ref[...] = jnp.sum(grads * unit, axis=0, keepdims=True)
            scaled = grads * gain_ref[...]
            grad_mid = top_ref[...] + scale * (
                scaled - unit * jnp.mean(scaled * unit, axis=-1, keepdims=True)
            )
            grad_mid_ref[...] = grad_mid
            grad_mid_b = grad_mid.astype(jnp.bfloat16)
            bundle_ref[:, 3 * FF + width :] = grad_mid_b
            grad_joined_ref[...] = lax.dot_general(
                grad_mid_b,
                out_w_ref[...].reshape(mixed, width),
                transposed,
                preferred_element_type=jnp.float32,
            )

    def whole(shape):
        return pl.BlockSpec(shape, lambda j: (0,) * len(shape))

    return pl.pallas_call(
        kernel,
        grid=(tiles,),
        out_shape=(
            jax.ShapeDtypeStruct((tokens, width), jnp.float32),
            jax.ShapeDtypeStruct((tokens, width), jnp.float32),
            jax.ShapeDtypeStruct((tokens, mixed), jnp.float32),
            jax.ShapeDtypeStruct((1, width), jnp.float32),
            jax.ShapeDtypeStruct((tokens, bundle_width), jnp.bfloat16),
        ),
        in_specs=[
            whole((tokens, mixed)),
            whole((tokens, width)),
            whole((tokens, width)),
            whole((1, width)),
            pl.BlockSpec((devs, block, width), lambda j: (0, 0, FF // width)),
            pl.BlockSpec((devs, block, TILE), lambda j: (0, 0, j)),
            pl.BlockSpec((down_devs, block, width), lambda j: (j, 0, FF // width + 1)),
        ],
        out_specs=(
            whole((tokens, width)),
            whole((tokens, width)),
            whole((tokens, mixed)),
            whole((1, width)),
            whole((tokens, bundle_width)),
        ),
        scratch_shapes=[pltpu.VMEM((tokens, width), jnp.float32)] * 3,
        compiler_params=pltpu.CompilerParams(
            dimension_semantics=("arbitrary",), vmem_limit_bytes=56 << 20
        ),
        name="dense_core",
    )(joined, residual, grad_top, norm_gain2.reshape(1, width), gathered, gathered, gathered)


def swap(array):
    return lax.ppermute(array, "wsh", [(0, 1), (1, 0)])


def half_pair(values, dev_count, core):
    tokens, width = values.shape
    blocks = values.T.reshape(dev_count, 2, width // (2 * dev_count), tokens)
    own = lax.dynamic_index_in_dim(blocks, core, 1, keepdims=False)
    other = lax.dynamic_index_in_dim(blocks, 1 - core, 1, keepdims=False)
    joined = jnp.concatenate([own, swap(other)], axis=-1)
    return joined.reshape(width // 2, 2 * tokens)


def both_cores(values):
    return jnp.concatenate([values, swap(values)], axis=0)


def exchange(array):
    return lax.all_to_all(array, "ctx", 0, 0, tiled=True)


def butterfly_sum(array):
    array = array + swap(array)
    size = lax.axis_size("ctx")
    step = 1
    while step < size:
        array = array + lax.ppermute(array, "ctx", [(i, i ^ step) for i in range(size)])
        step *= 2
    return array


def body(
    inputs,
    norm_gain1,
    mix_in,
    step_proj,
    conv_weight,
    conv_bias,
    step_bias,
    decay_log,
    skip_gain,
    mamba_gain,
    mix_out,
    norm_gain2,
    mlp_in,
    mlp_out,
    out_grad,
):
    residual = inputs[0]
    row_count, width = residual.shape
    half_rows = row_count // 2
    rim_len = CONV - 1
    q_width = ATT_HEADS * HEAD_DIM
    kv_width = KV_HEADS * HEAD_DIM
    dev_count = lax.axis_size("ctx")
    device = lax.axis_index("ctx")
    core = lax.axis_index("wsh")
    is_last = device == dev_count - 1
    state_rows = MHEADS * MHEAD_DIM // dev_count
    in_rows = mix_in.shape[0]
    out_rows = mix_out.shape[0]
    up = [(i, i + 1) for i in range(dev_count - 1)]
    down = [(j, i) for i, j in up]
    local_pos = token_positions(
        device, dev_count, row_count, jnp.arange(row_count, dtype=jnp.int32)
    )
    key_ids = jnp.arange(row_count * dev_count, dtype=jnp.int32)
    key_pos = token_positions(key_ids // row_count, dev_count, row_count, key_ids % row_count)
    mix_first = lax.all_gather(mix_in[:, INNER:], ("ctx", "wsh"), axis=0, tiled=True)
    half_gate = INNER // 2
    packed = jnp.concatenate(
        [
            jnp.concatenate([mlp_in[:, :FF], mlp_in[:, FF:]], axis=0),
            mix_out,
            mlp_out,
            jnp.concatenate([mix_in[:, :half_gate], mix_in[:, half_gate:INNER]], axis=0),
        ],
        axis=1,
    )
    normed1 = rms_scale(residual, norm_gain1).astype(jnp.bfloat16)
    tail_first = normed1[half_rows - rim_len : half_rows]
    tail_second = normed1[row_count - rim_len :]
    rim_first = lax.ppermute(tail_first, "ctx", up)
    rim_second = jnp.where(is_last, tail_first, lax.ppermute(tail_second, "ctx", down))
    spare = 16 - 2 * rim_len
    extended = jnp.concatenate(
        [normed1, rim_first, rim_second, jnp.zeros((spare, width), jnp.bfloat16)], axis=0
    )
    step_raw = jnp.dot(normed1, step_proj, preferred_element_type=jnp.float32)
    step_pair = step_raw.reshape(2, half_rows, MHEADS)
    early_steps = jax.nn.softplus(step_pair + step_bias[None, None, :])
    decays = jnp.exp(jnp.sum(early_steps * -jnp.exp(decay_log), axis=1))
    all_decays = exchange(
        jnp.broadcast_to(decays.reshape(1, 2 * MHEADS), (dev_count, 2 * MHEADS))
    ).reshape(dev_count, 2, MHEADS)
    span_decays = jnp.concatenate([all_decays[:, 0], all_decays[::-1, 1]], axis=0)
    row_head = (device * state_rows + jnp.arange(state_rows)) // MHEAD_DIM
    row_pick = (row_head[:, None] == jnp.arange(MHEADS)[None, :]).astype(jnp.float32)
    row_decays = jnp.dot(row_pick, span_decays.T, precision=HIGHEST)
    grad_top = out_grad[0]
    grad_top_b = grad_top.astype(jnp.bfloat16)
    extended, row_decays, packed = lax.optimization_barrier((extended, row_decays, packed))
    gathered = lax.all_gather(packed, ("ctx", "wsh"), axis=0)
    if out_rows < 64:
        group = 64 // out_rows
        gathered = jnp.concatenate(
            [
                jnp.concatenate(
                    [
                        part.reshape(-1, group * in_rows, part.shape[-1])
                        for part in (piece[:, :in_rows], piece[:, in_rows:])
                    ],
                    axis=1,
                )
                if split
                else piece.reshape(-1, group * out_rows, piece.shape[-1])
                for piece, split in (
                    (gathered[:, :, :FF], True),
                    (gathered[:, :, FF : FF + 2 * width], False),
                    (gathered[:, :, FF + 2 * width :], True),
                )
            ],
            axis=2,
        )
    split_row = gathered.shape[1] // 2
    mix_gate = jnp.concatenate(
        [
            gathered[:, :split_row, FF + 2 * width :].reshape(width, half_gate),
            gathered[:, split_row:, FF + 2 * width :].reshape(width, half_gate),
        ],
        axis=1,
    )

    projected = jnp.dot(extended, mix_first, preferred_element_type=jnp.float32)
    conv_all = projected[:, :CONV_CH]
    attn_cols = projected[:row_count, CONV_CH:]
    q_raw = attn_cols[:, :q_width].reshape(row_count, ATT_HEADS, HEAD_DIM)
    k_raw = attn_cols[:, q_width : q_width + kv_width].reshape(row_count, KV_HEADS, HEAD_DIM)
    v_raw = attn_cols[:, q_width + kv_width :]
    padded = jnp.stack(
        [
            jnp.concatenate(
                [conv_all[row_count : row_count + rim_len], conv_all[:half_rows]], axis=0
            ),
            jnp.concatenate(
                [
                    conv_all[row_count + rim_len : row_count + 2 * rim_len],
                    conv_all[half_rows:row_count],
                ],
                axis=0,
            ),
        ]
    )

    def local_parts(padded_one, step_one):
        x_heads, step_size, decay_rate, b_proj, c_proj = mixer_inputs(
            padded_one, step_one, conv_weight, conv_bias, step_bias, decay_log
        )
        local_out, fresh_state, cumulative = span_local(
            x_heads, step_size, decay_rate, b_proj, c_proj, skip_gain
        )
        return (local_out, fresh_state, cumulative, c_proj)

    local_out, fresh_state, cumulative, c_proj = jax.vmap(local_parts)(padded, step_pair)
    queries = rope_apply(q_raw, local_pos).astype(jnp.bfloat16)
    keys_local = rope_apply(k_raw, local_pos).reshape(row_count, kv_width).astype(jnp.bfloat16)

    def to_slices(states):
        return (
            states.astype(jnp.bfloat16)
            .reshape(2, dev_count, state_rows, STATE)
            .transpose(1, 0, 2, 3)
            .reshape(dev_count, 2 * state_rows, STATE)
        )

    def from_slices(slices):
        return (
            slices.reshape(dev_count, 2, state_rows, STATE)
            .transpose(1, 0, 2, 3)
            .reshape(2, MHEADS, MHEAD_DIM, STATE)
            .astype(jnp.float32)
        )

    kv_local = jnp.concatenate([keys_local, v_raw.astype(jnp.bfloat16)], axis=0)
    arrived = exchange(
        jnp.concatenate(
            [
                to_slices(fresh_state),
                jnp.broadcast_to(kv_local[None], (dev_count, 2 * row_count, kv_width)),
            ],
            axis=1,
        )
    )
    fresh_all = arrived[:, : 2 * state_rows].reshape(dev_count, 2, state_rows, STATE)
    all_keys = arrived[:, 2 * state_rows : 2 * state_rows + row_count].reshape(-1, kv_width)
    all_values = arrived[:, 2 * state_rows + row_count :].reshape(-1, kv_width)
    entering = chain_scan(fresh_all, row_decays, False)
    entering, local_out = lax.optimization_barrier((entering, local_out))
    states = from_slices(exchange(entering.reshape(dev_count, 2 * state_rows, STATE)))
    ssm_out = (local_out + jax.vmap(carry_term)(c_proj, cumulative, states)).reshape(
        row_count, INNER
    )
    gate_z = jnp.dot(normed1, mix_gate, preferred_element_type=jnp.float32)
    mamba_part = gated_tail(ssm_out, gate_z, mamba_gain)
    attn_f32, log_total = attention_forward(queries, all_keys, all_values, local_pos, key_pos)
    joined = jnp.concatenate(
        [mamba_part.astype(jnp.bfloat16), attn_f32.astype(jnp.bfloat16)], axis=1
    )
    outputs, grad_middle, grad_joined, gain2_part, bundle = dense_core(
        joined, residual, grad_top, norm_gain2, gathered
    )
    unused_tail, tail_back = jax.vjp(gated_tail, ssm_out, gate_z, mamba_gain)
    grad_ssm, grad_z, mgain_part = tail_back(grad_joined[:, :INNER])
    grad_z = grad_z.astype(jnp.bfloat16)

    def half_grad(values, grads):
        order = ring_order(dev_count)
        made = jnp.dot(
            half_pair(values, dev_count, core),
            both_cores(grads),
            preferred_element_type=jnp.float32,
        ).astype(jnp.bfloat16)
        made = made.reshape(dev_count, -1, grads.shape[1])
        return made[jnp.array(order)] if order != list(range(dev_count)) else made

    if in_rows % 16 == 0:
        bundle_s = swap(bundle)
        norm1_s, joined_s, top_s, grad_z_s = swap(normed1), swap(joined), swap(grad_top_b), swap(grad_z)
        mid_at = 3 * FF + width
        grad_pack = half_grads(
            core,
            dev_count,
            out_rows,
            (
                (
                    (bundle, bundle_s, 3 * FF, width),
                    ((bundle, bundle_s, FF), (bundle, bundle_s, 2 * FF)),
                    FF,
                ),
                ((joined, joined_s, 0, joined.shape[1]), ((bundle, bundle_s, mid_at),), width),
                ((bundle, bundle_s, 0, FF), ((grad_top_b, top_s, 0),), width),
                (
                    (normed1, norm1_s, 0, width),
                    ((grad_z, grad_z_s, 0), (grad_z, grad_z_s, half_gate)),
                    half_gate,
                ),
            ),
        )
    else:
        up_half = half_grad(bundle[:, 3 * FF : 3 * FF + width], bundle[:, FF : 3 * FF])
        gate_half = half_grad(normed1, grad_z)
        grad_pack = jnp.concatenate(
            [
                jnp.concatenate([up_half[:, :, :FF], up_half[:, :, FF:]], axis=1),
                half_grad(joined, bundle[:, 3 * FF + width :]),
                half_grad(bundle[:, :FF], grad_top_b),
                jnp.concatenate(
                    [gate_half[:, :, :half_gate], gate_half[:, :, half_gate:]], axis=1
                ),
            ],
            axis=2,
        )
    grad_pack = grad_pack.reshape(dev_count * out_rows, -1)
    grad_joined, grad_ssm, grad_pack = lax.optimization_barrier((grad_joined, grad_ssm, grad_pack))
    pack_shard = scatter_ring(grad_pack)
    grad_pair = grad_ssm.reshape(2, half_rows, INNER)
    grad_heads = grad_ssm.reshape(2, half_rows, MHEADS, MHEAD_DIM)
    own_grads = jnp.einsum(
        "athp,atn->ahpn",
        grad_heads * jnp.exp(cumulative)[:, :, :, None],
        c_proj,
        precision=HIGHEST,
    )
    grad_attn = grad_joined[:, INNER:].astype(jnp.bfloat16)
    grad_q, grad_keys, grad_values = attention_backward(
        queries, all_keys, all_values, local_pos, key_pos, log_total, attn_f32, grad_attn
    )
    kv_grads = jnp.concatenate(
        [
            grad_keys.astype(jnp.bfloat16).reshape(dev_count, row_count, kv_width),
            grad_values.astype(jnp.bfloat16).reshape(dev_count, row_count, kv_width),
        ],
        axis=1,
    )
    returned = exchange(jnp.concatenate([to_slices(own_grads), kv_grads], axis=1))
    own_all = returned[:, : 2 * state_rows].reshape(dev_count, 2, state_rows, STATE)
    kv_back = jnp.sum(returned[:, 2 * state_rows :].astype(jnp.float32), axis=0)
    keys_back = kv_back[:row_count]
    values_back = kv_back[row_count:]
    leaving = chain_scan(own_all, row_decays, True)
    end_grads = from_slices(exchange(leaving.reshape(dev_count, 2 * state_rows, STATE)))
    unused_q, rope_back_q = jax.vjp(partial(rope_apply, positions=local_pos), q_raw)
    unused_k, rope_back_k = jax.vjp(partial(rope_apply, positions=local_pos), k_raw)
    (grad_q_raw,) = rope_back_q(grad_q)
    (grad_k_raw,) = rope_back_k(keys_back.reshape(row_count, KV_HEADS, HEAD_DIM))
    pair_mixer = jax.vmap(half_mixer, in_axes=(0, 0, None, None, None, None, None, 0))
    unused_m, mixer_back = jax.vjp(
        pair_mixer,
        padded,
        step_pair,
        conv_weight,
        conv_bias,
        step_bias,
        decay_log,
        skip_gain,
        states,
    )
    mixer_grads = mixer_back((grad_pair, end_grads))
    grad_padded = mixer_grads[0]
    grad_rims = grad_padded[:, :rim_len].reshape(2 * rim_len, CONV_CH)
    grad_conv = grad_padded[:, rim_len:].reshape(row_count, CONV_CH)
    grad_proj = jnp.concatenate(
        [
            jnp.concatenate(
                [
                    grad_conv,
                    grad_q_raw.reshape(row_count, q_width),
                    grad_k_raw.reshape(row_count, kv_width),
                    values_back,
                ],
                axis=1,
            ).astype(jnp.bfloat16),
            jnp.pad(
                grad_rims.astype(jnp.bfloat16), ((0, spare), (0, q_width + 2 * kv_width))
            ),
        ],
        axis=0,
    )
    if in_rows % 16 == 0:
        in_half = half_grads(
            core,
            dev_count,
            in_rows,
            (
                (
                    (extended, swap(extended), 0, width),
                    ((grad_proj, swap(grad_proj), 0),),
                    grad_proj.shape[1],
                ),
            ),
        )
    else:
        in_half = half_grad(extended, grad_proj)
    in_half = in_half.reshape(dev_count * in_rows, -1)
    in_half, pack_shard = lax.optimization_barrier((in_half, pack_shard))
    in_shard = scatter_ring(in_half)
    grad_step = mixer_grads[1].reshape(row_count, MHEADS).astype(jnp.bfloat16)
    step_grad = jnp.dot(grad_step.T, normed1, preferred_element_type=jnp.float32)
    grad_ext = jnp.dot(grad_proj, mix_first.T, preferred_element_type=jnp.float32)
    back_first = grad_ext[row_count : row_count + rim_len]
    back_second = grad_ext[row_count + rim_len : row_count + 2 * rim_len]
    add_first = lax.ppermute(back_first, "ctx", down) + jnp.where(is_last, back_second, 0.0)
    add_second = lax.ppermute(back_second, "ctx", up)
    fill = jnp.zeros((half_rows - rim_len, width), jnp.float32)
    grad_normed1 = (
        grad_ext[:row_count]
        + jnp.concatenate([fill, add_first, fill, add_second], axis=0)
        + jnp.dot(grad_step, step_proj.T, preferred_element_type=jnp.float32)
        + jnp.dot(grad_z, mix_gate.T, preferred_element_type=jnp.float32)
    )
    unused_one, norm_back1 = jax.vjp(rms_scale, residual, norm_gain1)
    grad_res_n, gain1_part = norm_back1(grad_normed1)
    input_grad = grad_middle + grad_res_n
    parts = (
        gain1_part,
        step_grad,
        mixer_grads[2],
        mixer_grads[3],
        mgain_part,
        gain2_part,
        mixer_grads[4],
        mixer_grads[5],
        mixer_grads[6],
    )
    flat = jnp.concatenate([part.reshape(-1) for part in parts])
    total_len = flat.shape[0]
    summed = butterfly_sum(jnp.pad(flat, (0, -total_len % 1024)).reshape(-1, 128)).reshape(-1)
    sums = []
    start = 0
    for part in parts:
        sums.append(summed[start : start + part.size].reshape(part.shape))
        start += part.size
    pack_f32 = pack_shard.astype(jnp.float32)
    up_shard = jnp.concatenate([pack_f32[:in_rows, :FF], pack_f32[in_rows:, :FF]], axis=1)
    return (
        outputs[None],
        input_grad[None],
        sums[0],
        jnp.concatenate(
            [
                pack_f32[:in_rows, FF + 2 * width :],
                pack_f32[in_rows:, FF + 2 * width :],
                in_shard.astype(jnp.float32),
            ],
            axis=1,
        ),
        sums[1].T,
        sums[2],
        sums[3],
        sums[6],
        sums[7],
        sums[8],
        sums[4],
        pack_f32[:, FF : FF + width],
        sums[5].reshape(-1),
        up_shard,
        pack_f32[:, FF + width : FF + 2 * width],
    )


def solution(mesh):
    return jax.shard_map(
        body,
        mesh=mesh,
        in_specs=(
            P("wsh", "ctx", None),
            P(),
            P(("ctx", "wsh"), None),
            P(),
            P(),
            P(),
            P(),
            P(),
            P(),
            P(),
            P(("ctx", "wsh"), None),
            P(),
            P(("ctx", "wsh"), None),
            P(("ctx", "wsh"), None),
            P("wsh", "ctx", None),
        ),
        out_specs=(
            P("wsh", "ctx", None),
            P("wsh", "ctx", None),
            P(),
            P(("ctx", "wsh"), None),
            P(),
            P(),
            P(),
            P(),
            P(),
            P(),
            P(),
            P(("ctx", "wsh"), None),
            P(),
            P(("ctx", "wsh"), None),
            P(("ctx", "wsh"), None),
        ),
        check_vma=False,
    )
```

```python
from functools import partial

import jax
import jax.numpy as jnp
from jax import lax
from jax.experimental import pallas as pl
from jax.experimental.pallas import tpu as pltpu
from jax.sharding import PartitionSpec as P

MHEADS = 24
MHEAD_DIM = 64
STATE = 128
CONV = 4
ATT_HEADS = 8
KV_HEADS = 2
HEAD_DIM = 64
FF = 2048
INNER = 1536
CONV_CH = 1792


EPSILON = 1e-05
ROPE_BASE = 10000.0
NEG_LARGE = -1e30
HIGHEST = lax.Precision.HIGHEST


def rms_scale(values, gain_vec):
    return (
        values * lax.rsqrt(jnp.mean(values * values, axis=-1, keepdims=True) + EPSILON) * gain_vec
    )


def rope_apply(values, positions):
    half_dim = values.shape[-1] // 2
    frequency = ROPE_BASE ** (-jnp.arange(half_dim, dtype=jnp.float32) / half_dim)
    angles = positions.astype(jnp.float32)[:, None] * frequency[None, :]
    cosine = jnp.cos(angles)[:, None, :]
    sine_v = jnp.sin(angles)[:, None, :]
    first_part = values[..., :half_dim]
    second = values[..., half_dim:]
    return jnp.concatenate(
        [first_part * cosine - second * sine_v, second * cosine + first_part * sine_v], axis=-1
    )


def token_positions(device, dev_count, row_count, row_index):
    half_rows = row_count // 2
    return jnp.where(
        row_index < half_rows,
        device * half_rows + row_index,
        (2 * dev_count - 1 - device) * half_rows + row_index - half_rows,
    )


def conv_silu(padded, conv_weight, conv_bias):
    taps_count = conv_weight.shape[0]
    length = padded.shape[0] - taps_count + 1
    summed = conv_bias[None, :]
    for offset in range(taps_count):
        summed = summed + conv_weight[offset][None, :] * padded[offset : offset + length]
    return jax.nn.silu(summed)


def mixer_inputs(padded, step_raw, conv_weight, conv_bias, step_bias, decay_log):
    conv_act = conv_silu(padded, conv_weight, conv_bias)
    x_heads = conv_act[:, :INNER].reshape(conv_act.shape[0], MHEADS, MHEAD_DIM)
    b_proj = conv_act[:, INNER : INNER + STATE]
    c_proj = conv_act[:, INNER + STATE :]
    step_size = jax.nn.softplus(step_raw + step_bias[None, :])
    decay_rate = -jnp.exp(decay_log)
    return (x_heads, step_size, decay_rate, b_proj, c_proj)


def span_local(x_heads, step_size, decay_rate, b_proj, c_proj, skip_gain):
    length = x_heads.shape[0]
    causal = jnp.arange(length)[:, None] >= jnp.arange(length)[None, :]
    cumulative = jnp.cumsum(step_size * decay_rate[None, :], axis=0)
    log_gap = cumulative[:, None, :] - cumulative[None, :, :]
    causal3 = causal[:, :, None]
    decay_mat = jnp.where(causal3, jnp.exp(jnp.where(causal3, log_gap, 0.0)), 0.0)
    intersection = jnp.dot(c_proj, b_proj.T, precision=HIGHEST)
    weights = decay_mat * intersection[:, :, None] * step_size[None, :, :]
    intra_out = jnp.einsum("tsh,shp->thp", weights, x_heads, precision=HIGHEST)
    local_out = intra_out + skip_gain[None, :, None] * x_heads
    tail_weight = jnp.exp(cumulative[-1][None, :] - cumulative) * step_size
    weighted_x = tail_weight[:, :, None] * x_heads
    fresh_state = jnp.einsum("shp,sn->hpn", weighted_x, b_proj, precision=HIGHEST)
    return (local_out, fresh_state, cumulative)


def carry_term(c_proj, cumulative, state_in):
    return (
        jnp.einsum("tn,hpn->thp", c_proj, state_in, precision=HIGHEST)
        * jnp.exp(cumulative)[:, :, None]
    )


def half_mixer(padded, step_raw, conv_weight, conv_bias, step_bias, decay_log, skip_gain, state_in):
    x_heads, step_size, decay_rate, b_proj, c_proj = mixer_inputs(
        padded, step_raw, conv_weight, conv_bias, step_bias, decay_log
    )
    local_out, fresh_state, cumulative = span_local(
        x_heads, step_size, decay_rate, b_proj, c_proj, skip_gain
    )
    result = local_out + carry_term(c_proj, cumulative, state_in)
    new_state = jnp.exp(cumulative[-1])[:, None, None] * state_in + fresh_state
    return (result.reshape(result.shape[0], INNER), new_state)


def gated_tail(ssm_out, gate_z, mamba_gain):
    return rms_scale(ssm_out * jax.nn.silu(gate_z), mamba_gain)


def score_block(q_groups, query_pos, key_block, pos_block):
    raw_scores = jnp.einsum(
        "tkgd,skd->kgts", q_groups, key_block, preferred_element_type=jnp.float32
    ) * HEAD_DIM ** (-0.5)
    return jnp.where(
        pos_block[None, None, None, :] <= query_pos[None, None, :, None], raw_scores, NEG_LARGE
    )


def split_blocks(all_keys, all_values, key_pos):
    key_count = all_keys.shape[0]
    block_len = min(2048, key_count)
    blocks = key_count // block_len
    return (
        all_keys.reshape(blocks, block_len, KV_HEADS, HEAD_DIM),
        all_values.reshape(blocks, block_len, KV_HEADS, HEAD_DIM),
        key_pos.reshape(blocks, block_len),
    )


def attention_forward(queries, all_keys, all_values, query_pos, key_pos):
    row_count = queries.shape[0]
    group_size = ATT_HEADS // KV_HEADS
    q_groups = queries.reshape(row_count, KV_HEADS, group_size, HEAD_DIM)
    key_blocks, value_blocks, pos_blocks = split_blocks(all_keys, all_values, key_pos)

    def max_step(carried, block_item):
        running_max, running_sum = carried
        scores = score_block(q_groups, query_pos, block_item[0], block_item[1])
        new_max = jnp.maximum(running_max, jnp.max(scores, axis=-1))
        running_sum = running_sum * jnp.exp(running_max - new_max) + jnp.sum(
            jnp.exp(scores - new_max[..., None]), axis=-1
        )
        return ((new_max, running_sum), None)

    start_max = jnp.full((KV_HEADS, group_size, row_count), NEG_LARGE, jnp.float32)
    (final_max, final_sum), unused = lax.scan(
        max_step, (start_max, jnp.zeros_like(start_max)), (key_blocks, pos_blocks)
    )
    log_total = final_max + jnp.log(final_sum)

    def out_step(weighted, block_item):
        scores = score_block(q_groups, query_pos, block_item[0], block_item[2])
        attn_prob = jnp.exp(scores - log_total[..., None]).astype(jnp.bfloat16)
        return (
            weighted
            + jnp.einsum(
                "kgts,skd->tkgd", attn_prob, block_item[1], preferred_element_type=jnp.float32
            ),
            None,
        )

    start_out = jnp.zeros((row_count, KV_HEADS, group_size, HEAD_DIM), jnp.float32)
    weighted, unused_two = lax.scan(out_step, start_out, (key_blocks, value_blocks, pos_blocks))
    return (weighted.reshape(row_count, ATT_HEADS * HEAD_DIM), log_total)


def attention_backward(
    queries, all_keys, all_values, query_pos, key_pos, log_total, attn_f32, grad_attn
):
    row_count = queries.shape[0]
    key_count = all_keys.shape[0]
    group_size = ATT_HEADS // KV_HEADS
    score_scale = HEAD_DIM ** (-0.5)
    q_groups = queries.reshape(row_count, KV_HEADS, group_size, HEAD_DIM)
    d_groups = grad_attn.reshape(row_count, KV_HEADS, group_size, HEAD_DIM)
    row_dot = jnp.sum(
        (grad_attn.astype(jnp.float32) * attn_f32).reshape(
            row_count, KV_HEADS, group_size, HEAD_DIM
        ),
        axis=-1,
    )
    row_dot = jnp.transpose(row_dot, (1, 2, 0))
    key_blocks, value_blocks, pos_blocks = split_blocks(all_keys, all_values, key_pos)

    def grad_step(grad_q, block_item):
        key_block, value_block, pos_block = block_item
        scores = score_block(q_groups, query_pos, key_block, pos_block)
        attn_prob = jnp.exp(scores - log_total[..., None])
        grad_prob = jnp.einsum(
            "tkgd,skd->kgts", d_groups, value_block, preferred_element_type=jnp.float32
        )
        grad_score = (attn_prob * (grad_prob - row_dot[..., None])).astype(jnp.bfloat16)
        grad_vb = jnp.einsum(
            "kgts,tkgd->skd",
            attn_prob.astype(jnp.bfloat16),
            d_groups,
            preferred_element_type=jnp.float32,
        )
        grad_kb = (
            jnp.einsum("kgts,tkgd->skd", grad_score, q_groups, preferred_element_type=jnp.float32)
            * score_scale
        )
        grad_q = (
            grad_q
            + jnp.einsum(
                "kgts,skd->tkgd", grad_score, key_block, preferred_element_type=jnp.float32
            )
            * score_scale
        )
        return (grad_q, (grad_kb, grad_vb))

    start_q = jnp.zeros((row_count, KV_HEADS, group_size, HEAD_DIM), jnp.float32)
    grad_q, (grad_keys, grad_values) = lax.scan(
        grad_step, start_q, (key_blocks, value_blocks, pos_blocks)
    )
    return (
        grad_q.reshape(row_count, ATT_HEADS, HEAD_DIM),
        grad_keys.reshape(key_count, KV_HEADS * HEAD_DIM),
        grad_values.reshape(key_count, KV_HEADS * HEAD_DIM),
    )


def chain_scan(fresh, decays, reverse):
    dev_count, _, rows, width = fresh.shape
    spans = 2 * dev_count

    def kernel(fresh_ref, decay_ref, out_ref):
        state = jnp.zeros((rows, width), jnp.float32)
        for step in range(spans):
            at = spans - 1 - step if reverse else step
            dev, half = (at, 0) if at < dev_count else (spans - 1 - at, 1)
            out_ref[dev, half] = state.astype(jnp.bfloat16)
            state = decay_ref[:, at : at + 1] * state + fresh_ref[dev, half].astype(jnp.float32)

    return pl.pallas_call(
        kernel, out_shape=jax.ShapeDtypeStruct(fresh.shape, jnp.bfloat16), name="chain_scan"
    )(fresh, decays)


TILE = 256


def ring_order(dev_count):
    if dev_count != 16:
        return list(range(dev_count))
    order = []
    for k, plane in enumerate((0, 1, 3, 2)):
        line = range(4) if k % 2 == 0 else range(3, -1, -1)
        order += [4 * z + plane for z in line]
    return order


def scatter_ring(array):
    order = ring_order(lax.axis_size("ctx"))
    return lax.psum_scatter(
        array, "ctx", scatter_dimension=0, tiled=True, axis_index_groups=[order]
    )


def half_grads(core, dev_count, block_rows, segments):
    order = ring_order(dev_count)
    operands, specs, plan, scratch = [], [], [], []
    start = 0
    for (x_own, x_sib, x_col, x_width), pieces, columns in segments:
        tokens = x_own.shape[0]
        rows = x_width // (2 * dev_count)
        entry = {"rows": rows, "tokens": tokens, "width": x_width, "x": len(operands)}
        for arr in (x_own, x_sib):
            operands.append(arr)
            specs.append(pl.BlockSpec((tokens, x_width), lambda j, c, at=x_col // x_width: (0, at)))
        entry["dy"] = []
        count = columns // TILE
        for d_own, d_sib, d_col in pieces:
            entry["dy"].append(len(operands))
            for arr in (d_own, d_sib):
                operands.append(arr)
                specs.append(
                    pl.BlockSpec(
                        (tokens, TILE),
                        lambda j, c, base=d_col // TILE, first=start, last=count - 1: (
                            0,
                            base + jnp.clip(j - first, 0, last),
                        ),
                    )
                )
        entry["start"], entry["stop"] = start, start + count
        entry["scratch"] = len(scratch)
        scratch += [
            pltpu.VMEM((x_width, 2 * tokens), jnp.bfloat16),
            pltpu.VMEM((x_width // 2, 2 * tokens), jnp.bfloat16),
        ]
        start += count
        plan.append(entry)
    total = start

    def kernel(core_ref, *refs):
        ins = refs[: len(operands)]
        out_ref = refs[len(operands)]
        spare = refs[len(operands) + 1 :]
        step = pl.program_id(0)
        half = core_ref[0]
        for entry in plan:
            whole, picked = spare[entry["scratch"]], spare[entry["scratch"] + 1]
            rows = entry["rows"]

            @pl.when(step == entry["start"])
            def _():
                both = jnp.concatenate([ins[entry["x"]][...], ins[entry["x"] + 1][...]], axis=0)
                whole[...] = both.T
                for k, dev in enumerate(order):
                    at = pl.multiple_of(2 * dev * rows + half * rows, rows)
                    picked[k * rows : (k + 1) * rows, :] = whole[pl.ds(at, rows), :]

            @pl.when((step >= entry["start"]) & (step < entry["stop"]))
            def _():
                for slot, at in enumerate(entry["dy"]):
                    grads = jnp.concatenate([ins[at][...], ins[at + 1][...]], axis=0)
                    made = jnp.dot(picked[...], grads, preferred_element_type=jnp.float32)
                    out_ref[:, slot * rows : (slot + 1) * rows, :] = made.astype(
                        jnp.bfloat16
                    ).reshape(dev_count, rows, TILE)

    return pl.pallas_call(
        kernel,
        out_shape=jax.ShapeDtypeStruct((dev_count, block_rows, total * TILE), jnp.bfloat16),
        grid_spec=pltpu.PrefetchScalarGridSpec(
            num_scalar_prefetch=1,
            grid=(total,),
            in_specs=specs,
            out_specs=pl.BlockSpec((dev_count, block_rows, TILE), lambda j, c: (0, 0, j)),
            scratch_shapes=scratch,
        ),
        compiler_params=pltpu.CompilerParams(dimension_semantics=("arbitrary",)),
        name="half_grads",
    )(core.reshape(1), *operands)


def dense_core(joined, residual, grad_top, norm_gain2, gathered):
    tokens, width = residual.shape
    devs, block, _ = gathered.shape
    mixed = devs * block
    in_rows = block // 2
    down_devs = TILE // block
    tiles = FF // TILE
    bundle_width = 3 * FF + 2 * width
    transposed = (((1,), (1,)), ((), ()))

    def kernel(
        joined_ref,
        res_ref,
        top_ref,
        gain_ref,
        out_w_ref,
        in_w_ref,
        down_ref,
        outputs_ref,
        grad_mid_ref,
        grad_joined_ref,
        gain_grad_ref,
        bundle_ref,
        middle,
        total,
        grad_norm,
    ):
        step = pl.program_id(0)

        @pl.when(step == 0)
        def _():
            weights = out_w_ref[...].reshape(mixed, width)
            mid = res_ref[...] + jnp.dot(
                joined_ref[...], weights, preferred_element_type=jnp.float32
            )
            middle[...] = mid
            scale = lax.rsqrt(jnp.mean(mid * mid, axis=-1, keepdims=True) + EPSILON)
            bundle_ref[:, 3 * FF : 3 * FF + width] = (mid * scale * gain_ref[...]).astype(
                jnp.bfloat16
            )
            total[...] = jnp.zeros_like(total)
            grad_norm[...] = jnp.zeros_like(grad_norm)

        normed = bundle_ref[:, 3 * FF : 3 * FF + width]
        w_gate = in_w_ref[:, :in_rows, :].reshape(width, TILE)
        w_up = in_w_ref[:, in_rows:, :].reshape(width, TILE)
        w_down = down_ref[...].reshape(TILE, width)
        gate = jnp.dot(normed, w_gate, preferred_element_type=jnp.float32)
        up_part = jnp.dot(normed, w_up, preferred_element_type=jnp.float32)
        sig = jax.nn.sigmoid(gate)
        silu = gate * sig
        activated = (silu * up_part).astype(jnp.bfloat16)
        total[...] += jnp.dot(activated, w_down, preferred_element_type=jnp.float32)
        grad_act = lax.dot_general(
            top_ref[...].astype(jnp.bfloat16), w_down, transposed, preferred_element_type=jnp.float32
        )
        grad_gate = (grad_act * up_part * sig * (1.0 + gate * (1.0 - sig))).astype(jnp.bfloat16)
        grad_up = (grad_act * silu).astype(jnp.bfloat16)
        grad_norm[...] += lax.dot_general(
            grad_gate, w_gate, transposed, preferred_element_type=jnp.float32
        ) + lax.dot_general(grad_up, w_up, transposed, preferred_element_type=jnp.float32)
        at = pl.multiple_of(step * TILE, TILE)
        bundle_ref[:, pl.ds(at, TILE)] = activated
        bundle_ref[:, pl.ds(FF + at, TILE)] = grad_gate
        bundle_ref[:, pl.ds(2 * FF + at, TILE)] = grad_up

        @pl.when(step == tiles - 1)
        def _():
            mid = middle[...]
            outputs_ref[...] = mid + total[...]
            scale = lax.rsqrt(jnp.mean(mid * mid, axis=-1, keepdims=True) + EPSILON)
            unit = mid * scale
            grads = grad_norm[...]
            gain_grad_ref[...] = jnp.sum(grads * unit, axis=0, keepdims=True)
            scaled = grads * gain_ref[...]
            grad_mid = top_ref[...] + scale * (
                scaled - unit * jnp.mean(scaled * unit, axis=-1, keepdims=True)
            )
            grad_mid_ref[...] = grad_mid
            grad_mid_b = grad_mid.astype(jnp.bfloat16)
            bundle_ref[:, 3 * FF + width :] = grad_mid_b
            grad_joined_ref[...] = lax.dot_general(
                grad_mid_b,
                out_w_ref[...].reshape(mixed, width),
                transposed,
                preferred_element_type=jnp.float32,
            )

    def whole(shape):
        return pl.BlockSpec(shape, lambda j: (0,) * len(shape))

    return pl.pallas_call(
        kernel,
        grid=(tiles,),
        out_shape=(
            jax.ShapeDtypeStruct((tokens, width), jnp.float32),
            jax.ShapeDtypeStruct((tokens, width), jnp.float32),
            jax.ShapeDtypeStruct((tokens, mixed), jnp.float32),
            jax.ShapeDtypeStruct((1, width), jnp.float32),
            jax.ShapeDtypeStruct((tokens, bundle_width), jnp.bfloat16),
        ),
        in_specs=[
            whole((tokens, mixed)),
            whole((tokens, width)),
            whole((tokens, width)),
            whole((1, width)),
            pl.BlockSpec((devs, block, width), lambda j: (0, 0, FF // width)),
            pl.BlockSpec((devs, block, TILE), lambda j: (0, 0, j)),
            pl.BlockSpec((down_devs, block, width), lambda j: (j, 0, FF // width + 1)),
        ],
        out_specs=(
            whole((tokens, width)),
            whole((tokens, width)),
            whole((tokens, mixed)),
            whole((1, width)),
            whole((tokens, bundle_width)),
        ),
        scratch_shapes=[pltpu.VMEM((tokens, width), jnp.float32)] * 3,
        compiler_params=pltpu.CompilerParams(
            dimension_semantics=("arbitrary",), vmem_limit_bytes=56 << 20
        ),
        name="dense_core",
    )(joined, residual, grad_top, norm_gain2.reshape(1, width), gathered, gathered, gathered)


def swap(array):
    return lax.ppermute(array, "wsh", [(0, 1), (1, 0)])


def double(block, bits):
    size, me = lax.axis_size("ctx"), lax.axis_index("ctx")
    held = []
    for bit in bits:
        other = lax.ppermute(block, "ctx", [(i, i ^ (1 << bit)) for i in range(size)])
        low = ((me >> bit) & 1) == 0
        held = sorted(held + [bit], reverse=True)
        block = jnp.stack(
            [jnp.where(low, block, other), jnp.where(low, other, block)], axis=held.index(bit)
        )
    return block.reshape(-1, block.shape[-1])


def half_pair(values, dev_count, core):
    tokens, width = values.shape
    blocks = values.T.reshape(dev_count, 2, width // (2 * dev_count), tokens)
    own = lax.dynamic_index_in_dim(blocks, core, 1, keepdims=False)
    other = lax.dynamic_index_in_dim(blocks, 1 - core, 1, keepdims=False)
    joined = jnp.concatenate([own, swap(other)], axis=-1)
    return joined.reshape(width // 2, 2 * tokens)


def both_cores(values):
    return jnp.concatenate([values, swap(values)], axis=0)


def exchange(array):
    return lax.all_to_all(array, "ctx", 0, 0, tiled=True)


def butterfly_sum(array):
    array = array + swap(array)
    size = lax.axis_size("ctx")
    step = 1
    while step < size:
        array = array + lax.ppermute(array, "ctx", [(i, i ^ step) for i in range(size)])
        step *= 2
    return array


def body(
    inputs,
    norm_gain1,
    mix_in,
    step_proj,
    conv_weight,
    conv_bias,
    step_bias,
    decay_log,
    skip_gain,
    mamba_gain,
    mix_out,
    norm_gain2,
    mlp_in,
    mlp_out,
    out_grad,
):
    residual = inputs[0]
    row_count, width = residual.shape
    half_rows = row_count // 2
    rim_len = CONV - 1
    q_width = ATT_HEADS * HEAD_DIM
    kv_width = KV_HEADS * HEAD_DIM
    dev_count = lax.axis_size("ctx")
    device = lax.axis_index("ctx")
    core = lax.axis_index("wsh")
    is_last = device == dev_count - 1
    state_rows = MHEADS * MHEAD_DIM // dev_count
    in_rows = mix_in.shape[0]
    out_rows = mix_out.shape[0]
    up = [(i, i + 1) for i in range(dev_count - 1)]
    down = [(j, i) for i, j in up]
    local_pos = token_positions(
        device, dev_count, row_count, jnp.arange(row_count, dtype=jnp.int32)
    )
    key_ids = jnp.arange(row_count * dev_count, dtype=jnp.int32)
    key_pos = token_positions(key_ids // row_count, dev_count, row_count, key_ids % row_count)
    top = dev_count.bit_length() - 1
    high = tuple(range(top - 1, 1, -1))
    edges = (INNER, INNER + 1024, INNER + 2048, mix_in.shape[1])
    mix_own, mix_sib = [], []
    for piece, bits in enumerate((high + (1, 0), (0,) + high + (1,), (1, 0) + high)):
        mix_own.append(double(mix_in[:, edges[piece] : edges[piece + 1]], bits))
        mix_sib.append(swap(mix_own[-1]))
    half_gate = INNER // 2
    packed = jnp.concatenate(
        [
            jnp.concatenate([mlp_in[:, :FF], mlp_in[:, FF:]], axis=0),
            mix_out,
            mlp_out,
            jnp.concatenate([mix_in[:, :half_gate], mix_in[:, half_gate:INNER]], axis=0),
        ],
        axis=1,
    )
    normed1 = rms_scale(residual, norm_gain1).astype(jnp.bfloat16)
    tail_first = normed1[half_rows - rim_len : half_rows]
    tail_second = normed1[row_count - rim_len :]
    rim_first = lax.ppermute(tail_first, "ctx", up)
    rim_second = jnp.where(is_last, tail_first, lax.ppermute(tail_second, "ctx", down))
    spare = 16 - 2 * rim_len
    extended = jnp.concatenate(
        [normed1, rim_first, rim_second, jnp.zeros((spare, width), jnp.bfloat16)], axis=0
    )
    step_raw = jnp.dot(normed1, step_proj, preferred_element_type=jnp.float32)
    step_pair = step_raw.reshape(2, half_rows, MHEADS)
    early_steps = jax.nn.softplus(step_pair + step_bias[None, None, :])
    decays = jnp.exp(jnp.sum(early_steps * -jnp.exp(decay_log), axis=1))
    all_decays = exchange(
        jnp.broadcast_to(decays.reshape(1, 2 * MHEADS), (dev_count, 2 * MHEADS))
    ).reshape(dev_count, 2, MHEADS)
    span_decays = jnp.concatenate([all_decays[:, 0], all_decays[::-1, 1]], axis=0)
    row_head = (device * state_rows + jnp.arange(state_rows)) // MHEAD_DIM
    row_pick = (row_head[:, None] == jnp.arange(MHEADS)[None, :]).astype(jnp.float32)
    row_decays = jnp.dot(row_pick, span_decays.T, precision=HIGHEST)
    grad_top = out_grad[0]
    grad_top_b = grad_top.astype(jnp.bfloat16)
    extended, row_decays = lax.optimization_barrier((extended, row_decays))
    by_core = extended.reshape(-1, dev_count, 2, in_rows)
    ext_own = lax.dynamic_index_in_dim(by_core, core, 2, keepdims=False).reshape(-1, width // 2)
    ext_sib = lax.dynamic_index_in_dim(by_core, 1 - core, 2, keepdims=False).reshape(-1, width // 2)
    gathered = lax.all_gather(packed, ("ctx", "wsh"), axis=0)
    if out_rows < 64:
        group = 64 // out_rows
        gathered = jnp.concatenate(
            [
                jnp.concatenate(
                    [
                        part.reshape(-1, group * in_rows, part.shape[-1])
                        for part in (piece[:, :in_rows], piece[:, in_rows:])
                    ],
                    axis=1,
                )
                if split
                else piece.reshape(-1, group * out_rows, piece.shape[-1])
                for piece, split in (
                    (gathered[:, :, :FF], True),
                    (gathered[:, :, FF : FF + 2 * width], False),
                    (gathered[:, :, FF + 2 * width :], True),
                )
            ],
            axis=2,
        )
    split_row = gathered.shape[1] // 2
    mix_gate = jnp.concatenate(
        [
            gathered[:, :split_row, FF + 2 * width :].reshape(width, half_gate),
            gathered[:, split_row:, FF + 2 * width :].reshape(width, half_gate),
        ],
        axis=1,
    )

    projected = jnp.concatenate(
        [
            jnp.dot(ext_own, own, preferred_element_type=jnp.float32)
            + jnp.dot(ext_sib, sib, preferred_element_type=jnp.float32)
            for own, sib in zip(mix_own, mix_sib)
        ],
        axis=1,
    )
    conv_all = projected[:, :CONV_CH]
    attn_cols = projected[:row_count, CONV_CH:]
    q_raw = attn_cols[:, :q_width].reshape(row_count, ATT_HEADS, HEAD_DIM)
    k_raw = attn_cols[:, q_width : q_width + kv_width].reshape(row_count, KV_HEADS, HEAD_DIM)
    v_raw = attn_cols[:, q_width + kv_width :]
    padded = jnp.stack(
        [
            jnp.concatenate(
                [conv_all[row_count : row_count + rim_len], conv_all[:half_rows]], axis=0
            ),
            jnp.concatenate(
                [
                    conv_all[row_count + rim_len : row_count + 2 * rim_len],
                    conv_all[half_rows:row_count],
                ],
                axis=0,
            ),
        ]
    )

    def local_parts(padded_one, step_one):
        x_heads, step_size, decay_rate, b_proj, c_proj = mixer_inputs(
            padded_one, step_one, conv_weight, conv_bias, step_bias, decay_log
        )
        local_out, fresh_state, cumulative = span_local(
            x_heads, step_size, decay_rate, b_proj, c_proj, skip_gain
        )
        return (local_out, fresh_state, cumulative, c_proj)

    local_out, fresh_state, cumulative, c_proj = jax.vmap(local_parts)(padded, step_pair)
    queries = rope_apply(q_raw, local_pos).astype(jnp.bfloat16)
    keys_local = rope_apply(k_raw, local_pos).reshape(row_count, kv_width).astype(jnp.bfloat16)

    def to_slices(states):
        return (
            states.astype(jnp.bfloat16)
            .reshape(2, dev_count, state_rows, STATE)
            .transpose(1, 0, 2, 3)
            .reshape(dev_count, 2 * state_rows, STATE)
        )

    def from_slices(slices):
        return (
            slices.reshape(dev_count, 2, state_rows, STATE)
            .transpose(1, 0, 2, 3)
            .reshape(2, MHEADS, MHEAD_DIM, STATE)
            .astype(jnp.float32)
        )

    kv_local = jnp.concatenate([keys_local, v_raw.astype(jnp.bfloat16)], axis=0)
    arrived = exchange(
        jnp.concatenate(
            [
                to_slices(fresh_state),
                jnp.broadcast_to(kv_local[None], (dev_count, 2 * row_count, kv_width)),
            ],
            axis=1,
        )
    )
    fresh_all = arrived[:, : 2 * state_rows].reshape(dev_count, 2, state_rows, STATE)
    all_keys = arrived[:, 2 * state_rows : 2 * state_rows + row_count].reshape(-1, kv_width)
    all_values = arrived[:, 2 * state_rows + row_count :].reshape(-1, kv_width)
    entering = chain_scan(fresh_all, row_decays, False)
    entering, local_out = lax.optimization_barrier((entering, local_out))
    states = from_slices(exchange(entering.reshape(dev_count, 2 * state_rows, STATE)))
    ssm_out = (local_out + jax.vmap(carry_term)(c_proj, cumulative, states)).reshape(
        row_count, INNER
    )
    gate_z = jnp.dot(normed1, mix_gate, preferred_element_type=jnp.float32)
    mamba_part = gated_tail(ssm_out, gate_z, mamba_gain)
    attn_f32, log_total = attention_forward(queries, all_keys, all_values, local_pos, key_pos)
    joined = jnp.concatenate(
        [mamba_part.astype(jnp.bfloat16), attn_f32.astype(jnp.bfloat16)], axis=1
    )
    outputs, grad_middle, grad_joined, gain2_part, bundle = dense_core(
        joined, residual, grad_top, norm_gain2, gathered
    )
    unused_tail, tail_back = jax.vjp(gated_tail, ssm_out, gate_z, mamba_gain)
    grad_ssm, grad_z, mgain_part = tail_back(grad_joined[:, :INNER])
    grad_z = grad_z.astype(jnp.bfloat16)

    def half_grad(values, grads):
        order = ring_order(dev_count)
        made = jnp.dot(
            half_pair(values, dev_count, core),
            both_cores(grads),
            preferred_element_type=jnp.float32,
        ).astype(jnp.bfloat16)
        made = made.reshape(dev_count, -1, grads.shape[1])
        return made[jnp.array(order)] if order != list(range(dev_count)) else made

    if in_rows % 16 == 0:
        bundle_s = swap(bundle)
        norm1_s, joined_s, top_s, grad_z_s = swap(normed1), swap(joined), swap(grad_top_b), swap(grad_z)
        mid_at = 3 * FF + width
        grad_pack = half_grads(
            core,
            dev_count,
            out_rows,
            (
                (
                    (bundle, bundle_s, 3 * FF, width),
                    ((bundle, bundle_s, FF), (bundle, bundle_s, 2 * FF)),
                    FF,
                ),
                ((joined, joined_s, 0, joined.shape[1]), ((bundle, bundle_s, mid_at),), width),
                ((bundle, bundle_s, 0, FF), ((grad_top_b, top_s, 0),), width),
                (
                    (normed1, norm1_s, 0, width),
                    ((grad_z, grad_z_s, 0), (grad_z, grad_z_s, half_gate)),
                    half_gate,
                ),
            ),
        )
    else:
        up_half = half_grad(bundle[:, 3 * FF : 3 * FF + width], bundle[:, FF : 3 * FF])
        gate_half = half_grad(normed1, grad_z)
        grad_pack = jnp.concatenate(
            [
                jnp.concatenate([up_half[:, :, :FF], up_half[:, :, FF:]], axis=1),
                half_grad(joined, bundle[:, 3 * FF + width :]),
                half_grad(bundle[:, :FF], grad_top_b),
                jnp.concatenate(
                    [gate_half[:, :, :half_gate], gate_half[:, :, half_gate:]], axis=1
                ),
            ],
            axis=2,
        )
    grad_pack = grad_pack.reshape(dev_count * out_rows, -1)
    grad_joined, grad_ssm, grad_pack = lax.optimization_barrier((grad_joined, grad_ssm, grad_pack))
    pack_shard = scatter_ring(grad_pack)
    grad_pair = grad_ssm.reshape(2, half_rows, INNER)
    grad_heads = grad_ssm.reshape(2, half_rows, MHEADS, MHEAD_DIM)
    own_grads = jnp.einsum(
        "athp,atn->ahpn",
        grad_heads * jnp.exp(cumulative)[:, :, :, None],
        c_proj,
        precision=HIGHEST,
    )
    grad_attn = grad_joined[:, INNER:].astype(jnp.bfloat16)
    grad_q, grad_keys, grad_values = attention_backward(
        queries, all_keys, all_values, local_pos, key_pos, log_total, attn_f32, grad_attn
    )
    kv_grads = jnp.concatenate(
        [
            grad_keys.astype(jnp.bfloat16).reshape(dev_count, row_count, kv_width),
            grad_values.astype(jnp.bfloat16).reshape(dev_count, row_count, kv_width),
        ],
        axis=1,
    )
    returned = exchange(jnp.concatenate([to_slices(own_grads), kv_grads], axis=1))
    own_all = returned[:, : 2 * state_rows].reshape(dev_count, 2, state_rows, STATE)
    kv_back = jnp.sum(returned[:, 2 * state_rows :].astype(jnp.float32), axis=0)
    keys_back = kv_back[:row_count]
    values_back = kv_back[row_count:]
    leaving = chain_scan(own_all, row_decays, True)
    end_grads = from_slices(exchange(leaving.reshape(dev_count, 2 * state_rows, STATE)))
    unused_q, rope_back_q = jax.vjp(partial(rope_apply, positions=local_pos), q_raw)
    unused_k, rope_back_k = jax.vjp(partial(rope_apply, positions=local_pos), k_raw)
    (grad_q_raw,) = rope_back_q(grad_q)
    (grad_k_raw,) = rope_back_k(keys_back.reshape(row_count, KV_HEADS, HEAD_DIM))
    pair_mixer = jax.vmap(half_mixer, in_axes=(0, 0, None, None, None, None, None, 0))
    unused_m, mixer_back = jax.vjp(
        pair_mixer,
        padded,
        step_pair,
        conv_weight,
        conv_bias,
        step_bias,
        decay_log,
        skip_gain,
        states,
    )
    mixer_grads = mixer_back((grad_pair, end_grads))
    grad_padded = mixer_grads[0]
    grad_rims = grad_padded[:, :rim_len].reshape(2 * rim_len, CONV_CH)
    grad_conv = grad_padded[:, rim_len:].reshape(row_count, CONV_CH)
    grad_proj = jnp.concatenate(
        [
            jnp.concatenate(
                [
                    grad_conv,
                    grad_q_raw.reshape(row_count, q_width),
                    grad_k_raw.reshape(row_count, kv_width),
                    values_back,
                ],
                axis=1,
            ).astype(jnp.bfloat16),
            jnp.pad(
                grad_rims.astype(jnp.bfloat16), ((0, spare), (0, q_width + 2 * kv_width))
            ),
        ],
        axis=0,
    )
    if in_rows % 16 == 0:
        in_half = half_grads(
            core,
            dev_count,
            in_rows,
            (
                (
                    (extended, swap(extended), 0, width),
                    ((grad_proj, swap(grad_proj), 0),),
                    grad_proj.shape[1],
                ),
            ),
        )
    else:
        in_half = half_grad(extended, grad_proj)
    in_half = in_half.reshape(dev_count * in_rows, -1)
    in_half, pack_shard = lax.optimization_barrier((in_half, pack_shard))
    in_shard = scatter_ring(in_half)
    grad_step = mixer_grads[1].reshape(row_count, MHEADS).astype(jnp.bfloat16)
    step_grad = jnp.dot(grad_step.T, normed1, preferred_element_type=jnp.float32)
    ext_halves = [0.0, 0.0]
    for piece, pair in enumerate(zip(mix_own, mix_sib)):
        grads = grad_proj[:, edges[piece] - INNER : edges[piece + 1] - INNER]
        for side, weights in enumerate(pair):
            ext_halves[side] += jnp.dot(grads, weights.T, preferred_element_type=jnp.float32)
    first_core = core == 0
    halves = [half.reshape(-1, dev_count, in_rows) for half in ext_halves]
    grad_ext = jnp.stack(
        [jnp.where(first_core, halves[0], halves[1]), jnp.where(first_core, halves[1], halves[0])],
        axis=2,
    ).reshape(-1, width)
    back_first = grad_ext[row_count : row_count + rim_len]
    back_second = grad_ext[row_count + rim_len : row_count + 2 * rim_len]
    add_first = lax.ppermute(back_first, "ctx", down) + jnp.where(is_last, back_second, 0.0)
    add_second = lax.ppermute(back_second, "ctx", up)
    fill = jnp.zeros((half_rows - rim_len, width), jnp.float32)
    grad_normed1 = (
        grad_ext[:row_count]
        + jnp.concatenate([fill, add_first, fill, add_second], axis=0)
        + jnp.dot(grad_step, step_proj.T, preferred_element_type=jnp.float32)
        + jnp.dot(grad_z, mix_gate.T, preferred_element_type=jnp.float32)
    )
    unused_one, norm_back1 = jax.vjp(rms_scale, residual, norm_gain1)
    grad_res_n, gain1_part = norm_back1(grad_normed1)
    input_grad = grad_middle + grad_res_n
    parts = (
        gain1_part,
        step_grad,
        mixer_grads[2],
        mixer_grads[3],
        mgain_part,
        gain2_part,
        mixer_grads[4],
        mixer_grads[5],
        mixer_grads[6],
    )
    flat = jnp.concatenate([part.reshape(-1) for part in parts])
    total_len = flat.shape[0]
    summed = butterfly_sum(jnp.pad(flat, (0, -total_len % 1024)).reshape(-1, 128)).reshape(-1)
    sums = []
    start = 0
    for part in parts:
        sums.append(summed[start : start + part.size].reshape(part.shape))
        start += part.size
    pack_f32 = pack_shard.astype(jnp.float32)
    up_shard = jnp.concatenate([pack_f32[:in_rows, :FF], pack_f32[in_rows:, :FF]], axis=1)
    return (
        outputs[None],
        input_grad[None],
        sums[0],
        jnp.concatenate(
            [
                pack_f32[:in_rows, FF + 2 * width :],
                pack_f32[in_rows:, FF + 2 * width :],
                in_shard.astype(jnp.float32),
            ],
            axis=1,
        ),
        sums[1].T,
        sums[2],
        sums[3],
        sums[6],
        sums[7],
        sums[8],
        sums[4],
        pack_f32[:, FF : FF + width],
        sums[5].reshape(-1),
        up_shard,
        pack_f32[:, FF + width : FF + 2 * width],
    )


def solution(mesh):
    return jax.shard_map(
        body,
        mesh=mesh,
        in_specs=(
            P("wsh", "ctx", None),
            P(),
            P(("ctx", "wsh"), None),
            P(),
            P(),
            P(),
            P(),
            P(),
            P(),
            P(),
            P(("ctx", "wsh"), None),
            P(),
            P(("ctx", "wsh"), None),
            P(("ctx", "wsh"), None),
            P("wsh", "ctx", None),
        ),
        out_specs=(
            P("wsh", "ctx", None),
            P("wsh", "ctx", None),
            P(),
            P(("ctx", "wsh"), None),
            P(),
            P(),
            P(),
            P(),
            P(),
            P(),
            P(),
            P(("ctx", "wsh"), None),
            P(),
            P(("ctx", "wsh"), None),
            P(("ctx", "wsh"), None),
        ),
        check_vma=False,
    )
```

```python
from functools import partial

import jax
import jax.numpy as jnp
from jax import lax
from jax.experimental import pallas as pl
from jax.experimental.pallas import tpu as pltpu
from jax.sharding import PartitionSpec as P

MHEADS = 24
MHEAD_DIM = 64
STATE = 128
CONV = 4
ATT_HEADS = 8
KV_HEADS = 2
HEAD_DIM = 64
FF = 2048
INNER = 1536
CONV_CH = 1792


EPSILON = 1e-05
ROPE_BASE = 10000.0
NEG_LARGE = -1e30
HIGHEST = lax.Precision.HIGHEST


def rms_scale(values, gain_vec):
    return (
        values * lax.rsqrt(jnp.mean(values * values, axis=-1, keepdims=True) + EPSILON) * gain_vec
    )


def rope_apply(values, positions):
    half_dim = values.shape[-1] // 2
    frequency = ROPE_BASE ** (-jnp.arange(half_dim, dtype=jnp.float32) / half_dim)
    angles = positions.astype(jnp.float32)[:, None] * frequency[None, :]
    cosine = jnp.cos(angles)[:, None, :]
    sine_v = jnp.sin(angles)[:, None, :]
    first_part = values[..., :half_dim]
    second = values[..., half_dim:]
    return jnp.concatenate(
        [first_part * cosine - second * sine_v, second * cosine + first_part * sine_v], axis=-1
    )


def token_positions(device, dev_count, row_count, row_index):
    half_rows = row_count // 2
    return jnp.where(
        row_index < half_rows,
        device * half_rows + row_index,
        (2 * dev_count - 1 - device) * half_rows + row_index - half_rows,
    )


def conv_silu(padded, conv_weight, conv_bias):
    taps_count = conv_weight.shape[0]
    length = padded.shape[0] - taps_count + 1
    summed = conv_bias[None, :]
    for offset in range(taps_count):
        summed = summed + conv_weight[offset][None, :] * padded[offset : offset + length]
    return jax.nn.silu(summed)


def mixer_inputs(padded, step_raw, conv_weight, conv_bias, step_bias, decay_log):
    conv_act = conv_silu(padded, conv_weight, conv_bias)
    x_heads = conv_act[:, :INNER].reshape(conv_act.shape[0], MHEADS, MHEAD_DIM)
    b_proj = conv_act[:, INNER : INNER + STATE]
    c_proj = conv_act[:, INNER + STATE :]
    step_size = jax.nn.softplus(step_raw + step_bias[None, :])
    decay_rate = -jnp.exp(decay_log)
    return (x_heads, step_size, decay_rate, b_proj, c_proj)


def span_local(x_heads, step_size, decay_rate, b_proj, c_proj, skip_gain):
    length = x_heads.shape[0]
    causal = jnp.arange(length)[:, None] >= jnp.arange(length)[None, :]
    cumulative = jnp.cumsum(step_size * decay_rate[None, :], axis=0)
    log_gap = cumulative[:, None, :] - cumulative[None, :, :]
    causal3 = causal[:, :, None]
    decay_mat = jnp.where(causal3, jnp.exp(jnp.where(causal3, log_gap, 0.0)), 0.0)
    intersection = jnp.dot(c_proj, b_proj.T, precision=HIGHEST)
    weights = decay_mat * intersection[:, :, None] * step_size[None, :, :]
    intra_out = jnp.einsum("tsh,shp->thp", weights, x_heads, precision=HIGHEST)
    local_out = intra_out + skip_gain[None, :, None] * x_heads
    tail_weight = jnp.exp(cumulative[-1][None, :] - cumulative) * step_size
    weighted_x = tail_weight[:, :, None] * x_heads
    fresh_state = jnp.einsum("shp,sn->hpn", weighted_x, b_proj, precision=HIGHEST)
    return (local_out, fresh_state, cumulative)


def carry_term(c_proj, cumulative, state_in):
    return (
        jnp.einsum("tn,hpn->thp", c_proj, state_in, precision=HIGHEST)
        * jnp.exp(cumulative)[:, :, None]
    )


def half_mixer(padded, step_raw, conv_weight, conv_bias, step_bias, decay_log, skip_gain, state_in):
    x_heads, step_size, decay_rate, b_proj, c_proj = mixer_inputs(
        padded, step_raw, conv_weight, conv_bias, step_bias, decay_log
    )
    local_out, fresh_state, cumulative = span_local(
        x_heads, step_size, decay_rate, b_proj, c_proj, skip_gain
    )
    result = local_out + carry_term(c_proj, cumulative, state_in)
    new_state = jnp.exp(cumulative[-1])[:, None, None] * state_in + fresh_state
    return (result.reshape(result.shape[0], INNER), new_state)


def gated_tail(ssm_out, gate_z, mamba_gain):
    return rms_scale(ssm_out * jax.nn.silu(gate_z), mamba_gain)


def score_block(q_groups, query_pos, key_block, pos_block):
    raw_scores = jnp.einsum(
        "tkgd,skd->kgts", q_groups, key_block, preferred_element_type=jnp.float32
    ) * HEAD_DIM ** (-0.5)
    return jnp.where(
        pos_block[None, None, None, :] <= query_pos[None, None, :, None], raw_scores, NEG_LARGE
    )


def split_blocks(all_keys, all_values, key_pos):
    key_count = all_keys.shape[0]
    block_len = min(2048, key_count)
    blocks = key_count // block_len
    return (
        all_keys.reshape(blocks, block_len, KV_HEADS, HEAD_DIM),
        all_values.reshape(blocks, block_len, KV_HEADS, HEAD_DIM),
        key_pos.reshape(blocks, block_len),
    )


def attention_forward(queries, all_keys, all_values, query_pos, key_pos):
    row_count = queries.shape[0]
    group_size = ATT_HEADS // KV_HEADS
    q_groups = queries.reshape(row_count, KV_HEADS, group_size, HEAD_DIM)
    key_blocks, value_blocks, pos_blocks = split_blocks(all_keys, all_values, key_pos)

    def max_step(carried, block_item):
        running_max, running_sum = carried
        scores = score_block(q_groups, query_pos, block_item[0], block_item[1])
        new_max = jnp.maximum(running_max, jnp.max(scores, axis=-1))
        running_sum = running_sum * jnp.exp(running_max - new_max) + jnp.sum(
            jnp.exp(scores - new_max[..., None]), axis=-1
        )
        return ((new_max, running_sum), None)

    start_max = jnp.full((KV_HEADS, group_size, row_count), NEG_LARGE, jnp.float32)
    (final_max, final_sum), unused = lax.scan(
        max_step, (start_max, jnp.zeros_like(start_max)), (key_blocks, pos_blocks)
    )
    log_total = final_max + jnp.log(final_sum)

    def out_step(weighted, block_item):
        scores = score_block(q_groups, query_pos, block_item[0], block_item[2])
        attn_prob = jnp.exp(scores - log_total[..., None]).astype(jnp.bfloat16)
        return (
            weighted
            + jnp.einsum(
                "kgts,skd->tkgd", attn_prob, block_item[1], preferred_element_type=jnp.float32
            ),
            None,
        )

    start_out = jnp.zeros((row_count, KV_HEADS, group_size, HEAD_DIM), jnp.float32)
    weighted, unused_two = lax.scan(out_step, start_out, (key_blocks, value_blocks, pos_blocks))
    return (weighted.reshape(row_count, ATT_HEADS * HEAD_DIM), log_total)


def attention_backward(
    queries, all_keys, all_values, query_pos, key_pos, log_total, attn_f32, grad_attn
):
    row_count = queries.shape[0]
    key_count = all_keys.shape[0]
    group_size = ATT_HEADS // KV_HEADS
    score_scale = HEAD_DIM ** (-0.5)
    q_groups = queries.reshape(row_count, KV_HEADS, group_size, HEAD_DIM)
    d_groups = grad_attn.reshape(row_count, KV_HEADS, group_size, HEAD_DIM)
    row_dot = jnp.sum(
        (grad_attn.astype(jnp.float32) * attn_f32).reshape(
            row_count, KV_HEADS, group_size, HEAD_DIM
        ),
        axis=-1,
    )
    row_dot = jnp.transpose(row_dot, (1, 2, 0))
    key_blocks, value_blocks, pos_blocks = split_blocks(all_keys, all_values, key_pos)

    def grad_step(grad_q, block_item):
        key_block, value_block, pos_block = block_item
        scores = score_block(q_groups, query_pos, key_block, pos_block)
        attn_prob = jnp.exp(scores - log_total[..., None])
        grad_prob = jnp.einsum(
            "tkgd,skd->kgts", d_groups, value_block, preferred_element_type=jnp.float32
        )
        grad_score = (attn_prob * (grad_prob - row_dot[..., None])).astype(jnp.bfloat16)
        grad_vb = jnp.einsum(
            "kgts,tkgd->skd",
            attn_prob.astype(jnp.bfloat16),
            d_groups,
            preferred_element_type=jnp.float32,
        )
        grad_kb = (
            jnp.einsum("kgts,tkgd->skd", grad_score, q_groups, preferred_element_type=jnp.float32)
            * score_scale
        )
        grad_q = (
            grad_q
            + jnp.einsum(
                "kgts,skd->tkgd", grad_score, key_block, preferred_element_type=jnp.float32
            )
            * score_scale
        )
        return (grad_q, (grad_kb, grad_vb))

    start_q = jnp.zeros((row_count, KV_HEADS, group_size, HEAD_DIM), jnp.float32)
    grad_q, (grad_keys, grad_values) = lax.scan(
        grad_step, start_q, (key_blocks, value_blocks, pos_blocks)
    )
    return (
        grad_q.reshape(row_count, ATT_HEADS, HEAD_DIM),
        grad_keys.reshape(key_count, KV_HEADS * HEAD_DIM),
        grad_values.reshape(key_count, KV_HEADS * HEAD_DIM),
    )


def chain_scan(fresh, decays, reverse):
    dev_count, _, rows, width = fresh.shape
    spans = 2 * dev_count

    def kernel(fresh_ref, decay_ref, out_ref):
        state = jnp.zeros((rows, width), jnp.float32)
        for step in range(spans):
            at = spans - 1 - step if reverse else step
            dev, half = (at, 0) if at < dev_count else (spans - 1 - at, 1)
            out_ref[dev, half] = state.astype(jnp.bfloat16)
            state = decay_ref[:, at : at + 1] * state + fresh_ref[dev, half].astype(jnp.float32)

    return pl.pallas_call(
        kernel, out_shape=jax.ShapeDtypeStruct(fresh.shape, jnp.bfloat16), name="chain_scan"
    )(fresh, decays)


TILE = 256


def ring_order(dev_count):
    if dev_count != 16:
        return list(range(dev_count))
    order = []
    for k, plane in enumerate((0, 1, 3, 2)):
        line = range(4) if k % 2 == 0 else range(3, -1, -1)
        order += [4 * z + plane for z in line]
    return order


def scatter_ring(array):
    order = ring_order(lax.axis_size("ctx"))
    return lax.psum_scatter(
        array, "ctx", scatter_dimension=0, tiled=True, axis_index_groups=[order]
    )


def half_grads(core, dev_count, block_rows, segments):
    order = ring_order(dev_count)
    operands, specs, plan, scratch = [], [], [], []
    start = 0
    for (x_own, x_sib, x_col, x_width), pieces, columns in segments:
        tokens = x_own.shape[0]
        rows = x_width // (2 * dev_count)
        entry = {"rows": rows, "tokens": tokens, "width": x_width, "x": len(operands)}
        for arr in (x_own, x_sib):
            operands.append(arr)
            specs.append(pl.BlockSpec((tokens, x_width), lambda j, c, at=x_col // x_width: (0, at)))
        entry["dy"] = []
        count = columns // TILE
        for d_own, d_sib, d_col in pieces:
            entry["dy"].append(len(operands))
            for arr in (d_own, d_sib):
                operands.append(arr)
                specs.append(
                    pl.BlockSpec(
                        (tokens, TILE),
                        lambda j, c, base=d_col // TILE, first=start, last=count - 1: (
                            0,
                            base + jnp.clip(j - first, 0, last),
                        ),
                    )
                )
        entry["start"], entry["stop"] = start, start + count
        entry["scratch"] = len(scratch)
        scratch += [
            pltpu.VMEM((x_width, 2 * tokens), jnp.bfloat16),
            pltpu.VMEM((x_width // 2, 2 * tokens), jnp.bfloat16),
        ]
        start += count
        plan.append(entry)
    total = start

    def kernel(core_ref, *refs):
        ins = refs[: len(operands)]
        out_ref = refs[len(operands)]
        spare = refs[len(operands) + 1 :]
        step = pl.program_id(0)
        half = core_ref[0]
        for entry in plan:
            whole, picked = spare[entry["scratch"]], spare[entry["scratch"] + 1]
            rows = entry["rows"]

            @pl.when(step == entry["start"])
            def _():
                both = jnp.concatenate([ins[entry["x"]][...], ins[entry["x"] + 1][...]], axis=0)
                whole[...] = both.T
                for k, dev in enumerate(order):
                    at = pl.multiple_of(2 * dev * rows + half * rows, rows)
                    picked[k * rows : (k + 1) * rows, :] = whole[pl.ds(at, rows), :]

            @pl.when((step >= entry["start"]) & (step < entry["stop"]))
            def _():
                for slot, at in enumerate(entry["dy"]):
                    grads = jnp.concatenate([ins[at][...], ins[at + 1][...]], axis=0)
                    made = jnp.dot(picked[...], grads, preferred_element_type=jnp.float32)
                    out_ref[:, slot * rows : (slot + 1) * rows, :] = made.astype(
                        jnp.bfloat16
                    ).reshape(dev_count, rows, TILE)

    return pl.pallas_call(
        kernel,
        out_shape=jax.ShapeDtypeStruct((dev_count, block_rows, total * TILE), jnp.bfloat16),
        grid_spec=pltpu.PrefetchScalarGridSpec(
            num_scalar_prefetch=1,
            grid=(total,),
            in_specs=specs,
            out_specs=pl.BlockSpec((dev_count, block_rows, TILE), lambda j, c: (0, 0, j)),
            scratch_shapes=scratch,
        ),
        compiler_params=pltpu.CompilerParams(dimension_semantics=("arbitrary",)),
        name="half_grads",
    )(core.reshape(1), *operands)


def dense_core(joined, residual, grad_top, norm_gain2, gathered):
    tokens, width = residual.shape
    devs, block, _ = gathered.shape
    mixed = devs * block
    in_rows = block // 2
    down_devs = TILE // block
    tiles = FF // TILE
    bundle_width = 3 * FF + 2 * width

    def kernel(
        joined_ref,
        res_ref,
        top_ref,
        gain_ref,
        out_w_ref,
        in_w_ref,
        down_ref,
        outputs_ref,
        grad_mid_ref,
        grad_joined_ref,
        gain_grad_ref,
        bundle_ref,
        middle,
        total,
        grad_norm,
        top_turned,
    ):
        step = pl.program_id(0)

        @pl.when(step == 0)
        def _():
            weights = out_w_ref[...].reshape(mixed, width)
            mid = res_ref[...] + jnp.dot(
                joined_ref[...], weights, preferred_element_type=jnp.float32
            )
            middle[...] = mid
            scale = lax.rsqrt(jnp.mean(mid * mid, axis=-1, keepdims=True) + EPSILON)
            bundle_ref[:, 3 * FF : 3 * FF + width] = (mid * scale * gain_ref[...]).astype(
                jnp.bfloat16
            )
            total[...] = jnp.zeros_like(total)
            grad_norm[...] = jnp.zeros_like(grad_norm)
            top_turned[...] = top_ref[...].T.astype(jnp.bfloat16)

        normed = bundle_ref[:, 3 * FF : 3 * FF + width]
        w_gate = in_w_ref[:, :in_rows, :].reshape(width, TILE)
        w_up = in_w_ref[:, in_rows:, :].reshape(width, TILE)
        w_down = down_ref[...].reshape(TILE, width)
        gate = jnp.dot(normed, w_gate, preferred_element_type=jnp.float32)
        up_part = jnp.dot(normed, w_up, preferred_element_type=jnp.float32)
        sig = jax.nn.sigmoid(gate)
        silu = gate * sig
        activated = (silu * up_part).astype(jnp.bfloat16)
        total[...] += jnp.dot(activated, w_down, preferred_element_type=jnp.float32)
        grad_act = jnp.dot(w_down, top_turned[...], preferred_element_type=jnp.float32).T
        grad_gate = grad_act * up_part * sig * (1.0 + gate * (1.0 - sig))
        grad_up = grad_act * silu
        grad_norm[...] += jnp.dot(
            w_gate, grad_gate.T.astype(jnp.bfloat16), preferred_element_type=jnp.float32
        ) + jnp.dot(w_up, grad_up.T.astype(jnp.bfloat16), preferred_element_type=jnp.float32)
        at = pl.multiple_of(step * TILE, TILE)
        bundle_ref[:, pl.ds(at, TILE)] = activated
        bundle_ref[:, pl.ds(FF + at, TILE)] = grad_gate.astype(jnp.bfloat16)
        bundle_ref[:, pl.ds(2 * FF + at, TILE)] = grad_up.astype(jnp.bfloat16)

        @pl.when(step == tiles - 1)
        def _():
            mid = middle[...]
            outputs_ref[...] = mid + total[...]
            scale = lax.rsqrt(jnp.mean(mid * mid, axis=-1, keepdims=True) + EPSILON)
            unit = mid * scale
            grads = grad_norm[...].T
            gain_grad_ref[...] = jnp.sum(grads * unit, axis=0, keepdims=True)
            scaled = grads * gain_ref[...]
            grad_mid = top_ref[...] + scale * (
                scaled - unit * jnp.mean(scaled * unit, axis=-1, keepdims=True)
            )
            grad_mid_ref[...] = grad_mid
            grad_mid_b = grad_mid.astype(jnp.bfloat16)
            bundle_ref[:, 3 * FF + width :] = grad_mid_b
            grad_joined_ref[...] = jnp.dot(
                out_w_ref[...].reshape(mixed, width),
                grad_mid.T.astype(jnp.bfloat16),
                preferred_element_type=jnp.float32,
            ).T

    def whole(shape):
        return pl.BlockSpec(shape, lambda j: (0,) * len(shape))

    return pl.pallas_call(
        kernel,
        grid=(tiles,),
        out_shape=(
            jax.ShapeDtypeStruct((tokens, width), jnp.float32),
            jax.ShapeDtypeStruct((tokens, width), jnp.float32),
            jax.ShapeDtypeStruct((tokens, mixed), jnp.float32),
            jax.ShapeDtypeStruct((1, width), jnp.float32),
            jax.ShapeDtypeStruct((tokens, bundle_width), jnp.bfloat16),
        ),
        in_specs=[
            whole((tokens, mixed)),
            whole((tokens, width)),
            whole((tokens, width)),
            whole((1, width)),
            pl.BlockSpec((devs, block, width), lambda j: (0, 0, FF // width)),
            pl.BlockSpec((devs, block, TILE), lambda j: (0, 0, j)),
            pl.BlockSpec((down_devs, block, width), lambda j: (j, 0, FF // width + 1)),
        ],
        out_specs=(
            whole((tokens, width)),
            whole((tokens, width)),
            whole((tokens, mixed)),
            whole((1, width)),
            whole((tokens, bundle_width)),
        ),
        scratch_shapes=[
            pltpu.VMEM((tokens, width), jnp.float32),
            pltpu.VMEM((tokens, width), jnp.float32),
            pltpu.VMEM((width, tokens), jnp.float32),
            pltpu.VMEM((width, tokens), jnp.bfloat16),
        ],
        compiler_params=pltpu.CompilerParams(
            dimension_semantics=("arbitrary",), vmem_limit_bytes=40 << 20
        ),
        name="dense_core",
    )(joined, residual, grad_top, norm_gain2.reshape(1, width), gathered, gathered, gathered)


def swap(array):
    return lax.ppermute(array, "wsh", [(0, 1), (1, 0)])


def double_step(block, held, bit):
    size, me = lax.axis_size("ctx"), lax.axis_index("ctx")
    other = lax.ppermute(block, "ctx", [(i, i ^ (1 << bit)) for i in range(size)])
    low = ((me >> bit) & 1) == 0
    held = sorted(held + [bit], reverse=True)
    block = jnp.stack(
        [jnp.where(low, block, other), jnp.where(low, other, block)], axis=held.index(bit)
    )
    return block, held


def double(block, bits):
    held = []
    for bit in bits:
        block, held = double_step(block, held, bit)
    return block.reshape(-1, block.shape[-1])


def halve(blocks, bits):
    size, me = lax.axis_size("ctx"), lax.axis_index("ctx")
    shape = blocks.shape[1:]
    held = list(range(size.bit_length() - 2, -1, -1))
    blocks = blocks.reshape((2,) * len(held) + shape)
    for bit in bits:
        axis, mine = held.index(bit), (me >> bit) & 1
        sent = lax.dynamic_index_in_dim(blocks, 1 - mine, axis, keepdims=False)
        kept = lax.dynamic_index_in_dim(blocks, mine, axis, keepdims=False)
        other = lax.ppermute(
            sent.astype(jnp.bfloat16), "ctx", [(i, i ^ (1 << bit)) for i in range(size)]
        )
        blocks = kept.astype(jnp.float32) + other.astype(jnp.float32)
        held.remove(bit)
    return blocks


def half_pair(values, dev_count, core):
    tokens, width = values.shape
    blocks = values.T.reshape(dev_count, 2, width // (2 * dev_count), tokens)
    own = lax.dynamic_index_in_dim(blocks, core, 1, keepdims=False)
    other = lax.dynamic_index_in_dim(blocks, 1 - core, 1, keepdims=False)
    joined = jnp.concatenate([own, swap(other)], axis=-1)
    return joined.reshape(width // 2, 2 * tokens)


def both_cores(values):
    return jnp.concatenate([values, swap(values)], axis=0)


def exchange(array):
    return lax.all_to_all(array, "ctx", 0, 0, tiled=True)


def butterfly_sum(array):
    array = array + swap(array)
    size = lax.axis_size("ctx")
    step = 1
    while step < size:
        array = array + lax.ppermute(array, "ctx", [(i, i ^ step) for i in range(size)])
        step *= 2
    return array


def body(
    inputs,
    norm_gain1,
    mix_in,
    step_proj,
    conv_weight,
    conv_bias,
    step_bias,
    decay_log,
    skip_gain,
    mamba_gain,
    mix_out,
    norm_gain2,
    mlp_in,
    mlp_out,
    out_grad,
):
    residual = inputs[0]
    row_count, width = residual.shape
    half_rows = row_count // 2
    rim_len = CONV - 1
    q_width = ATT_HEADS * HEAD_DIM
    kv_width = KV_HEADS * HEAD_DIM
    dev_count = lax.axis_size("ctx")
    device = lax.axis_index("ctx")
    core = lax.axis_index("wsh")
    is_last = device == dev_count - 1
    state_rows = MHEADS * MHEAD_DIM // dev_count
    in_rows = mix_in.shape[0]
    out_rows = mix_out.shape[0]
    up = [(i, i + 1) for i in range(dev_count - 1)]
    down = [(j, i) for i, j in up]
    local_pos = token_positions(
        device, dev_count, row_count, jnp.arange(row_count, dtype=jnp.int32)
    )
    key_ids = jnp.arange(row_count * dev_count, dtype=jnp.int32)
    key_pos = token_positions(key_ids // row_count, dev_count, row_count, key_ids % row_count)
    half_gate = INNER // 2
    packed = jnp.concatenate(
        [
            jnp.concatenate([mlp_in[:, :FF], mlp_in[:, FF:]], axis=0),
            mix_out,
            mlp_out,
            jnp.concatenate([mix_in[:, :half_gate], mix_in[:, half_gate:INNER]], axis=0),
        ],
        axis=1,
    )
    top = dev_count.bit_length() - 1
    high = tuple(range(top - 1, 1, -1))
    edges = (INNER, INNER + 1024, INNER + 2048, mix_in.shape[1])
    orders = (high + (1, 0), (0,) + high + (1,), (1, 0) + high)
    streams = [(mix_in[:, edges[i] : edges[i + 1]], []) for i in range(3)]
    streams = [double_step(*stream, bits[0]) for stream, bits in zip(streams, orders)]
    led, packed = lax.optimization_barrier((streams[0][0], packed))
    gathered = lax.all_gather(packed, ("ctx", "wsh"), axis=0)
    streams[0] = (led, streams[0][1])
    streams = [double_step(*stream, bits[1]) for stream, bits in zip(streams, orders)]

    normed1 = rms_scale(residual, norm_gain1).astype(jnp.bfloat16)
    led, normed1 = lax.optimization_barrier((streams[2][0], normed1))
    streams[2] = (led, streams[2][1])
    for step in range(2, top - 1):
        streams = [double_step(*stream, bits[step]) for stream, bits in zip(streams, orders)]
    tail_first = normed1[half_rows - rim_len : half_rows]
    tail_second = normed1[row_count - rim_len :]
    rim_first = lax.ppermute(tail_first, "ctx", up)
    rim_second = jnp.where(is_last, tail_first, lax.ppermute(tail_second, "ctx", down))
    spare = 16 - 2 * rim_len
    extended = jnp.concatenate(
        [normed1, rim_first, rim_second, jnp.zeros((spare, width), jnp.bfloat16)], axis=0
    )
    step_raw = jnp.dot(normed1, step_proj, preferred_element_type=jnp.float32)
    step_pair = step_raw.reshape(2, half_rows, MHEADS)
    early_steps = jax.nn.softplus(step_pair + step_bias[None, None, :])
    decays = jnp.exp(jnp.sum(early_steps * -jnp.exp(decay_log), axis=1))
    all_decays = exchange(
        jnp.broadcast_to(decays.reshape(1, 2 * MHEADS), (dev_count, 2 * MHEADS))
    ).reshape(dev_count, 2, MHEADS)
    span_decays = jnp.concatenate([all_decays[:, 0], all_decays[::-1, 1]], axis=0)
    row_head = (device * state_rows + jnp.arange(state_rows)) // MHEAD_DIM
    row_pick = (row_head[:, None] == jnp.arange(MHEADS)[None, :]).astype(jnp.float32)
    row_decays = jnp.dot(row_pick, span_decays.T, precision=HIGHEST)
    grad_top = out_grad[0]
    grad_top_b = grad_top.astype(jnp.bfloat16)
    led, extended, row_decays = lax.optimization_barrier((streams[0][0], extended, row_decays))
    streams[0] = (led, streams[0][1])
    streams = [double_step(*stream, bits[top - 1]) for stream, bits in zip(streams, orders)]
    mix_own = [block.reshape(width // 2, -1) for block, _ in streams]
    mix_sib = [swap(own) for own in mix_own]
    by_core = extended.reshape(-1, dev_count, 2, in_rows)
    ext_own = lax.dynamic_index_in_dim(by_core, core, 2, keepdims=False).reshape(-1, width // 2)
    ext_sib = lax.dynamic_index_in_dim(by_core, 1 - core, 2, keepdims=False).reshape(-1, width // 2)
    if out_rows < 64:
        group = 64 // out_rows
        gathered = jnp.concatenate(
            [
                jnp.concatenate(
                    [
                        part.reshape(-1, group * in_rows, part.shape[-1])
                        for part in (piece[:, :in_rows], piece[:, in_rows:])
                    ],
                    axis=1,
                )
                if split
                else piece.reshape(-1, group * out_rows, piece.shape[-1])
                for piece, split in (
                    (gathered[:, :, :FF], True),
                    (gathered[:, :, FF : FF + 2 * width], False),
                    (gathered[:, :, FF + 2 * width :], True),
                )
            ],
            axis=2,
        )
    split_row = gathered.shape[1] // 2
    mix_gate = jnp.concatenate(
        [
            gathered[:, :split_row, FF + 2 * width :].reshape(width, half_gate),
            gathered[:, split_row:, FF + 2 * width :].reshape(width, half_gate),
        ],
        axis=1,
    )

    projected = jnp.concatenate(
        [
            jnp.dot(ext_own, own, preferred_element_type=jnp.float32)
            + jnp.dot(ext_sib, sib, preferred_element_type=jnp.float32)
            for own, sib in zip(mix_own, mix_sib)
        ],
        axis=1,
    )
    conv_all = projected[:, :CONV_CH]
    attn_cols = projected[:row_count, CONV_CH:]
    q_raw = attn_cols[:, :q_width].reshape(row_count, ATT_HEADS, HEAD_DIM)
    k_raw = attn_cols[:, q_width : q_width + kv_width].reshape(row_count, KV_HEADS, HEAD_DIM)
    v_raw = attn_cols[:, q_width + kv_width :]
    padded = jnp.stack(
        [
            jnp.concatenate(
                [conv_all[row_count : row_count + rim_len], conv_all[:half_rows]], axis=0
            ),
            jnp.concatenate(
                [
                    conv_all[row_count + rim_len : row_count + 2 * rim_len],
                    conv_all[half_rows:row_count],
                ],
                axis=0,
            ),
        ]
    )

    def local_parts(padded_one, step_one):
        x_heads, step_size, decay_rate, b_proj, c_proj = mixer_inputs(
            padded_one, step_one, conv_weight, conv_bias, step_bias, decay_log
        )
        local_out, fresh_state, cumulative = span_local(
            x_heads, step_size, decay_rate, b_proj, c_proj, skip_gain
        )
        return (local_out, fresh_state, cumulative, c_proj)

    local_out, fresh_state, cumulative, c_proj = jax.vmap(local_parts)(padded, step_pair)
    queries = rope_apply(q_raw, local_pos).astype(jnp.bfloat16)
    keys_local = rope_apply(k_raw, local_pos).reshape(row_count, kv_width).astype(jnp.bfloat16)

    def to_slices(states):
        return (
            states.astype(jnp.bfloat16)
            .reshape(2, dev_count, state_rows, STATE)
            .transpose(1, 0, 2, 3)
            .reshape(dev_count, 2 * state_rows, STATE)
        )

    def from_slices(slices):
        return (
            slices.reshape(dev_count, 2, state_rows, STATE)
            .transpose(1, 0, 2, 3)
            .reshape(2, MHEADS, MHEAD_DIM, STATE)
            .astype(jnp.float32)
        )

    kv_local = jnp.concatenate([keys_local, v_raw.astype(jnp.bfloat16)], axis=0)
    fresh_all = exchange(to_slices(fresh_state)).reshape(dev_count, 2, state_rows, STATE)
    kv_all = double(kv_local, high + (1, 0)).reshape(dev_count, 2 * row_count, kv_width)
    all_keys = kv_all[:, :row_count].reshape(-1, kv_width)
    all_values = kv_all[:, row_count:].reshape(-1, kv_width)
    entering = chain_scan(fresh_all, row_decays, False)
    entering, local_out = lax.optimization_barrier((entering, local_out))
    states = from_slices(exchange(entering.reshape(dev_count, 2 * state_rows, STATE)))
    ssm_out = (local_out + jax.vmap(carry_term)(c_proj, cumulative, states)).reshape(
        row_count, INNER
    )
    gate_z = jnp.dot(normed1, mix_gate, preferred_element_type=jnp.float32)
    mamba_part = gated_tail(ssm_out, gate_z, mamba_gain)
    attn_f32, log_total = attention_forward(queries, all_keys, all_values, local_pos, key_pos)
    joined = jnp.concatenate(
        [mamba_part.astype(jnp.bfloat16), attn_f32.astype(jnp.bfloat16)], axis=1
    )
    outputs, grad_middle, grad_joined, gain2_part, bundle = dense_core(
        joined, residual, grad_top, norm_gain2, gathered
    )
    unused_tail, tail_back = jax.vjp(gated_tail, ssm_out, gate_z, mamba_gain)
    grad_ssm, grad_z, mgain_part = tail_back(grad_joined[:, :INNER])
    grad_z = grad_z.astype(jnp.bfloat16)

    def half_grad(values, grads):
        order = ring_order(dev_count)
        made = jnp.dot(
            half_pair(values, dev_count, core),
            both_cores(grads),
            preferred_element_type=jnp.float32,
        ).astype(jnp.bfloat16)
        made = made.reshape(dev_count, -1, grads.shape[1])
        return made[jnp.array(order)] if order != list(range(dev_count)) else made

    if in_rows % 16 == 0:
        bundle_s = swap(bundle)
        norm1_s, joined_s, top_s, grad_z_s = swap(normed1), swap(joined), swap(grad_top_b), swap(grad_z)
        mid_at = 3 * FF + width
        grad_pack = half_grads(
            core,
            dev_count,
            out_rows,
            (
                (
                    (bundle, bundle_s, 3 * FF, width),
                    ((bundle, bundle_s, FF), (bundle, bundle_s, 2 * FF)),
                    FF,
                ),
                ((joined, joined_s, 0, joined.shape[1]), ((bundle, bundle_s, mid_at),), width),
                ((bundle, bundle_s, 0, FF), ((grad_top_b, top_s, 0),), width),
                (
                    (normed1, norm1_s, 0, width),
                    ((grad_z, grad_z_s, 0), (grad_z, grad_z_s, half_gate)),
                    half_gate,
                ),
            ),
        )
    else:
        up_half = half_grad(bundle[:, 3 * FF : 3 * FF + width], bundle[:, FF : 3 * FF])
        gate_half = half_grad(normed1, grad_z)
        grad_pack = jnp.concatenate(
            [
                jnp.concatenate([up_half[:, :, :FF], up_half[:, :, FF:]], axis=1),
                half_grad(joined, bundle[:, 3 * FF + width :]),
                half_grad(bundle[:, :FF], grad_top_b),
                jnp.concatenate(
                    [gate_half[:, :, :half_gate], gate_half[:, :, half_gate:]], axis=1
                ),
            ],
            axis=2,
        )
    grad_pack = grad_pack.reshape(dev_count * out_rows, -1)
    grad_joined, grad_ssm, grad_pack = lax.optimization_barrier((grad_joined, grad_ssm, grad_pack))
    pack_shard = scatter_ring(grad_pack)
    grad_pair = grad_ssm.reshape(2, half_rows, INNER)
    grad_heads = grad_ssm.reshape(2, half_rows, MHEADS, MHEAD_DIM)
    own_grads = jnp.einsum(
        "athp,atn->ahpn",
        grad_heads * jnp.exp(cumulative)[:, :, :, None],
        c_proj,
        precision=HIGHEST,
    )
    grad_attn = grad_joined[:, INNER:].astype(jnp.bfloat16)
    own_slices, grad_attn = lax.optimization_barrier((to_slices(own_grads), grad_attn))
    grad_q, grad_keys, grad_values = attention_backward(
        queries, all_keys, all_values, local_pos, key_pos, log_total, attn_f32, grad_attn
    )
    kv_grads = jnp.concatenate(
        [
            grad_keys.astype(jnp.bfloat16).reshape(dev_count, row_count, kv_width),
            grad_values.astype(jnp.bfloat16).reshape(dev_count, row_count, kv_width),
        ],
        axis=1,
    )
    own_all = exchange(own_slices).reshape(dev_count, 2, state_rows, STATE)
    kv_back = halve(kv_grads, (0, 1) + high)
    keys_back = kv_back[:row_count]
    values_back = kv_back[row_count:]
    leaving = chain_scan(own_all, row_decays, True)
    end_grads = from_slices(exchange(leaving.reshape(dev_count, 2 * state_rows, STATE)))
    unused_q, rope_back_q = jax.vjp(partial(rope_apply, positions=local_pos), q_raw)
    unused_k, rope_back_k = jax.vjp(partial(rope_apply, positions=local_pos), k_raw)
    (grad_q_raw,) = rope_back_q(grad_q)
    (grad_k_raw,) = rope_back_k(keys_back.reshape(row_count, KV_HEADS, HEAD_DIM))
    pair_mixer = jax.vmap(half_mixer, in_axes=(0, 0, None, None, None, None, None, 0))
    unused_m, mixer_back = jax.vjp(
        pair_mixer,
        padded,
        step_pair,
        conv_weight,
        conv_bias,
        step_bias,
        decay_log,
        skip_gain,
        states,
    )
    mixer_grads = mixer_back((grad_pair, end_grads))
    grad_padded = mixer_grads[0]
    grad_rims = grad_padded[:, :rim_len].reshape(2 * rim_len, CONV_CH)
    grad_conv = grad_padded[:, rim_len:].reshape(row_count, CONV_CH)
    grad_proj = jnp.concatenate(
        [
            jnp.concatenate(
                [
                    grad_conv,
                    grad_q_raw.reshape(row_count, q_width),
                    grad_k_raw.reshape(row_count, kv_width),
                    values_back,
                ],
                axis=1,
            ).astype(jnp.bfloat16),
            jnp.pad(
                grad_rims.astype(jnp.bfloat16), ((0, spare), (0, q_width + 2 * kv_width))
            ),
        ],
        axis=0,
    )
    if in_rows % 16 == 0:
        in_half = half_grads(
            core,
            dev_count,
            in_rows,
            (
                (
                    (extended, swap(extended), 0, width),
                    ((grad_proj, swap(grad_proj), 0),),
                    grad_proj.shape[1],
                ),
            ),
        )
    else:
        in_half = half_grad(extended, grad_proj)
    in_half = in_half.reshape(dev_count * in_rows, -1)
    in_half, pack_shard = lax.optimization_barrier((in_half, pack_shard))
    in_shard = scatter_ring(in_half)
    grad_step = mixer_grads[1].reshape(row_count, MHEADS).astype(jnp.bfloat16)
    step_grad = jnp.dot(grad_step.T, normed1, preferred_element_type=jnp.float32)
    ext_halves = [0.0, 0.0]
    for piece, pair in enumerate(zip(mix_own, mix_sib)):
        grads = grad_proj[:, edges[piece] - INNER : edges[piece + 1] - INNER]
        for side, weights in enumerate(pair):
            ext_halves[side] += jnp.dot(grads, weights.T, preferred_element_type=jnp.float32)
    first_core = core == 0
    halves = [half.reshape(-1, dev_count, in_rows) for half in ext_halves]
    grad_ext = jnp.stack(
        [jnp.where(first_core, halves[0], halves[1]), jnp.where(first_core, halves[1], halves[0])],
        axis=2,
    ).reshape(-1, width)
    back_first = grad_ext[row_count : row_count + rim_len]
    back_second = grad_ext[row_count + rim_len : row_count + 2 * rim_len]
    add_first = lax.ppermute(back_first, "ctx", down) + jnp.where(is_last, back_second, 0.0)
    add_second = lax.ppermute(back_second, "ctx", up)
    fill = jnp.zeros((half_rows - rim_len, width), jnp.float32)
    grad_normed1 = (
        grad_ext[:row_count]
        + jnp.concatenate([fill, add_first, fill, add_second], axis=0)
        + jnp.dot(grad_step, step_proj.T, preferred_element_type=jnp.float32)
        + jnp.dot(grad_z, mix_gate.T, preferred_element_type=jnp.float32)
    )
    unused_one, norm_back1 = jax.vjp(rms_scale, residual, norm_gain1)
    grad_res_n, gain1_part = norm_back1(grad_normed1)
    input_grad = grad_middle + grad_res_n
    parts = (
        step_grad,
        mixer_grads[2],
        mixer_grads[3],
        mgain_part,
        gain2_part,
        mixer_grads[4],
        mixer_grads[5],
        mixer_grads[6],
    )
    flat = jnp.concatenate([part.reshape(-1) for part in parts])
    total_len = flat.shape[0]
    summed = butterfly_sum(jnp.pad(flat, (0, -total_len % 1024)).reshape(-1, 128)).reshape(-1)
    sums = [butterfly_sum(gain1_part.reshape(-1, 128)).reshape(-1)]
    start = 0
    for part in parts:
        sums.append(summed[start : start + part.size].reshape(part.shape))
        start += part.size
    pack_f32 = pack_shard.astype(jnp.float32)
    up_shard = jnp.concatenate([pack_f32[:in_rows, :FF], pack_f32[in_rows:, :FF]], axis=1)
    return (
        outputs[None],
        input_grad[None],
        sums[0],
        jnp.concatenate(
            [
                pack_f32[:in_rows, FF + 2 * width :],
                pack_f32[in_rows:, FF + 2 * width :],
                in_shard.astype(jnp.float32),
            ],
            axis=1,
        ),
        sums[1].T,
        sums[2],
        sums[3],
        sums[6],
        sums[7],
        sums[8],
        sums[4],
        pack_f32[:, FF : FF + width],
        sums[5].reshape(-1),
        up_shard,
        pack_f32[:, FF + width : FF + 2 * width],
    )


def solution(mesh):
    return jax.shard_map(
        body,
        mesh=mesh,
        in_specs=(
            P("wsh", "ctx", None),
            P(),
            P(("ctx", "wsh"), None),
            P(),
            P(),
            P(),
            P(),
            P(),
            P(),
            P(),
            P(("ctx", "wsh"), None),
            P(),
            P(("ctx", "wsh"), None),
            P(("ctx", "wsh"), None),
            P("wsh", "ctx", None),
        ),
        out_specs=(
            P("wsh", "ctx", None),
            P("wsh", "ctx", None),
            P(),
            P(("ctx", "wsh"), None),
            P(),
            P(),
            P(),
            P(),
            P(),
            P(),
            P(),
            P(("ctx", "wsh"), None),
            P(),
            P(("ctx", "wsh"), None),
            P(("ctx", "wsh"), None),
        ),
        check_vma=False,
    )
```

```python
from functools import partial

import jax
import jax.numpy as jnp
from jax import lax
from jax.experimental import pallas as pl
from jax.experimental.pallas import tpu as pltpu
from jax.sharding import PartitionSpec as P


MHEADS = 24
MHEAD_DIM = 64
STATE = 128
CONV = 4
ATT_HEADS = 8
KV_HEADS = 2
HEAD_DIM = 64
FF = 2048
INNER = 1536
CONV_CH = 1792


EPSILON = 1e-05
ROPE_BASE = 10000.0
NEG_LARGE = -1e30
HIGHEST = lax.Precision.HIGHEST


def rms_scale(values, gain_vec):
    return (
        values * lax.rsqrt(jnp.mean(values * values, axis=-1, keepdims=True) + EPSILON) * gain_vec
    )


def rope_apply(values, positions):
    half_dim = values.shape[-1] // 2
    frequency = ROPE_BASE ** (-jnp.arange(half_dim, dtype=jnp.float32) / half_dim)
    angles = positions.astype(jnp.float32)[:, None] * frequency[None, :]
    cosine = jnp.cos(angles)[:, None, :]
    sine_v = jnp.sin(angles)[:, None, :]
    first_part = values[..., :half_dim]
    second = values[..., half_dim:]
    return jnp.concatenate(
        [first_part * cosine - second * sine_v, second * cosine + first_part * sine_v], axis=-1
    )


def token_positions(device, dev_count, row_count, row_index):
    half_rows = row_count // 2
    return jnp.where(
        row_index < half_rows,
        device * half_rows + row_index,
        (2 * dev_count - 1 - device) * half_rows + row_index - half_rows,
    )


def conv_silu(padded, conv_weight, conv_bias):
    taps_count = conv_weight.shape[0]
    length = padded.shape[0] - taps_count + 1
    summed = conv_bias[None, :]
    for offset in range(taps_count):
        summed = summed + conv_weight[offset][None, :] * padded[offset : offset + length]
    return jax.nn.silu(summed)


def mixer_inputs(padded, step_raw, conv_weight, conv_bias, step_bias, decay_log):
    conv_act = conv_silu(padded, conv_weight, conv_bias)
    x_heads = conv_act[:, :INNER].reshape(conv_act.shape[0], MHEADS, MHEAD_DIM)
    b_proj = conv_act[:, INNER : INNER + STATE]
    c_proj = conv_act[:, INNER + STATE :]
    step_size = jax.nn.softplus(step_raw + step_bias[None, :])
    decay_rate = -jnp.exp(decay_log)
    return (x_heads, step_size, decay_rate, b_proj, c_proj)


def span_local(x_heads, step_size, decay_rate, b_proj, c_proj, skip_gain):
    length = x_heads.shape[0]
    causal = jnp.arange(length)[:, None] >= jnp.arange(length)[None, :]
    cumulative = jnp.cumsum(step_size * decay_rate[None, :], axis=0)
    log_gap = cumulative[:, None, :] - cumulative[None, :, :]
    causal3 = causal[:, :, None]
    decay_mat = jnp.where(causal3, jnp.exp(jnp.where(causal3, log_gap, 0.0)), 0.0)
    intersection = jnp.dot(c_proj, b_proj.T, precision=HIGHEST)
    weights = decay_mat * intersection[:, :, None] * step_size[None, :, :]
    intra_out = jnp.einsum("tsh,shp->thp", weights, x_heads, precision=HIGHEST)
    local_out = intra_out + skip_gain[None, :, None] * x_heads
    tail_weight = jnp.exp(cumulative[-1][None, :] - cumulative) * step_size
    weighted_x = tail_weight[:, :, None] * x_heads
    fresh_state = jnp.einsum("shp,sn->hpn", weighted_x, b_proj, precision=HIGHEST)
    return (local_out, fresh_state, cumulative)


def carry_term(c_proj, cumulative, state_in):
    return (
        jnp.einsum("tn,hpn->thp", c_proj, state_in, precision=HIGHEST)
        * jnp.exp(cumulative)[:, :, None]
    )


def half_mixer(padded, step_raw, conv_weight, conv_bias, step_bias, decay_log, skip_gain, state_in):
    x_heads, step_size, decay_rate, b_proj, c_proj = mixer_inputs(
        padded, step_raw, conv_weight, conv_bias, step_bias, decay_log
    )
    local_out, fresh_state, cumulative = span_local(
        x_heads, step_size, decay_rate, b_proj, c_proj, skip_gain
    )
    result = local_out + carry_term(c_proj, cumulative, state_in)
    new_state = jnp.exp(cumulative[-1])[:, None, None] * state_in + fresh_state
    return (result.reshape(result.shape[0], INNER), new_state)


def gated_tail(ssm_out, gate_z, mamba_gain):
    return rms_scale(ssm_out * jax.nn.silu(gate_z), mamba_gain)


def score_block(q_groups, query_pos, key_block, pos_block):
    raw_scores = jnp.einsum(
        "tkgd,skd->kgts", q_groups, key_block, preferred_element_type=jnp.float32
    ) * HEAD_DIM ** (-0.5)
    return jnp.where(
        pos_block[None, None, None, :] <= query_pos[None, None, :, None], raw_scores, NEG_LARGE
    )


def split_blocks(all_keys, all_values, key_pos):
    key_count = all_keys.shape[0]
    block_len = min(2048, key_count)
    blocks = key_count // block_len
    return (
        all_keys.reshape(blocks, block_len, KV_HEADS, HEAD_DIM),
        all_values.reshape(blocks, block_len, KV_HEADS, HEAD_DIM),
        key_pos.reshape(blocks, block_len),
    )


def attention_forward(queries, all_keys, all_values, query_pos, key_pos):
    row_count = queries.shape[0]
    group_size = ATT_HEADS // KV_HEADS
    q_groups = queries.reshape(row_count, KV_HEADS, group_size, HEAD_DIM)
    key_blocks, value_blocks, pos_blocks = split_blocks(all_keys, all_values, key_pos)

    def max_step(carried, block_item):
        running_max, running_sum = carried
        scores = score_block(q_groups, query_pos, block_item[0], block_item[1])
        new_max = jnp.maximum(running_max, jnp.max(scores, axis=-1))
        running_sum = running_sum * jnp.exp(running_max - new_max) + jnp.sum(
            jnp.exp(scores - new_max[..., None]), axis=-1
        )
        return ((new_max, running_sum), None)

    start_max = jnp.full((KV_HEADS, group_size, row_count), NEG_LARGE, jnp.float32)
    (final_max, final_sum), unused = lax.scan(
        max_step, (start_max, jnp.zeros_like(start_max)), (key_blocks, pos_blocks)
    )
    log_total = final_max + jnp.log(final_sum)

    def out_step(weighted, block_item):
        scores = score_block(q_groups, query_pos, block_item[0], block_item[2])
        attn_prob = jnp.exp(scores - log_total[..., None]).astype(jnp.bfloat16)
        return (
            weighted
            + jnp.einsum(
                "kgts,skd->tkgd", attn_prob, block_item[1], preferred_element_type=jnp.float32
            ),
            None,
        )

    start_out = jnp.zeros((row_count, KV_HEADS, group_size, HEAD_DIM), jnp.float32)
    weighted, _ = lax.scan(out_step, start_out, (key_blocks, value_blocks, pos_blocks))
    return (weighted.reshape(row_count, ATT_HEADS * HEAD_DIM), log_total)


def attention_backward(
    queries, all_keys, all_values, query_pos, key_pos, log_total, attn_f32, grad_attn
):
    row_count = queries.shape[0]
    key_count = all_keys.shape[0]
    group_size = ATT_HEADS // KV_HEADS
    score_scale = HEAD_DIM ** (-0.5)
    q_groups = queries.reshape(row_count, KV_HEADS, group_size, HEAD_DIM)
    d_groups = grad_attn.reshape(row_count, KV_HEADS, group_size, HEAD_DIM)
    row_dot = jnp.sum(
        (grad_attn.astype(jnp.float32) * attn_f32).reshape(
            row_count, KV_HEADS, group_size, HEAD_DIM
        ),
        axis=-1,
    )
    row_dot = jnp.transpose(row_dot, (1, 2, 0))
    key_blocks, value_blocks, pos_blocks = split_blocks(all_keys, all_values, key_pos)

    def grad_step(grad_q, block_item):
        key_block, value_block, pos_block = block_item
        scores = score_block(q_groups, query_pos, key_block, pos_block)
        attn_prob = jnp.exp(scores - log_total[..., None])
        grad_prob = jnp.einsum(
            "tkgd,skd->kgts", d_groups, value_block, preferred_element_type=jnp.float32
        )
        grad_score = (attn_prob * (grad_prob - row_dot[..., None])).astype(jnp.bfloat16)
        grad_vb = jnp.einsum(
            "kgts,tkgd->skd",
            attn_prob.astype(jnp.bfloat16),
            d_groups,
            preferred_element_type=jnp.float32,
        )
        grad_kb = (
            jnp.einsum("kgts,tkgd->skd", grad_score, q_groups, preferred_element_type=jnp.float32)
            * score_scale
        )
        grad_q = (
            grad_q
            + jnp.einsum(
                "kgts,skd->tkgd", grad_score, key_block, preferred_element_type=jnp.float32
            )
            * score_scale
        )
        return (grad_q, (grad_kb, grad_vb))

    start_q = jnp.zeros((row_count, KV_HEADS, group_size, HEAD_DIM), jnp.float32)
    grad_q, (grad_keys, grad_values) = lax.scan(
        grad_step, start_q, (key_blocks, value_blocks, pos_blocks)
    )
    return (
        grad_q.reshape(row_count, ATT_HEADS, HEAD_DIM),
        grad_keys.reshape(key_count, KV_HEADS * HEAD_DIM),
        grad_values.reshape(key_count, KV_HEADS * HEAD_DIM),
    )


def chain_scan(fresh, decays, reverse):
    dev_count, _, rows, width = fresh.shape
    spans = 2 * dev_count

    def kernel(fresh_ref, decay_ref, out_ref):
        state = jnp.zeros((rows, width), jnp.float32)
        for step in range(spans):
            at = spans - 1 - step if reverse else step
            dev, half = (at, 0) if at < dev_count else (spans - 1 - at, 1)
            out_ref[dev, half] = state.astype(jnp.bfloat16)
            state = decay_ref[:, at : at + 1] * state + fresh_ref[dev, half].astype(jnp.float32)

    return pl.pallas_call(
        kernel, out_shape=jax.ShapeDtypeStruct(fresh.shape, jnp.bfloat16), name="chain_scan"
    )(fresh, decays)


TILE = 512


def ring_order(dev_count):
    if dev_count != 16:
        return list(range(dev_count))
    order = []
    for k, plane in enumerate((0, 1, 3, 2)):
        line = range(4) if k % 2 == 0 else range(3, -1, -1)
        order += [4 * z + plane for z in line]
    return order


def scatter_ring(array):
    order = ring_order(lax.axis_size("ctx"))
    return lax.psum_scatter(
        array, "ctx", scatter_dimension=0, tiled=True, axis_index_groups=[order]
    )


def half_grads(core, dev_count, block_rows, segments):
    order = ring_order(dev_count)
    operands, specs, plan, scratch = [], [], [], []
    start = 0
    for (x_own, x_sib, x_col, x_width), pieces, columns in segments:
        tokens = x_own.shape[0]
        rows = x_width // (2 * dev_count)
        entry = {"rows": rows, "tokens": tokens, "width": x_width, "x": len(operands)}
        for arr in (x_own, x_sib):
            operands.append(arr)
            specs.append(pl.BlockSpec((tokens, x_width), lambda j, c, at=x_col // x_width: (0, at)))
        entry["dy"] = []
        count = pl.cdiv(columns, TILE)
        for d_own, d_sib, d_col in pieces:
            entry["dy"].append(len(operands))
            for arr in (d_own, d_sib):
                operands.append(arr)
                specs.append(
                    pl.BlockSpec(
                        (tokens, TILE),
                        lambda j, c, base=d_col // TILE, first=start, last=count - 1: (
                            0,
                            base + jnp.clip(j - first, 0, last),
                        ),
                    )
                )
        entry["start"], entry["stop"] = start, start + count
        entry["scratch"] = len(scratch)
        scratch += [
            pltpu.VMEM((x_width, 2 * tokens), jnp.bfloat16),
            pltpu.VMEM((x_width // 2, 2 * tokens), jnp.bfloat16),
        ]
        start += count
        plan.append(entry)
    total = start
    width_out = sum(columns for _, _, columns in segments)

    def kernel(core_ref, *refs):
        ins = refs[: len(operands)]
        out_ref = refs[len(operands)]
        spare = refs[len(operands) + 1 :]
        step = pl.program_id(0)
        half = core_ref[0]
        for entry in plan:
            whole, picked = spare[entry["scratch"]], spare[entry["scratch"] + 1]
            rows = entry["rows"]

            @pl.when(step == entry["start"])
            def _():
                both = jnp.concatenate([ins[entry["x"]][...], ins[entry["x"] + 1][...]], axis=0)
                whole[...] = both.T
                for k, dev in enumerate(order):
                    at = pl.multiple_of(2 * dev * rows + half * rows, rows)
                    picked[k * rows : (k + 1) * rows, :] = whole[pl.ds(at, rows), :]

            @pl.when((step >= entry["start"]) & (step < entry["stop"]))
            def _():
                for slot, at in enumerate(entry["dy"]):
                    grads = jnp.concatenate([ins[at][...], ins[at + 1][...]], axis=0)
                    made = jnp.dot(picked[...], grads, preferred_element_type=jnp.float32)
                    out_ref[:, slot * rows : (slot + 1) * rows, :] = made.astype(
                        jnp.bfloat16
                    ).reshape(dev_count, rows, TILE)

    return pl.pallas_call(
        kernel,
        out_shape=jax.ShapeDtypeStruct((dev_count, block_rows, width_out), jnp.bfloat16),
        grid_spec=pltpu.PrefetchScalarGridSpec(
            num_scalar_prefetch=1,
            grid=(total,),
            in_specs=specs,
            out_specs=pl.BlockSpec((dev_count, block_rows, TILE), lambda j, c: (0, 0, j)),
            scratch_shapes=scratch,
        ),
        compiler_params=pltpu.CompilerParams(dimension_semantics=("arbitrary",)),
        name="half_grads",
    )(core.reshape(1), *operands)


def dense_core(joined, residual, grad_top, norm_gain2, gathered):
    tokens, width = residual.shape
    devs, block, _ = gathered.shape
    mixed = devs * block
    in_rows = block // 2
    down_devs = TILE // block
    tiles = FF // TILE
    bundle_width = 3 * FF + 2 * width

    def kernel(
        joined_ref,
        res_ref,
        top_ref,
        gain_ref,
        out_w_ref,
        in_w_ref,
        down_ref,
        outputs_ref,
        grad_mid_ref,
        grad_joined_ref,
        gain_grad_ref,
        bundle_ref,
        middle,
        total,
        grad_norm,
        top_turned,
    ):
        step = pl.program_id(0)

        @pl.when(step == 0)
        def _():
            weights = out_w_ref[...].reshape(mixed, width)
            mid = res_ref[...] + jnp.dot(
                joined_ref[...], weights, preferred_element_type=jnp.float32
            )
            middle[...] = mid
            scale = lax.rsqrt(jnp.mean(mid * mid, axis=-1, keepdims=True) + EPSILON)
            bundle_ref[:, 3 * FF : 3 * FF + width] = (mid * scale * gain_ref[...]).astype(
                jnp.bfloat16
            )
            total[...] = jnp.zeros_like(total)
            grad_norm[...] = jnp.zeros_like(grad_norm)
            top_turned[...] = top_ref[...].T.astype(jnp.bfloat16)

        normed = bundle_ref[:, 3 * FF : 3 * FF + width]
        w_gate = in_w_ref[:, :in_rows, :].reshape(width, TILE)
        w_up = in_w_ref[:, in_rows:, :].reshape(width, TILE)
        w_down = down_ref[...].reshape(TILE, width)
        gate = jnp.dot(normed, w_gate, preferred_element_type=jnp.float32)
        up_part = jnp.dot(normed, w_up, preferred_element_type=jnp.float32)
        sig = jax.nn.sigmoid(gate)
        silu = gate * sig
        activated = (silu * up_part).astype(jnp.bfloat16)
        total[...] += jnp.dot(activated, w_down, preferred_element_type=jnp.float32)
        grad_act = jnp.dot(w_down, top_turned[...], preferred_element_type=jnp.float32).T
        grad_gate = grad_act * up_part * sig * (1.0 + gate * (1.0 - sig))
        grad_up = grad_act * silu
        grad_norm[...] += jnp.dot(
            w_gate, grad_gate.T.astype(jnp.bfloat16), preferred_element_type=jnp.float32
        ) + jnp.dot(w_up, grad_up.T.astype(jnp.bfloat16), preferred_element_type=jnp.float32)
        at = pl.multiple_of(step * TILE, TILE)
        bundle_ref[:, pl.ds(at, TILE)] = activated
        bundle_ref[:, pl.ds(FF + at, TILE)] = grad_gate.astype(jnp.bfloat16)
        bundle_ref[:, pl.ds(2 * FF + at, TILE)] = grad_up.astype(jnp.bfloat16)

        @pl.when(step == tiles - 1)
        def _():
            mid = middle[...]
            outputs_ref[...] = mid + total[...]
            scale = lax.rsqrt(jnp.mean(mid * mid, axis=-1, keepdims=True) + EPSILON)
            unit = mid * scale
            grads = grad_norm[...].T
            gain_grad_ref[...] = jnp.sum(grads * unit, axis=0, keepdims=True)
            scaled = grads * gain_ref[...]
            grad_mid = top_ref[...] + scale * (
                scaled - unit * jnp.mean(scaled * unit, axis=-1, keepdims=True)
            )
            grad_mid_ref[...] = grad_mid
            grad_mid_b = grad_mid.astype(jnp.bfloat16)
            bundle_ref[:, 3 * FF + width :] = grad_mid_b
            grad_joined_ref[...] = jnp.dot(
                out_w_ref[...].reshape(mixed, width),
                grad_mid.T.astype(jnp.bfloat16),
                preferred_element_type=jnp.float32,
            ).T

    def whole(shape):
        return pl.BlockSpec(shape, lambda j: (0,) * len(shape))

    return pl.pallas_call(
        kernel,
        grid=(tiles,),
        out_shape=(
            jax.ShapeDtypeStruct((tokens, width), jnp.float32),
            jax.ShapeDtypeStruct((tokens, width), jnp.float32),
            jax.ShapeDtypeStruct((tokens, mixed), jnp.float32),
            jax.ShapeDtypeStruct((1, width), jnp.float32),
            jax.ShapeDtypeStruct((tokens, bundle_width), jnp.bfloat16),
        ),
        in_specs=[
            whole((tokens, mixed)),
            whole((tokens, width)),
            whole((tokens, width)),
            whole((1, width)),
            pl.BlockSpec((devs, block, width), lambda j: (0, 0, FF // width)),
            pl.BlockSpec((devs, block, TILE), lambda j: (0, 0, j)),
            pl.BlockSpec((down_devs, block, width), lambda j: (j, 0, FF // width + 1)),
        ],
        out_specs=(
            whole((tokens, width)),
            whole((tokens, width)),
            whole((tokens, mixed)),
            whole((1, width)),
            whole((tokens, bundle_width)),
        ),
        scratch_shapes=[
            pltpu.VMEM((tokens, width), jnp.float32),
            pltpu.VMEM((tokens, width), jnp.float32),
            pltpu.VMEM((width, tokens), jnp.float32),
            pltpu.VMEM((width, tokens), jnp.bfloat16),
        ],
        compiler_params=pltpu.CompilerParams(
            dimension_semantics=("arbitrary",), vmem_limit_bytes=40 << 20
        ),
        name="dense_core",
    )(joined, residual, grad_top, norm_gain2.reshape(1, width), gathered, gathered, gathered)


def swap(array):
    return lax.ppermute(array, "wsh", [(0, 1), (1, 0)])


def double_step(block, held, bit):
    size, me = lax.axis_size("ctx"), lax.axis_index("ctx")
    other = lax.ppermute(block, "ctx", [(i, i ^ (1 << bit)) for i in range(size)])
    low = ((me >> bit) & 1) == 0
    held = sorted(held + [bit], reverse=True)
    block = jnp.stack(
        [jnp.where(low, block, other), jnp.where(low, other, block)], axis=held.index(bit)
    )
    return block, held


def double(block, bits):
    held = []
    for bit in bits:
        block, held = double_step(block, held, bit)
    return block.reshape(-1, block.shape[-1])


def halve(blocks, bits):
    size, me = lax.axis_size("ctx"), lax.axis_index("ctx")
    shape = blocks.shape[1:]
    held = list(range(size.bit_length() - 2, -1, -1))
    held = held[: blocks.shape[0].bit_length() - 1]
    blocks = blocks.reshape((2,) * len(held) + shape)
    for bit in bits:
        axis, mine = held.index(bit), (me >> bit) & 1
        sent = lax.dynamic_index_in_dim(blocks, 1 - mine, axis, keepdims=False)
        kept = lax.dynamic_index_in_dim(blocks, mine, axis, keepdims=False)
        other = lax.ppermute(
            sent.astype(jnp.bfloat16), "ctx", [(i, i ^ (1 << bit)) for i in range(size)]
        )
        blocks = kept.astype(jnp.float32) + other.astype(jnp.float32)
        held.remove(bit)
    return blocks


def half_pair(values, dev_count, core):
    tokens, width = values.shape
    blocks = values.T.reshape(dev_count, 2, width // (2 * dev_count), tokens)
    own = lax.dynamic_index_in_dim(blocks, core, 1, keepdims=False)
    other = lax.dynamic_index_in_dim(blocks, 1 - core, 1, keepdims=False)
    joined = jnp.concatenate([own, swap(other)], axis=-1)
    return joined.reshape(width // 2, 2 * tokens)


def both_cores(values):
    return jnp.concatenate([values, swap(values)], axis=0)


def exchange(array):
    return lax.all_to_all(array, "ctx", 0, 0, tiled=True)


def butterfly_sum(array):
    array = array + swap(array)
    size = lax.axis_size("ctx")
    step = 1
    while step < size:
        array = array + lax.ppermute(array, "ctx", [(i, i ^ step) for i in range(size)])
        step *= 2
    return array


def body(
    inputs,
    norm_gain1,
    mix_in,
    step_proj,
    conv_weight,
    conv_bias,
    step_bias,
    decay_log,
    skip_gain,
    mamba_gain,
    mix_out,
    norm_gain2,
    mlp_in,
    mlp_out,
    out_grad,
):
    residual = inputs[0]
    row_count, width = residual.shape
    half_rows = row_count // 2
    rim_len = CONV - 1
    q_width = ATT_HEADS * HEAD_DIM
    kv_width = KV_HEADS * HEAD_DIM
    dev_count = lax.axis_size("ctx")
    device = lax.axis_index("ctx")
    core = lax.axis_index("wsh")
    is_last = device == dev_count - 1
    state_rows = MHEADS * MHEAD_DIM // dev_count
    in_rows = mix_in.shape[0]
    out_rows = mix_out.shape[0]
    up = [(i, i + 1) for i in range(dev_count - 1)]
    down = [(j, i) for i, j in up]
    local_pos = token_positions(
        device, dev_count, row_count, jnp.arange(row_count, dtype=jnp.int32)
    )
    key_ids = jnp.arange(row_count * dev_count, dtype=jnp.int32)
    key_pos = token_positions(key_ids // row_count, dev_count, row_count, key_ids % row_count)
    half_gate = INNER // 2
    packed = jnp.concatenate(
        [
            jnp.concatenate([mlp_in[:, :FF], mlp_in[:, FF:]], axis=0),
            mix_out,
            mlp_out,
            jnp.concatenate([mix_in[:, :half_gate], mix_in[:, half_gate:INNER]], axis=0),
        ],
        axis=1,
    )
    top = dev_count.bit_length() - 1
    high = tuple(range(top - 1, 1, -1))
    edges = (INNER, INNER + 1024, INNER + 2048, mix_in.shape[1])
    orders = (high + (1, 0), (0,) + high + (1,), (1, 0) + high)
    streams = [(mix_in[:, edges[i] : edges[i + 1]], []) for i in range(3)]
    streams = [double_step(*stream, bits[0]) for stream, bits in zip(streams, orders)]
    led, packed = lax.optimization_barrier((streams[0][0], packed))
    gathered = lax.all_gather(packed, ("ctx", "wsh"), axis=0)
    streams[0] = (led, streams[0][1])
    streams = [double_step(*stream, bits[1]) for stream, bits in zip(streams, orders)]

    normed1 = rms_scale(residual, norm_gain1).astype(jnp.bfloat16)
    led, normed1 = lax.optimization_barrier((streams[2][0], normed1))
    streams[2] = (led, streams[2][1])
    for step in range(2, top - 1):
        streams = [double_step(*stream, bits[step]) for stream, bits in zip(streams, orders)]
    tail_first = normed1[half_rows - rim_len : half_rows]
    tail_second = normed1[row_count - rim_len :]
    rim_first = lax.ppermute(tail_first, "ctx", up)
    rim_second = jnp.where(is_last, tail_first, lax.ppermute(tail_second, "ctx", down))
    spare = 16 - 2 * rim_len
    extended = jnp.concatenate(
        [normed1, rim_first, rim_second, jnp.zeros((spare, width), jnp.bfloat16)], axis=0
    )
    step_raw = jnp.dot(normed1, step_proj, preferred_element_type=jnp.float32)
    step_pair = step_raw.reshape(2, half_rows, MHEADS)
    early_steps = jax.nn.softplus(step_pair + step_bias[None, None, :])
    decays = jnp.exp(jnp.sum(early_steps * -jnp.exp(decay_log), axis=1))
    all_decays = exchange(
        jnp.broadcast_to(decays.reshape(1, 2 * MHEADS), (dev_count, 2 * MHEADS))
    ).reshape(dev_count, 2, MHEADS)
    span_decays = jnp.concatenate([all_decays[:, 0], all_decays[::-1, 1]], axis=0)
    row_head = (device * state_rows + jnp.arange(state_rows)) // MHEAD_DIM
    row_pick = (row_head[:, None] == jnp.arange(MHEADS)[None, :]).astype(jnp.float32)
    row_decays = jnp.dot(row_pick, span_decays.T, precision=HIGHEST)
    grad_top = out_grad[0]
    grad_top_b = grad_top.astype(jnp.bfloat16)
    led, extended, row_decays = lax.optimization_barrier((streams[0][0], extended, row_decays))
    streams[0] = (led, streams[0][1])
    streams = [double_step(*stream, bits[top - 1]) for stream, bits in zip(streams, orders)]
    mix_own = [block.reshape(width // 2, -1) for block, _ in streams]
    mix_sib = [swap(own) for own in mix_own]
    by_core = extended.reshape(-1, dev_count, 2, in_rows)
    ext_own = lax.dynamic_index_in_dim(by_core, core, 2, keepdims=False).reshape(-1, width // 2)
    ext_sib = lax.dynamic_index_in_dim(by_core, 1 - core, 2, keepdims=False).reshape(-1, width // 2)
    if out_rows < 64:
        group = 64 // out_rows
        gathered = jnp.concatenate(
            [
                jnp.concatenate(
                    [
                        part.reshape(-1, group * in_rows, part.shape[-1])
                        for part in (piece[:, :in_rows], piece[:, in_rows:])
                    ],
                    axis=1,
                )
                if split
                else piece.reshape(-1, group * out_rows, piece.shape[-1])
                for piece, split in (
                    (gathered[:, :, :FF], True),
                    (gathered[:, :, FF : FF + 2 * width], False),
                    (gathered[:, :, FF + 2 * width :], True),
                )
            ],
            axis=2,
        )
    split_row = gathered.shape[1] // 2
    mix_gate = jnp.concatenate(
        [
            gathered[:, :split_row, FF + 2 * width :].reshape(width, half_gate),
            gathered[:, split_row:, FF + 2 * width :].reshape(width, half_gate),
        ],
        axis=1,
    )

    projected = jnp.concatenate(
        [
            jnp.dot(ext_own, own, preferred_element_type=jnp.float32)
            + jnp.dot(ext_sib, sib, preferred_element_type=jnp.float32)
            for own, sib in zip(mix_own, mix_sib)
        ],
        axis=1,
    )
    conv_all = projected[:, :CONV_CH]
    attn_cols = projected[:row_count, CONV_CH:]
    q_raw = attn_cols[:, :q_width].reshape(row_count, ATT_HEADS, HEAD_DIM)
    k_raw = attn_cols[:, q_width : q_width + kv_width].reshape(row_count, KV_HEADS, HEAD_DIM)
    v_raw = attn_cols[:, q_width + kv_width :]
    padded = jnp.stack(
        [
            jnp.concatenate(
                [conv_all[row_count : row_count + rim_len], conv_all[:half_rows]], axis=0
            ),
            jnp.concatenate(
                [
                    conv_all[row_count + rim_len : row_count + 2 * rim_len],
                    conv_all[half_rows:row_count],
                ],
                axis=0,
            ),
        ]
    )

    def local_parts(padded_one, step_one):
        x_heads, step_size, decay_rate, b_proj, c_proj = mixer_inputs(
            padded_one, step_one, conv_weight, conv_bias, step_bias, decay_log
        )
        local_out, fresh_state, cumulative = span_local(
            x_heads, step_size, decay_rate, b_proj, c_proj, skip_gain
        )
        return (local_out, fresh_state, cumulative, c_proj)

    local_out, fresh_state, cumulative, c_proj = jax.vmap(local_parts)(padded, step_pair)
    queries = rope_apply(q_raw, local_pos).astype(jnp.bfloat16)
    keys_local = rope_apply(k_raw, local_pos).reshape(row_count, kv_width).astype(jnp.bfloat16)

    def to_slices(states):
        return (
            states.astype(jnp.bfloat16)
            .reshape(2, dev_count, state_rows, STATE)
            .transpose(1, 0, 2, 3)
            .reshape(dev_count, 2 * state_rows, STATE)
        )

    def from_slices(slices):
        return (
            slices.reshape(dev_count, 2, state_rows, STATE)
            .transpose(1, 0, 2, 3)
            .reshape(2, MHEADS, MHEAD_DIM, STATE)
            .astype(jnp.float32)
        )

    kv_local = jnp.concatenate([keys_local, v_raw.astype(jnp.bfloat16)], axis=0)
    fresh_slices, kv_local = lax.optimization_barrier((to_slices(fresh_state), kv_local))
    fresh_all = exchange(fresh_slices)
    fresh_all = fresh_all.reshape(dev_count, 2, state_rows, STATE)
    kv_all = double(kv_local, high + (1, 0))
    kv_all = kv_all.reshape(dev_count, 2 * row_count, kv_width)
    all_keys = kv_all[:, :row_count].reshape(-1, kv_width)
    all_values = kv_all[:, row_count:].reshape(-1, kv_width)
    entering = chain_scan(fresh_all, row_decays, False)
    entering, local_out = lax.optimization_barrier((entering, local_out))
    states = from_slices(exchange(entering.reshape(dev_count, 2 * state_rows, STATE)))
    ssm_out = (local_out + jax.vmap(carry_term)(c_proj, cumulative, states)).reshape(
        row_count, INNER
    )
    gate_z = jnp.dot(normed1, mix_gate, preferred_element_type=jnp.float32)
    mamba_part = gated_tail(ssm_out, gate_z, mamba_gain)
    attn_f32, log_total = attention_forward(queries, all_keys, all_values, local_pos, key_pos)
    joined = jnp.concatenate(
        [mamba_part.astype(jnp.bfloat16), attn_f32.astype(jnp.bfloat16)], axis=1
    )
    outputs, grad_middle, grad_joined, gain2_part, bundle = dense_core(
        joined, residual, grad_top, norm_gain2, gathered
    )
    _, tail_back = jax.vjp(gated_tail, ssm_out, gate_z, mamba_gain)
    grad_ssm, grad_z, mgain_part = tail_back(grad_joined[:, :INNER])
    grad_z = grad_z.astype(jnp.bfloat16)

    def half_grad(values, grads):
        order = ring_order(dev_count)
        made = jnp.dot(
            half_pair(values, dev_count, core),
            both_cores(grads),
            preferred_element_type=jnp.float32,
        ).astype(jnp.bfloat16)
        made = made.reshape(dev_count, -1, grads.shape[1])
        return made[jnp.array(order)] if order != list(range(dev_count)) else made

    if in_rows % 16 == 0:
        bundle_s = swap(bundle)
        norm1_s, joined_s, top_s, grad_z_s = swap(normed1), swap(joined), swap(grad_top_b), swap(grad_z)
        mid_at = 3 * FF + width
        grad_pack = half_grads(
            core,
            dev_count,
            out_rows,
            (
                (
                    (bundle, bundle_s, 3 * FF, width),
                    ((bundle, bundle_s, FF), (bundle, bundle_s, 2 * FF)),
                    FF,
                ),
                ((joined, joined_s, 0, joined.shape[1]), ((bundle, bundle_s, mid_at),), width),
                ((bundle, bundle_s, 0, FF), ((grad_top_b, top_s, 0),), width),
                (
                    (normed1, norm1_s, 0, width),
                    (
                        (grad_z[:, :half_gate], grad_z_s[:, :half_gate], 0),
                        (grad_z[:, half_gate:], grad_z_s[:, half_gate:], 0),
                    ),
                    half_gate,
                ),
            ),
        )
    else:
        up_half = half_grad(bundle[:, 3 * FF : 3 * FF + width], bundle[:, FF : 3 * FF])
        gate_half = half_grad(normed1, grad_z)
        grad_pack = jnp.concatenate(
            [
                jnp.concatenate([up_half[:, :, :FF], up_half[:, :, FF:]], axis=1),
                half_grad(joined, bundle[:, 3 * FF + width :]),
                half_grad(bundle[:, :FF], grad_top_b),
                jnp.concatenate(
                    [gate_half[:, :, :half_gate], gate_half[:, :, half_gate:]], axis=1
                ),
            ],
            axis=2,
        )
    grad_pack = grad_pack.reshape(dev_count * out_rows, -1)
    grad_joined, grad_ssm, grad_pack = lax.optimization_barrier((grad_joined, grad_ssm, grad_pack))
    pack_shard = scatter_ring(grad_pack)
    grad_pair = grad_ssm.reshape(2, half_rows, INNER)
    grad_heads = grad_ssm.reshape(2, half_rows, MHEADS, MHEAD_DIM)
    own_grads = jnp.einsum(
        "athp,atn->ahpn",
        grad_heads * jnp.exp(cumulative)[:, :, :, None],
        c_proj,
        precision=HIGHEST,
    )
    grad_attn = grad_joined[:, INNER:].astype(jnp.bfloat16)
    own_slices, grad_attn = lax.optimization_barrier((to_slices(own_grads), grad_attn))
    grad_q, grad_keys, grad_values = attention_backward(
        queries, all_keys, all_values, local_pos, key_pos, log_total, attn_f32, grad_attn
    )
    kv_grads = jnp.concatenate(
        [
            grad_keys.astype(jnp.bfloat16).reshape(dev_count, row_count, kv_width),
            grad_values.astype(jnp.bfloat16).reshape(dev_count, row_count, kv_width),
        ],
        axis=1,
    )
    own_all = exchange(own_slices).reshape(dev_count, 2, state_rows, STATE)
    leaving = chain_scan(own_all, row_decays, True)
    kv_held = halve(kv_grads, (0, 1))
    end_slices = exchange(leaving.reshape(dev_count, 2 * state_rows, STATE))
    end_slices, kv_held = lax.optimization_barrier((end_slices, kv_held))
    end_grads = from_slices(end_slices)
    kv_back = halve(kv_held.reshape(dev_count // 4, 2 * row_count, kv_width), high)
    keys_back = kv_back[:row_count]
    values_back = kv_back[row_count:]
    _, rope_back_q = jax.vjp(partial(rope_apply, positions=local_pos), q_raw)
    _, rope_back_k = jax.vjp(partial(rope_apply, positions=local_pos), k_raw)
    (grad_q_raw,) = rope_back_q(grad_q)
    (grad_k_raw,) = rope_back_k(keys_back.reshape(row_count, KV_HEADS, HEAD_DIM))
    pair_mixer = jax.vmap(half_mixer, in_axes=(0, 0, None, None, None, None, None, 0))
    _, mixer_back = jax.vjp(
        pair_mixer,
        padded,
        step_pair,
        conv_weight,
        conv_bias,
        step_bias,
        decay_log,
        skip_gain,
        states,
    )
    mixer_grads = mixer_back((grad_pair, end_grads))
    grad_padded = mixer_grads[0]
    grad_rims = grad_padded[:, :rim_len].reshape(2 * rim_len, CONV_CH)

    def to_width(grads):
        sides = [0.0, 0.0]
        for piece, pair in enumerate(zip(mix_own, mix_sib)):
            low = edges[piece] - INNER
            part = grads[:, low : low + pair[0].shape[1]]
            if part.shape[1] == 0:
                continue
            for side, weights in enumerate(pair):
                sides[side] += jnp.dot(
                    part, weights[:, : part.shape[1]].T, preferred_element_type=jnp.float32
                )
        first_core = core == 0
        sides = [side.reshape(-1, dev_count, in_rows) for side in sides]
        return jnp.stack(
            [jnp.where(first_core, sides[0], sides[1]), jnp.where(first_core, sides[1], sides[0])],
            axis=2,
        ).reshape(-1, width)

    rims_b = jnp.pad(grad_rims.astype(jnp.bfloat16), ((0, spare), (0, 0)))
    rim_back = to_width(rims_b)
    back_first = rim_back[:rim_len]
    back_second = rim_back[rim_len : 2 * rim_len]
    add_first = lax.ppermute(back_first, "ctx", down) + jnp.where(is_last, back_second, 0.0)
    add_second = lax.ppermute(back_second, "ctx", up)
    grad_conv = grad_padded[:, rim_len:].reshape(row_count, CONV_CH)
    grad_proj = jnp.concatenate(
        [
            jnp.concatenate(
                [
                    grad_conv,
                    grad_q_raw.reshape(row_count, q_width),
                    grad_k_raw.reshape(row_count, kv_width),
                    values_back,
                ],
                axis=1,
            ).astype(jnp.bfloat16),
            jnp.pad(rims_b, ((0, 0), (0, q_width + 2 * kv_width))),
        ],
        axis=0,
    )
    if in_rows % 16 == 0:
        in_half = half_grads(
            core,
            dev_count,
            in_rows,
            (
                (
                    (extended, swap(extended), 0, width),
                    ((grad_proj, swap(grad_proj), 0),),
                    grad_proj.shape[1],
                ),
            ),
        )
    else:
        in_half = half_grad(extended, grad_proj)
    in_half = in_half.reshape(dev_count * in_rows, -1)
    in_half, pack_shard = lax.optimization_barrier((in_half, pack_shard))
    in_shard = scatter_ring(in_half)
    grad_step = mixer_grads[1].reshape(row_count, MHEADS).astype(jnp.bfloat16)
    step_grad = jnp.dot(grad_step.T, normed1, preferred_element_type=jnp.float32)
    grad_main = to_width(grad_proj[:row_count])
    fill = jnp.zeros((half_rows - rim_len, width), jnp.float32)
    grad_normed1 = (
        grad_main
        + jnp.concatenate([fill, add_first, fill, add_second], axis=0)
        + jnp.dot(grad_step, step_proj.T, preferred_element_type=jnp.float32)
        + jnp.dot(grad_z, mix_gate.T, preferred_element_type=jnp.float32)
    )
    _, norm_back1 = jax.vjp(rms_scale, residual, norm_gain1)
    grad_res_n, gain1_part = norm_back1(grad_normed1)
    input_grad = grad_middle + grad_res_n
    parts = (
        step_grad,
        mixer_grads[2],
        mixer_grads[3],
        mgain_part,
        gain2_part,
        mixer_grads[4],
        mixer_grads[5],
        mixer_grads[6],
        gain1_part,
    )
    flat = jnp.concatenate([part.reshape(-1) for part in parts])
    total_len = flat.shape[0]
    summed = butterfly_sum(jnp.pad(flat, (0, -total_len % 1024)).reshape(-1, 128)).reshape(-1)
    sums = []
    start = 0
    for part in parts:
        sums.append(summed[start : start + part.size].reshape(part.shape))
        start += part.size
    sums = [sums.pop()] + sums
    pack_f32 = pack_shard.astype(jnp.float32)
    up_shard = jnp.concatenate([pack_f32[:in_rows, :FF], pack_f32[in_rows:, :FF]], axis=1)
    return (
        outputs[None],
        input_grad[None],
        sums[0],
        jnp.concatenate(
            [
                pack_f32[:in_rows, FF + 2 * width :],
                pack_f32[in_rows:, FF + 2 * width :],
                in_shard.astype(jnp.float32),
            ],
            axis=1,
        ),
        sums[1].T,
        sums[2],
        sums[3],
        sums[6],
        sums[7],
        sums[8],
        sums[4],
        pack_f32[:, FF : FF + width],
        sums[5].reshape(-1),
        up_shard,
        pack_f32[:, FF + width : FF + 2 * width],
    )


def solution(mesh):
    return jax.shard_map(
        body,
        mesh=mesh,
        in_specs=(
            P("wsh", "ctx", None),
            P(),
            P(("ctx", "wsh"), None),
            P(),
            P(),
            P(),
            P(),
            P(),
            P(),
            P(),
            P(("ctx", "wsh"), None),
            P(),
            P(("ctx", "wsh"), None),
            P(("ctx", "wsh"), None),
            P("wsh", "ctx", None),
        ),
        out_specs=(
            P("wsh", "ctx", None),
            P("wsh", "ctx", None),
            P(),
            P(("ctx", "wsh"), None),
            P(),
            P(),
            P(),
            P(),
            P(),
            P(),
            P(),
            P(("ctx", "wsh"), None),
            P(),
            P(("ctx", "wsh"), None),
            P(("ctx", "wsh"), None),
        ),
        check_vma=False,
    )
```

```python
from functools import partial

import jax
import jax.numpy as jnp
from jax import lax
from jax.experimental import pallas as pl
from jax.experimental.pallas import tpu as pltpu
from jax.sharding import PartitionSpec as P

MHEADS = 24
MHEAD_DIM = 64
STATE = 128
CONV = 4
ATT_HEADS = 8
KV_HEADS = 2
HEAD_DIM = 64
FF = 2048
INNER = 1536
CONV_CH = 1792


EPSILON = 1e-05
ROPE_BASE = 10000.0
NEG_LARGE = -1e30
HIGHEST = lax.Precision.HIGHEST


def rms_scale(values, gain_vec):
    return (
        values * lax.rsqrt(jnp.mean(values * values, axis=-1, keepdims=True) + EPSILON) * gain_vec
    )


def rope_apply(values, positions):
    half_dim = values.shape[-1] // 2
    frequency = ROPE_BASE ** (-jnp.arange(half_dim, dtype=jnp.float32) / half_dim)
    angles = positions.astype(jnp.float32)[:, None] * frequency[None, :]
    cosine = jnp.cos(angles)[:, None, :]
    sine_v = jnp.sin(angles)[:, None, :]
    first_part = values[..., :half_dim]
    second = values[..., half_dim:]
    return jnp.concatenate(
        [first_part * cosine - second * sine_v, second * cosine + first_part * sine_v], axis=-1
    )


def token_positions(device, dev_count, row_count, row_index):
    half_rows = row_count // 2
    return jnp.where(
        row_index < half_rows,
        device * half_rows + row_index,
        (2 * dev_count - 1 - device) * half_rows + row_index - half_rows,
    )


def conv_silu(padded, conv_weight, conv_bias):
    taps_count = conv_weight.shape[0]
    length = padded.shape[0] - taps_count + 1
    summed = conv_bias[None, :]
    for offset in range(taps_count):
        summed = summed + conv_weight[offset][None, :] * padded[offset : offset + length]
    return jax.nn.silu(summed)


def mixer_inputs(padded, step_raw, conv_weight, conv_bias, step_bias, decay_log):
    conv_act = conv_silu(padded, conv_weight, conv_bias)
    x_heads = conv_act[:, :INNER].reshape(conv_act.shape[0], MHEADS, MHEAD_DIM)
    b_proj = conv_act[:, INNER : INNER + STATE]
    c_proj = conv_act[:, INNER + STATE :]
    step_size = jax.nn.softplus(step_raw + step_bias[None, :])
    decay_rate = -jnp.exp(decay_log)
    return (x_heads, step_size, decay_rate, b_proj, c_proj)


def span_local(x_heads, step_size, decay_rate, b_proj, c_proj, skip_gain):
    length = x_heads.shape[0]
    causal = jnp.arange(length)[:, None] >= jnp.arange(length)[None, :]
    cumulative = jnp.cumsum(step_size * decay_rate[None, :], axis=0)
    log_gap = cumulative[:, None, :] - cumulative[None, :, :]
    causal3 = causal[:, :, None]
    decay_mat = jnp.where(causal3, jnp.exp(jnp.where(causal3, log_gap, 0.0)), 0.0)
    intersection = jnp.dot(c_proj, b_proj.T, precision=HIGHEST)
    weights = decay_mat * intersection[:, :, None] * step_size[None, :, :]
    intra_out = jnp.einsum("tsh,shp->thp", weights, x_heads, precision=HIGHEST)
    local_out = intra_out + skip_gain[None, :, None] * x_heads
    tail_weight = jnp.exp(cumulative[-1][None, :] - cumulative) * step_size
    weighted_x = tail_weight[:, :, None] * x_heads
    fresh_state = jnp.einsum("shp,sn->hpn", weighted_x, b_proj, precision=HIGHEST)
    return (local_out, fresh_state, cumulative)


def carry_term(c_proj, cumulative, state_in):
    return (
        jnp.einsum("tn,hpn->thp", c_proj, state_in, precision=HIGHEST)
        * jnp.exp(cumulative)[:, :, None]
    )


def half_mixer(padded, step_raw, conv_weight, conv_bias, step_bias, decay_log, skip_gain, state_in):
    x_heads, step_size, decay_rate, b_proj, c_proj = mixer_inputs(
        padded, step_raw, conv_weight, conv_bias, step_bias, decay_log
    )
    local_out, fresh_state, cumulative = span_local(
        x_heads, step_size, decay_rate, b_proj, c_proj, skip_gain
    )
    result = local_out + carry_term(c_proj, cumulative, state_in)
    new_state = jnp.exp(cumulative[-1])[:, None, None] * state_in + fresh_state
    return (result.reshape(result.shape[0], INNER), new_state)


def gated_tail(ssm_out, gate_z, mamba_gain):
    return rms_scale(ssm_out * jax.nn.silu(gate_z), mamba_gain)


def score_block(q_groups, query_pos, key_block, pos_block):
    raw_scores = jnp.einsum(
        "tkgd,skd->kgts", q_groups, key_block, preferred_element_type=jnp.float32
    ) * HEAD_DIM ** (-0.5)
    return jnp.where(
        pos_block[None, None, None, :] <= query_pos[None, None, :, None], raw_scores, NEG_LARGE
    )


def split_blocks(all_keys, all_values, key_pos):
    key_count = all_keys.shape[0]
    block_len = min(2048, key_count)
    blocks = key_count // block_len
    return (
        all_keys.reshape(blocks, block_len, KV_HEADS, HEAD_DIM),
        all_values.reshape(blocks, block_len, KV_HEADS, HEAD_DIM),
        key_pos.reshape(blocks, block_len),
    )


def attention_forward(queries, all_keys, all_values, query_pos, key_pos):
    row_count = queries.shape[0]
    group_size = ATT_HEADS // KV_HEADS
    q_groups = queries.reshape(row_count, KV_HEADS, group_size, HEAD_DIM)
    key_blocks, value_blocks, pos_blocks = split_blocks(all_keys, all_values, key_pos)

    def max_step(carried, block_item):
        running_max, running_sum = carried
        scores = score_block(q_groups, query_pos, block_item[0], block_item[1])
        new_max = jnp.maximum(running_max, jnp.max(scores, axis=-1))
        running_sum = running_sum * jnp.exp(running_max - new_max) + jnp.sum(
            jnp.exp(scores - new_max[..., None]), axis=-1
        )
        return ((new_max, running_sum), None)

    start_max = jnp.full((KV_HEADS, group_size, row_count), NEG_LARGE, jnp.float32)
    (final_max, final_sum), unused = lax.scan(
        max_step, (start_max, jnp.zeros_like(start_max)), (key_blocks, pos_blocks)
    )
    log_total = final_max + jnp.log(final_sum)

    def out_step(weighted, block_item):
        scores = score_block(q_groups, query_pos, block_item[0], block_item[2])
        attn_prob = jnp.exp(scores - log_total[..., None]).astype(jnp.bfloat16)
        return (
            weighted
            + jnp.einsum(
                "kgts,skd->tkgd", attn_prob, block_item[1], preferred_element_type=jnp.float32
            ),
            None,
        )

    start_out = jnp.zeros((row_count, KV_HEADS, group_size, HEAD_DIM), jnp.float32)
    weighted, unused_two = lax.scan(out_step, start_out, (key_blocks, value_blocks, pos_blocks))
    return (weighted.reshape(row_count, ATT_HEADS * HEAD_DIM), log_total)


def attention_backward(
    queries, all_keys, all_values, query_pos, key_pos, log_total, attn_f32, grad_attn
):
    row_count = queries.shape[0]
    key_count = all_keys.shape[0]
    group_size = ATT_HEADS // KV_HEADS
    score_scale = HEAD_DIM ** (-0.5)
    q_groups = queries.reshape(row_count, KV_HEADS, group_size, HEAD_DIM)
    d_groups = grad_attn.reshape(row_count, KV_HEADS, group_size, HEAD_DIM)
    row_dot = jnp.sum(
        (grad_attn.astype(jnp.float32) * attn_f32).reshape(
            row_count, KV_HEADS, group_size, HEAD_DIM
        ),
        axis=-1,
    )
    row_dot = jnp.transpose(row_dot, (1, 2, 0))
    key_blocks, value_blocks, pos_blocks = split_blocks(all_keys, all_values, key_pos)

    def grad_step(grad_q, block_item):
        key_block, value_block, pos_block = block_item
        scores = score_block(q_groups, query_pos, key_block, pos_block)
        attn_prob = jnp.exp(scores - log_total[..., None])
        grad_prob = jnp.einsum(
            "tkgd,skd->kgts", d_groups, value_block, preferred_element_type=jnp.float32
        )
        grad_score = (attn_prob * (grad_prob - row_dot[..., None])).astype(jnp.bfloat16)
        grad_vb = jnp.einsum(
            "kgts,tkgd->skd",
            attn_prob.astype(jnp.bfloat16),
            d_groups,
            preferred_element_type=jnp.float32,
        )
        grad_kb = (
            jnp.einsum("kgts,tkgd->skd", grad_score, q_groups, preferred_element_type=jnp.float32)
            * score_scale
        )
        grad_q = (
            grad_q
            + jnp.einsum(
                "kgts,skd->tkgd", grad_score, key_block, preferred_element_type=jnp.float32
            )
            * score_scale
        )
        return (grad_q, (grad_kb, grad_vb))

    start_q = jnp.zeros((row_count, KV_HEADS, group_size, HEAD_DIM), jnp.float32)
    grad_q, (grad_keys, grad_values) = lax.scan(
        grad_step, start_q, (key_blocks, value_blocks, pos_blocks)
    )
    return (
        grad_q.reshape(row_count, ATT_HEADS, HEAD_DIM),
        grad_keys.reshape(key_count, KV_HEADS * HEAD_DIM),
        grad_values.reshape(key_count, KV_HEADS * HEAD_DIM),
    )


def chain_scan(fresh, decays, reverse):
    dev_count, _, rows, width = fresh.shape
    spans = 2 * dev_count

    def kernel(fresh_ref, decay_ref, out_ref):
        state = jnp.zeros((rows, width), jnp.float32)
        for step in range(spans):
            at = spans - 1 - step if reverse else step
            dev, half = (at, 0) if at < dev_count else (spans - 1 - at, 1)
            out_ref[dev, half] = state.astype(jnp.bfloat16)
            state = decay_ref[:, at : at + 1] * state + fresh_ref[dev, half].astype(jnp.float32)

    return pl.pallas_call(
        kernel, out_shape=jax.ShapeDtypeStruct(fresh.shape, jnp.bfloat16), name="chain_scan"
    )(fresh, decays)


TILE = 512


def ring_order(dev_count):
    if dev_count != 16:
        return list(range(dev_count))
    order = []
    for k, plane in enumerate((0, 1, 3, 2)):
        line = range(4) if k % 2 == 0 else range(3, -1, -1)
        order += [4 * z + plane for z in line]
    return order


def scatter_ring(array):
    order = ring_order(lax.axis_size("ctx"))
    return lax.psum_scatter(
        array, "ctx", scatter_dimension=0, tiled=True, axis_index_groups=[order]
    )


def half_grads(core, dev_count, block_rows, segments):
    order = ring_order(dev_count)
    operands, specs, plan, scratch = [], [], [], []
    start = 0
    for (x_own, x_sib, x_col, x_width), pieces, columns in segments:
        tokens = x_own.shape[0]
        rows = x_width // (2 * dev_count)
        entry = {"rows": rows, "tokens": tokens, "width": x_width, "x": len(operands)}
        for arr in (x_own, x_sib):
            operands.append(arr)
            specs.append(pl.BlockSpec((tokens, x_width), lambda j, c, at=x_col // x_width: (0, at)))
        entry["dy"] = []
        count = pl.cdiv(columns, TILE)
        for d_own, d_sib, d_col in pieces:
            entry["dy"].append(len(operands))
            for arr in (d_own, d_sib):
                operands.append(arr)
                specs.append(
                    pl.BlockSpec(
                        (tokens, TILE),
                        lambda j, c, base=d_col // TILE, first=start, last=count - 1: (
                            0,
                            base + jnp.clip(j - first, 0, last),
                        ),
                    )
                )
        entry["start"], entry["stop"] = start, start + count
        entry["scratch"] = len(scratch)
        scratch += [
            pltpu.VMEM((x_width, 2 * tokens), jnp.bfloat16),
            pltpu.VMEM((x_width // 2, 2 * tokens), jnp.bfloat16),
        ]
        start += count
        plan.append(entry)
    total = start
    width_out = sum(columns for _, _, columns in segments)

    def kernel(core_ref, *refs):
        ins = refs[: len(operands)]
        out_ref = refs[len(operands)]
        spare = refs[len(operands) + 1 :]
        step = pl.program_id(0)
        half = core_ref[0]
        for entry in plan:
            whole, picked = spare[entry["scratch"]], spare[entry["scratch"] + 1]
            rows = entry["rows"]

            @pl.when(step == entry["start"])
            def _():
                both = jnp.concatenate([ins[entry["x"]][...], ins[entry["x"] + 1][...]], axis=0)
                whole[...] = both.T
                for k, dev in enumerate(order):
                    at = pl.multiple_of(2 * dev * rows + half * rows, rows)
                    picked[k * rows : (k + 1) * rows, :] = whole[pl.ds(at, rows), :]

            @pl.when((step >= entry["start"]) & (step < entry["stop"]))
            def _():
                for slot, at in enumerate(entry["dy"]):
                    grads = jnp.concatenate([ins[at][...], ins[at + 1][...]], axis=0)
                    made = jnp.dot(picked[...], grads, preferred_element_type=jnp.float32)
                    out_ref[:, slot * rows : (slot + 1) * rows, :] = made.astype(
                        jnp.bfloat16
                    ).reshape(dev_count, rows, TILE)

    return pl.pallas_call(
        kernel,
        out_shape=jax.ShapeDtypeStruct((dev_count, block_rows, width_out), jnp.bfloat16),
        grid_spec=pltpu.PrefetchScalarGridSpec(
            num_scalar_prefetch=1,
            grid=(total,),
            in_specs=specs,
            out_specs=pl.BlockSpec((dev_count, block_rows, TILE), lambda j, c: (0, 0, j)),
            scratch_shapes=scratch,
        ),
        compiler_params=pltpu.CompilerParams(
            dimension_semantics=("arbitrary",), vmem_limit_bytes=32 << 20
        ),
        name="half_grads",
    )(core.reshape(1), *operands)


def dense_core(joined, residual, grad_top, norm_gain2, gathered):
    tokens, width = residual.shape
    devs, block, _ = gathered.shape
    mixed = devs * block
    in_rows = block // 2
    down_devs = TILE // block
    tiles = FF // TILE
    bundle_width = 3 * FF + 2 * width

    def kernel(
        joined_ref,
        res_ref,
        top_ref,
        gain_ref,
        out_w_ref,
        in_w_ref,
        down_ref,
        outputs_ref,
        grad_mid_ref,
        grad_joined_ref,
        gain_grad_ref,
        bundle_ref,
        middle,
        total,
        grad_norm,
        top_turned,
    ):
        step = pl.program_id(0)

        @pl.when(step == 0)
        def _():
            weights = out_w_ref[...].reshape(mixed, width)
            mid = res_ref[...] + jnp.dot(
                joined_ref[...], weights, preferred_element_type=jnp.float32
            )
            middle[...] = mid
            scale = lax.rsqrt(jnp.mean(mid * mid, axis=-1, keepdims=True) + EPSILON)
            bundle_ref[:, 3 * FF : 3 * FF + width] = (mid * scale * gain_ref[...]).astype(
                jnp.bfloat16
            )
            total[...] = jnp.zeros_like(total)
            grad_norm[...] = jnp.zeros_like(grad_norm)
            top_turned[...] = top_ref[...].T.astype(jnp.bfloat16)

        normed = bundle_ref[:, 3 * FF : 3 * FF + width]
        w_gate = in_w_ref[:, :in_rows, :].reshape(width, TILE)
        w_up = in_w_ref[:, in_rows:, :].reshape(width, TILE)
        w_down = down_ref[...].reshape(TILE, width)
        gate = jnp.dot(normed, w_gate, preferred_element_type=jnp.float32)
        up_part = jnp.dot(normed, w_up, preferred_element_type=jnp.float32)
        sig = jax.nn.sigmoid(gate)
        silu = gate * sig
        activated = (silu * up_part).astype(jnp.bfloat16)
        total[...] += jnp.dot(activated, w_down, preferred_element_type=jnp.float32)
        grad_act = jnp.dot(w_down, top_turned[...], preferred_element_type=jnp.float32).T
        grad_gate = grad_act * up_part * sig * (1.0 + gate * (1.0 - sig))
        grad_up = grad_act * silu
        grad_norm[...] += jnp.dot(
            w_gate, grad_gate.T.astype(jnp.bfloat16), preferred_element_type=jnp.float32
        ) + jnp.dot(w_up, grad_up.T.astype(jnp.bfloat16), preferred_element_type=jnp.float32)
        at = pl.multiple_of(step * TILE, TILE)
        bundle_ref[:, pl.ds(at, TILE)] = activated
        bundle_ref[:, pl.ds(FF + at, TILE)] = grad_gate.astype(jnp.bfloat16)
        bundle_ref[:, pl.ds(2 * FF + at, TILE)] = grad_up.astype(jnp.bfloat16)

        @pl.when(step == tiles - 1)
        def _():
            mid = middle[...]
            outputs_ref[...] = mid + total[...]
            scale = lax.rsqrt(jnp.mean(mid * mid, axis=-1, keepdims=True) + EPSILON)
            unit = mid * scale
            grads = grad_norm[...].T
            gain_grad_ref[...] = jnp.sum(grads * unit, axis=0, keepdims=True)
            scaled = grads * gain_ref[...]
            grad_mid = top_ref[...] + scale * (
                scaled - unit * jnp.mean(scaled * unit, axis=-1, keepdims=True)
            )
            grad_mid_ref[...] = grad_mid
            grad_mid_b = grad_mid.astype(jnp.bfloat16)
            bundle_ref[:, 3 * FF + width :] = grad_mid_b
            grad_joined_ref[...] = jnp.dot(
                out_w_ref[...].reshape(mixed, width),
                grad_mid.T.astype(jnp.bfloat16),
                preferred_element_type=jnp.float32,
            ).T

    def whole(shape):
        return pl.BlockSpec(shape, lambda j: (0,) * len(shape))

    return pl.pallas_call(
        kernel,
        grid=(tiles,),
        out_shape=(
            jax.ShapeDtypeStruct((tokens, width), jnp.float32),
            jax.ShapeDtypeStruct((tokens, width), jnp.float32),
            jax.ShapeDtypeStruct((tokens, mixed), jnp.float32),
            jax.ShapeDtypeStruct((1, width), jnp.float32),
            jax.ShapeDtypeStruct((tokens, bundle_width), jnp.bfloat16),
        ),
        in_specs=[
            whole((tokens, mixed)),
            whole((tokens, width)),
            whole((tokens, width)),
            whole((1, width)),
            pl.BlockSpec((devs, block, width), lambda j: (0, 0, FF // width)),
            pl.BlockSpec((devs, block, TILE), lambda j: (0, 0, j)),
            pl.BlockSpec((down_devs, block, width), lambda j: (j, 0, FF // width + 1)),
        ],
        out_specs=(
            whole((tokens, width)),
            whole((tokens, width)),
            whole((tokens, mixed)),
            whole((1, width)),
            whole((tokens, bundle_width)),
        ),
        scratch_shapes=[
            pltpu.VMEM((tokens, width), jnp.float32),
            pltpu.VMEM((tokens, width), jnp.float32),
            pltpu.VMEM((width, tokens), jnp.float32),
            pltpu.VMEM((width, tokens), jnp.bfloat16),
        ],
        compiler_params=pltpu.CompilerParams(
            dimension_semantics=("arbitrary",), vmem_limit_bytes=36 << 20
        ),
        name="dense_core",
    )(joined, residual, grad_top, norm_gain2.reshape(1, width), gathered, gathered, gathered)


def swap(array):
    return lax.ppermute(array, "wsh", [(0, 1), (1, 0)])


def double_step(block, held, bit):
    size, me = lax.axis_size("ctx"), lax.axis_index("ctx")
    other = lax.ppermute(block, "ctx", [(i, i ^ (1 << bit)) for i in range(size)])
    low = ((me >> bit) & 1) == 0
    held = sorted(held + [bit], reverse=True)
    block = jnp.stack(
        [jnp.where(low, block, other), jnp.where(low, other, block)], axis=held.index(bit)
    )
    return block, held


def double(block, bits):
    held = []
    for bit in bits:
        block, held = double_step(block, held, bit)
    return block.reshape(-1, block.shape[-1])


def halve(blocks, bits):
    size, me = lax.axis_size("ctx"), lax.axis_index("ctx")
    shape = blocks.shape[1:]
    held = list(range(size.bit_length() - 2, -1, -1))
    held = held[: blocks.shape[0].bit_length() - 1]
    blocks = blocks.reshape((2,) * len(held) + shape)
    for bit in bits:
        axis, mine = held.index(bit), (me >> bit) & 1
        sent = lax.dynamic_index_in_dim(blocks, 1 - mine, axis, keepdims=False)
        kept = lax.dynamic_index_in_dim(blocks, mine, axis, keepdims=False)
        other = lax.ppermute(
            sent.astype(jnp.bfloat16), "ctx", [(i, i ^ (1 << bit)) for i in range(size)]
        )
        blocks = kept.astype(jnp.float32) + other.astype(jnp.float32)
        held.remove(bit)
    return blocks


def half_pair(values, dev_count, core):
    tokens, width = values.shape
    blocks = values.T.reshape(dev_count, 2, width // (2 * dev_count), tokens)
    own = lax.dynamic_index_in_dim(blocks, core, 1, keepdims=False)
    other = lax.dynamic_index_in_dim(blocks, 1 - core, 1, keepdims=False)
    joined = jnp.concatenate([own, swap(other)], axis=-1)
    return joined.reshape(width // 2, 2 * tokens)


def both_cores(values):
    return jnp.concatenate([values, swap(values)], axis=0)


def exchange(array):
    return lax.all_to_all(array, "ctx", 0, 0, tiled=True)


def butterfly_sum(array):
    array = array + swap(array)
    size = lax.axis_size("ctx")
    step = 1
    while step < size:
        array = array + lax.ppermute(array, "ctx", [(i, i ^ step) for i in range(size)])
        step *= 2
    return array


def body(
    inputs,
    norm_gain1,
    mix_in,
    step_proj,
    conv_weight,
    conv_bias,
    step_bias,
    decay_log,
    skip_gain,
    mamba_gain,
    mix_out,
    norm_gain2,
    mlp_in,
    mlp_out,
    out_grad,
):
    residual = inputs[0]
    row_count, width = residual.shape
    half_rows = row_count // 2
    rim_len = CONV - 1
    q_width = ATT_HEADS * HEAD_DIM
    kv_width = KV_HEADS * HEAD_DIM
    dev_count = lax.axis_size("ctx")
    device = lax.axis_index("ctx")
    core = lax.axis_index("wsh")
    is_last = device == dev_count - 1
    state_rows = MHEADS * MHEAD_DIM // dev_count
    in_rows = mix_in.shape[0]
    out_rows = mix_out.shape[0]
    up = [(i, i + 1) for i in range(dev_count - 1)]
    down = [(j, i) for i, j in up]
    local_pos = token_positions(
        device, dev_count, row_count, jnp.arange(row_count, dtype=jnp.int32)
    )
    key_ids = jnp.arange(row_count * dev_count, dtype=jnp.int32)
    key_pos = token_positions(key_ids // row_count, dev_count, row_count, key_ids % row_count)
    half_gate = INNER // 2
    packed = jnp.concatenate(
        [
            jnp.concatenate([mlp_in[:, :FF], mlp_in[:, FF:]], axis=0),
            mix_out,
            mlp_out,
            jnp.concatenate([mix_in[:, :half_gate], mix_in[:, half_gate:INNER]], axis=0),
        ],
        axis=1,
    )
    top = dev_count.bit_length() - 1
    high = tuple(range(top - 1, 1, -1))
    split = (CONV_CH + q_width) // 2
    edges = (INNER, INNER + split, INNER + 2 * split, mix_in.shape[1])
    orders = (high + (1, 0), (0,) + high + (1,), (1, 0) + high)
    streams = [(mix_in[:, edges[i] : edges[i + 1]], []) for i in range(3)]
    streams = [double_step(*stream, bits[0]) for stream, bits in zip(streams, orders)]
    led, packed = lax.optimization_barrier((streams[0][0], packed))
    gathered = lax.all_gather(packed, ("ctx", "wsh"), axis=0)
    streams[0] = (led, streams[0][1])
    streams = [double_step(*stream, bits[1]) for stream, bits in zip(streams, orders)]

    normed1 = rms_scale(residual, norm_gain1).astype(jnp.bfloat16)
    led, normed1 = lax.optimization_barrier(([block for block, _ in streams], normed1))
    streams = [(block, held) for block, (_, held) in zip(led, streams)]
    for step in range(2, top - 1):
        streams = [double_step(*stream, bits[step]) for stream, bits in zip(streams, orders)]

    def core_halves(values):
        by_core = values.reshape(-1, dev_count, 2, in_rows)
        return [
            lax.dynamic_index_in_dim(by_core, side, 2, keepdims=False).reshape(-1, width // 2)
            for side in (core, 1 - core)
        ]

    kv_own = double_step(*streams[2], orders[2][top - 1])[0].reshape(width // 2, -1)
    kv_sib = swap(kv_own)
    kv_cols = sum(
        jnp.dot(side, weights, preferred_element_type=jnp.float32)
        for side, weights in zip(core_halves(normed1), (kv_own, kv_sib))
    )
    k_raw = kv_cols[:, :kv_width].reshape(row_count, KV_HEADS, HEAD_DIM)
    keys_local = rope_apply(k_raw, local_pos).reshape(row_count, kv_width).astype(jnp.bfloat16)
    kv_local = jnp.concatenate([keys_local, kv_cols[:, kv_width:].astype(jnp.bfloat16)], axis=0)
    kv_all = double(kv_local, high + (1, 0)).reshape(dev_count, 2 * row_count, kv_width)
    all_keys = kv_all[:, :row_count].reshape(-1, kv_width)
    all_values = kv_all[:, row_count:].reshape(-1, kv_width)
    tail_first = normed1[half_rows - rim_len : half_rows]
    tail_second = normed1[row_count - rim_len :]
    rim_first = lax.ppermute(tail_first, "ctx", up)
    rim_second = jnp.where(is_last, tail_first, lax.ppermute(tail_second, "ctx", down))
    spare = 16 - 2 * rim_len
    extended = jnp.concatenate(
        [normed1, rim_first, rim_second, jnp.zeros((spare, width), jnp.bfloat16)], axis=0
    )
    step_raw = jnp.dot(normed1, step_proj, preferred_element_type=jnp.float32)
    step_pair = step_raw.reshape(2, half_rows, MHEADS)
    early_steps = jax.nn.softplus(step_pair + step_bias[None, None, :])
    decays = jnp.exp(jnp.sum(early_steps * -jnp.exp(decay_log), axis=1))
    all_decays = exchange(
        jnp.broadcast_to(decays.reshape(1, 2 * MHEADS), (dev_count, 2 * MHEADS))
    ).reshape(dev_count, 2, MHEADS)
    span_decays = jnp.concatenate([all_decays[:, 0], all_decays[::-1, 1]], axis=0)
    row_head = (device * state_rows + jnp.arange(state_rows)) // MHEAD_DIM
    row_pick = (row_head[:, None] == jnp.arange(MHEADS)[None, :]).astype(jnp.float32)
    row_decays = jnp.dot(row_pick, span_decays.T, precision=HIGHEST)
    grad_top = out_grad[0]
    grad_top_b = grad_top.astype(jnp.bfloat16)
    led, extended, row_decays = lax.optimization_barrier((streams[0][0], extended, row_decays))
    streams[0] = (led, streams[0][1])
    streams = [double_step(*stream, bits[top - 1]) for stream, bits in zip(streams[:2], orders)]
    mix_own = [block.reshape(width // 2, -1) for block, _ in streams] + [kv_own]
    mix_sib = [swap(own) for own in mix_own[:2]] + [kv_sib]
    ext_own, ext_sib = core_halves(extended)
    if out_rows < 64:
        group = 64 // out_rows
        gathered = jnp.concatenate(
            [
                jnp.concatenate(
                    [
                        part.reshape(-1, group * in_rows, part.shape[-1])
                        for part in (piece[:, :in_rows], piece[:, in_rows:])
                    ],
                    axis=1,
                )
                if split
                else piece.reshape(-1, group * out_rows, piece.shape[-1])
                for piece, split in (
                    (gathered[:, :, :FF], True),
                    (gathered[:, :, FF : FF + 2 * width], False),
                    (gathered[:, :, FF + 2 * width :], True),
                )
            ],
            axis=2,
        )
    split_row = gathered.shape[1] // 2
    mix_gate = jnp.concatenate(
        [
            gathered[:, :split_row, FF + 2 * width :].reshape(width, half_gate),
            gathered[:, split_row:, FF + 2 * width :].reshape(width, half_gate),
        ],
        axis=1,
    )

    projected = jnp.concatenate(
        [
            jnp.dot(ext_own, own, preferred_element_type=jnp.float32)
            + jnp.dot(ext_sib, sib, preferred_element_type=jnp.float32)
            for own, sib in zip(mix_own[:2], mix_sib[:2])
        ],
        axis=1,
    )
    conv_all = projected[:, :CONV_CH]
    q_raw = projected[:row_count, CONV_CH:].reshape(row_count, ATT_HEADS, HEAD_DIM)
    padded = jnp.stack(
        [
            jnp.concatenate(
                [conv_all[row_count : row_count + rim_len], conv_all[:half_rows]], axis=0
            ),
            jnp.concatenate(
                [
                    conv_all[row_count + rim_len : row_count + 2 * rim_len],
                    conv_all[half_rows:row_count],
                ],
                axis=0,
            ),
        ]
    )

    def local_parts(padded_one, step_one):
        x_heads, step_size, decay_rate, b_proj, c_proj = mixer_inputs(
            padded_one, step_one, conv_weight, conv_bias, step_bias, decay_log
        )
        local_out, fresh_state, cumulative = span_local(
            x_heads, step_size, decay_rate, b_proj, c_proj, skip_gain
        )
        return (local_out, fresh_state, cumulative, c_proj)

    local_out, fresh_state, cumulative, c_proj = jax.vmap(local_parts)(padded, step_pair)
    queries = rope_apply(q_raw, local_pos).astype(jnp.bfloat16)

    def to_slices(states):
        return (
            states.astype(jnp.bfloat16)
            .reshape(2, dev_count, state_rows, STATE)
            .transpose(1, 0, 2, 3)
            .reshape(dev_count, 2 * state_rows, STATE)
        )

    def from_slices(slices):
        return (
            slices.reshape(dev_count, 2, state_rows, STATE)
            .transpose(1, 0, 2, 3)
            .reshape(2, MHEADS, MHEAD_DIM, STATE)
            .astype(jnp.float32)
        )

    fresh_all = exchange(to_slices(fresh_state)).reshape(dev_count, 2, state_rows, STATE)
    entering = chain_scan(fresh_all, row_decays, False)
    entering, local_out = lax.optimization_barrier((entering, local_out))
    states = from_slices(exchange(entering.reshape(dev_count, 2 * state_rows, STATE)))
    ssm_out = (local_out + jax.vmap(carry_term)(c_proj, cumulative, states)).reshape(
        row_count, INNER
    )
    gate_z = jnp.dot(normed1, mix_gate, preferred_element_type=jnp.float32)
    mamba_part = gated_tail(ssm_out, gate_z, mamba_gain)
    attn_f32, log_total = attention_forward(queries, all_keys, all_values, local_pos, key_pos)
    joined = jnp.concatenate(
        [mamba_part.astype(jnp.bfloat16), attn_f32.astype(jnp.bfloat16)], axis=1
    )
    outputs, grad_middle, grad_joined, gain2_part, bundle = dense_core(
        joined, residual, grad_top, norm_gain2, gathered
    )
    unused_tail, tail_back = jax.vjp(gated_tail, ssm_out, gate_z, mamba_gain)
    grad_ssm, grad_z, mgain_part = tail_back(grad_joined[:, :INNER])
    grad_z = grad_z.astype(jnp.bfloat16)

    def half_grad(values, grads):
        order = ring_order(dev_count)
        made = jnp.dot(
            half_pair(values, dev_count, core),
            both_cores(grads),
            preferred_element_type=jnp.float32,
        ).astype(jnp.bfloat16)
        made = made.reshape(dev_count, -1, grads.shape[1])
        return made[jnp.array(order)] if order != list(range(dev_count)) else made

    if in_rows % 16 == 0:
        bundle_s = swap(bundle)
        norm1_s, joined_s, top_s, grad_z_s = swap(normed1), swap(joined), swap(grad_top_b), swap(grad_z)
        mid_at = 3 * FF + width
        grad_pack = half_grads(
            core,
            dev_count,
            out_rows,
            (
                (
                    (bundle, bundle_s, 3 * FF, width),
                    ((bundle, bundle_s, FF), (bundle, bundle_s, 2 * FF)),
                    FF,
                ),
                ((joined, joined_s, 0, joined.shape[1]), ((bundle, bundle_s, mid_at),), width),
                ((bundle, bundle_s, 0, FF), ((grad_top_b, top_s, 0),), width),
                (
                    (normed1, norm1_s, 0, width),
                    (
                        (grad_z[:, :half_gate], grad_z_s[:, :half_gate], 0),
                        (grad_z[:, half_gate:], grad_z_s[:, half_gate:], 0),
                    ),
                    half_gate,
                ),
            ),
        )
    else:
        up_half = half_grad(bundle[:, 3 * FF : 3 * FF + width], bundle[:, FF : 3 * FF])
        gate_half = half_grad(normed1, grad_z)
        grad_pack = jnp.concatenate(
            [
                jnp.concatenate([up_half[:, :, :FF], up_half[:, :, FF:]], axis=1),
                half_grad(joined, bundle[:, 3 * FF + width :]),
                half_grad(bundle[:, :FF], grad_top_b),
                jnp.concatenate(
                    [gate_half[:, :, :half_gate], gate_half[:, :, half_gate:]], axis=1
                ),
            ],
            axis=2,
        )
    grad_pack = grad_pack.reshape(dev_count * out_rows, -1)
    grad_joined, grad_ssm, grad_pack = lax.optimization_barrier((grad_joined, grad_ssm, grad_pack))
    pack_shard = scatter_ring(grad_pack)
    grad_pair = grad_ssm.reshape(2, half_rows, INNER)
    grad_heads = grad_ssm.reshape(2, half_rows, MHEADS, MHEAD_DIM)
    own_grads = jnp.einsum(
        "athp,atn->ahpn",
        grad_heads * jnp.exp(cumulative)[:, :, :, None],
        c_proj,
        precision=HIGHEST,
    )
    grad_attn = grad_joined[:, INNER:].astype(jnp.bfloat16)
    own_slices, grad_attn = lax.optimization_barrier((to_slices(own_grads), grad_attn))
    grad_q, grad_keys, grad_values = attention_backward(
        queries, all_keys, all_values, local_pos, key_pos, log_total, attn_f32, grad_attn
    )
    kv_grads = jnp.concatenate(
        [
            grad_keys.astype(jnp.bfloat16).reshape(dev_count, row_count, kv_width),
            grad_values.astype(jnp.bfloat16).reshape(dev_count, row_count, kv_width),
        ],
        axis=1,
    )
    own_all = exchange(own_slices).reshape(dev_count, 2, state_rows, STATE)
    leaving = chain_scan(own_all, row_decays, True)
    kv_held = halve(kv_grads, (0, 1))
    end_slices = exchange(leaving.reshape(dev_count, 2 * state_rows, STATE))
    end_slices, kv_held = lax.optimization_barrier((end_slices, kv_held))
    end_grads = from_slices(end_slices)
    kv_back = halve(kv_held.reshape(dev_count // 4, 2 * row_count, kv_width), high)
    keys_back = kv_back[:row_count]
    values_back = kv_back[row_count:]
    unused_q, rope_back_q = jax.vjp(partial(rope_apply, positions=local_pos), q_raw)
    unused_k, rope_back_k = jax.vjp(partial(rope_apply, positions=local_pos), k_raw)
    (grad_q_raw,) = rope_back_q(grad_q)
    (grad_k_raw,) = rope_back_k(keys_back.reshape(row_count, KV_HEADS, HEAD_DIM))
    pair_mixer = jax.vmap(half_mixer, in_axes=(0, 0, None, None, None, None, None, 0))
    unused_m, mixer_back = jax.vjp(
        pair_mixer,
        padded,
        step_pair,
        conv_weight,
        conv_bias,
        step_bias,
        decay_log,
        skip_gain,
        states,
    )
    mixer_grads = mixer_back((grad_pair, end_grads))
    grad_padded = mixer_grads[0]
    grad_rims = grad_padded[:, :rim_len].reshape(2 * rim_len, CONV_CH)

    def to_width(grads):
        sides = [0.0, 0.0]
        for piece, pair in enumerate(zip(mix_own, mix_sib)):
            low = edges[piece] - INNER
            part = grads[:, low : low + pair[0].shape[1]]
            if part.shape[1] == 0:
                continue
            for side, weights in enumerate(pair):
                sides[side] += jnp.dot(
                    part, weights[:, : part.shape[1]].T, preferred_element_type=jnp.float32
                )
        first_core = core == 0
        sides = [side.reshape(-1, dev_count, in_rows) for side in sides]
        return jnp.stack(
            [jnp.where(first_core, sides[0], sides[1]), jnp.where(first_core, sides[1], sides[0])],
            axis=2,
        ).reshape(-1, width)

    rims_b = jnp.pad(grad_rims.astype(jnp.bfloat16), ((0, spare), (0, 0)))
    rim_back = to_width(rims_b)
    back_first = rim_back[:rim_len]
    back_second = rim_back[rim_len : 2 * rim_len]
    add_first = lax.ppermute(back_first, "ctx", down) + jnp.where(is_last, back_second, 0.0)
    add_second = lax.ppermute(back_second, "ctx", up)
    grad_conv = grad_padded[:, rim_len:].reshape(row_count, CONV_CH)
    grad_proj = jnp.concatenate(
        [
            jnp.concatenate(
                [
                    grad_conv,
                    grad_q_raw.reshape(row_count, q_width),
                    grad_k_raw.reshape(row_count, kv_width),
                    values_back,
                ],
                axis=1,
            ).astype(jnp.bfloat16),
            jnp.pad(rims_b, ((0, 0), (0, q_width + 2 * kv_width))),
        ],
        axis=0,
    )
    if in_rows % 16 == 0:
        in_half = half_grads(
            core,
            dev_count,
            in_rows,
            (
                (
                    (extended, swap(extended), 0, width),
                    ((grad_proj, swap(grad_proj), 0),),
                    grad_proj.shape[1],
                ),
            ),
        )
    else:
        in_half = half_grad(extended, grad_proj)
    in_half = in_half.reshape(dev_count * in_rows, -1)
    in_half, pack_shard = lax.optimization_barrier((in_half, pack_shard))
    in_shard = scatter_ring(in_half)
    grad_step = mixer_grads[1].reshape(row_count, MHEADS).astype(jnp.bfloat16)
    step_grad = jnp.dot(grad_step.T, normed1, preferred_element_type=jnp.float32)
    grad_main = to_width(grad_proj[:row_count])
    fill = jnp.zeros((half_rows - rim_len, width), jnp.float32)
    grad_normed1 = (
        grad_main
        + jnp.concatenate([fill, add_first, fill, add_second], axis=0)
        + jnp.dot(grad_step, step_proj.T, preferred_element_type=jnp.float32)
        + jnp.dot(grad_z, mix_gate.T, preferred_element_type=jnp.float32)
    )
    unused_one, norm_back1 = jax.vjp(rms_scale, residual, norm_gain1)
    grad_res_n, gain1_part = norm_back1(grad_normed1)
    input_grad = grad_middle + grad_res_n
    parts = (
        step_grad,
        mixer_grads[2],
        mixer_grads[3],
        mgain_part,
        gain2_part,
        mixer_grads[4],
        mixer_grads[5],
        mixer_grads[6],
        gain1_part,
    )
    flat = jnp.concatenate([part.reshape(-1) for part in parts])
    total_len = flat.shape[0]
    summed = butterfly_sum(jnp.pad(flat, (0, -total_len % 1024)).reshape(-1, 128)).reshape(-1)
    sums = []
    start = 0
    for part in parts:
        sums.append(summed[start : start + part.size].reshape(part.shape))
        start += part.size
    sums = [sums.pop()] + sums
    pack_f32 = pack_shard.astype(jnp.float32)
    up_shard = jnp.concatenate([pack_f32[:in_rows, :FF], pack_f32[in_rows:, :FF]], axis=1)
    return (
        outputs[None],
        input_grad[None],
        sums[0],
        jnp.concatenate(
            [
                pack_f32[:in_rows, FF + 2 * width :],
                pack_f32[in_rows:, FF + 2 * width :],
                in_shard.astype(jnp.float32),
            ],
            axis=1,
        ),
        sums[1].T,
        sums[2],
        sums[3],
        sums[6],
        sums[7],
        sums[8],
        sums[4],
        pack_f32[:, FF : FF + width],
        sums[5].reshape(-1),
        up_shard,
        pack_f32[:, FF + width : FF + 2 * width],
    )


def solution(mesh):
    return jax.shard_map(
        body,
        mesh=mesh,
        in_specs=(
            P("wsh", "ctx", None),
            P(),
            P(("ctx", "wsh"), None),
            P(),
            P(),
            P(),
            P(),
            P(),
            P(),
            P(),
            P(("ctx", "wsh"), None),
            P(),
            P(("ctx", "wsh"), None),
            P(("ctx", "wsh"), None),
            P("wsh", "ctx", None),
        ),
        out_specs=(
            P("wsh", "ctx", None),
            P("wsh", "ctx", None),
            P(),
            P(("ctx", "wsh"), None),
            P(),
            P(),
            P(),
            P(),
            P(),
            P(),
            P(),
            P(("ctx", "wsh"), None),
            P(),
            P(("ctx", "wsh"), None),
            P(("ctx", "wsh"), None),
        ),
        check_vma=False,
    )
```
